32 devices in a mesh: dp: 8 (over z, y), mp: 4 (over x, core).
Axes of the slice: x: 2, y: 2, z: 4, core: 2. Of those that a mesh axis runs over, the one named last changes fastest.
Arguments:
- hidden_in: bfloat16 [16384, 1024], P(('dp', 'mp')), may hold values from -6 to 6
- out_grad: bfloat16 [16384, 1024], P(('dp', 'mp')), may hold values from -6 to 6
- seq_lengths: int32 [16], replicated, may hold values from 256 to 1792, as said below
- dealing: int32 [16384], replicated, may hold values from 0 to 16383, as said below
- attn_gain: float32 [1024], P(('dp', 'mp')), may hold values from 0.1 to 1.9
- mlp_gain: float32 [1024], P(('dp', 'mp')), may hold values from 0.1 to 1.9
- w_qkv: bfloat16 [3, 1024, 1024], P(None, 'dp', 'mp'), may hold values from -0.25 to 0.25
- w_out: bfloat16 [1024, 1024], P('mp', 'dp'), may hold values from -0.5 to 0.5
- w_in: bfloat16 [2, 1024, 2624], P(None, 'dp', 'mp'), may hold values from -0.1875 to 0.1875
- w_down: bfloat16 [2624, 1024], P('mp', 'dp'), may hold values from -0.25 to 0.25
Outputs:
- output: bfloat16 [16384, 1024], P(('dp', 'mp'))
- input_grad: bfloat16 [16384, 1024], P(('dp', 'mp'))
- attn_gain_grad: float32 [1024], P(('dp', 'mp'))
- mlp_gain_grad: float32 [1024], P(('dp', 'mp'))
- w_qkv_grad: float32 [3, 1024, 1024], P(None, 'dp', 'mp')
- w_out_grad: float32 [1024, 1024], P('mp', 'dp')
- w_in_grad: float32 [2, 1024, 2624], P(None, 'dp', 'mp')
- w_down_grad: float32 [2624, 1024], P('mp', 'dp')
- w_qkv_clipped: bfloat16 [3, 1024, 1024], P(None, 'dp', 'mp')
The draws below stay inside these ranges and needn't reach their ends.
Inputs may be any that keep to these rules, and one draw needn't show every extreme that they name: `seq_lengths`: entries 2o and 2o + 1 are the lengths of owner o's two sequences and sum to 2048. `dealing`: A permutation. Cut the input order and the dealt order into blocks of 512 rows, block b standing on dp index b // 4 and mp index b % 4; each dealt block takes exactly 64 rows from each input block of the same mp index and none from others.
All inputs are finite; a program needn't handle non-finite values.
Results may differ from the reference program's by a relative error of at most 0.019.
The reference program's roundings to bfloat16 on the way count: a program that leaves them out, or rounds other values in their place, can miss the bound.
Values may be sent and summed in bfloat16 or wider, within the bound.
No kernel may reach another device: no remote copies, remote signals or barrier semaphores. Data moves between devices by JAX's collectives and lax.ppermute only.
A program may use at most 192 MiB of HBM per device.

```python
import math
import jax
import jax.numpy as jnp
from jax import lax

D = 1024
HEADS = 16
HEAD_DIM = 64
FF = 2624
TOK_DEV = 2048
MIN_LEN = 256
TOKENS = 16384
N_DP = 8
N_MP = 4


def draw_seq_lengths(key, part):
    first_key, second_key, third_key = jax.random.split(key, 3)
    firsts = jax.random.randint(first_key, (N_DP,), MIN_LEN, TOK_DEV - MIN_LEN + 1)
    chosen = jax.random.randint(second_key, (), 0, N_DP)
    flip_side = jax.random.randint(third_key, (), 0, 2)
    forced = jnp.where(flip_side == 0, MIN_LEN, TOK_DEV - MIN_LEN)
    firsts = jnp.where(jnp.arange(N_DP) == chosen, forced, firsts)
    return jnp.stack([firsts, TOK_DEV - firsts], axis=1).reshape(-1).astype(jnp.int32)


def draw_dealing(key, part):
    row_count = TOK_DEV // N_MP
    slot_count = row_count // N_DP
    first_key, second_key = jax.random.split(key)
    base_rows = jnp.broadcast_to(jnp.arange(row_count, dtype=jnp.int32), (N_MP, N_DP, row_count))
    shuffled = jax.random.permutation(first_key, base_rows, axis=2, independent=True)
    lane_ids = jnp.arange(N_MP, dtype=jnp.int32)[:, None, None]
    sources = jnp.arange(N_DP, dtype=jnp.int32)[None, :, None]
    anchor = (sources * N_MP + lane_ids) * row_count + shuffled
    grouped = anchor.reshape(N_MP, N_DP, N_DP, slot_count).transpose(0, 2, 1, 3).reshape(N_MP, N_DP, row_count)
    mixed_rows = jax.random.permutation(second_key, grouped, axis=2, independent=True)
    return mixed_rows.transpose(1, 0, 2).reshape(-1).astype(jnp.int32)


def block_levels(own_key, extent, cuts, smallest, high):
    loudness = 1.0
    for axis_at, blocks in cuts:
        heights = jax.random.uniform(jax.random.fold_in(jax.random.fold_in(own_key, 6), axis_at), (blocks,), jnp.float32, smallest / len(cuts), high / len(cuts))
        loudness = loudness * jnp.repeat(jnp.exp(heights), extent[axis_at] // blocks).reshape((-1,) + (1,) * (len(extent) - 1 - axis_at))
    return loudness


def normal_values(key, dims, scale, bound, cuts=(), kind=jnp.bfloat16):
    factor_of = block_levels(key, dims, cuts, -0.22, 0.18) if cuts else 1.0
    values = jax.random.normal(key, dims, jnp.float32) * scale * factor_of
    return jnp.minimum(jnp.maximum(values, -bound), bound).astype(kind)


def setup_inputs(seed: int = 0) -> dict:
    key_of = jax.random.split(jax.random.key(seed), 11)
    return {
        "hidden_in": normal_values(key_of[0], (TOKENS, D), 1.0, 6.0, ((0, 32),)),
        "out_grad": normal_values(key_of[1], (TOKENS, D), 1.0, 6.0, ((0, 32),)),
        "seq_lengths": draw_seq_lengths(jax.random.fold_in(key_of[10], 71), 0),
        "dealing": draw_dealing(jax.random.fold_in(key_of[10], 71), 0),
        "attn_gain": jnp.clip(1.0 + 0.18 * jax.random.normal(key_of[4], (D,), jnp.float32), 0.1, 1.9),
        "mlp_gain": jnp.clip(1.0 + 0.18 * jax.random.normal(key_of[5], (D,), jnp.float32), 0.1, 1.9),
        "w_qkv": normal_values(key_of[6], (3, D, D), (D // 2) ** -0.5, 0.25, ((1, 8), (2, 4))),
        "w_out": normal_values(key_of[7], (D, D), (D // 8) ** -0.5, 0.5, ((0, 4), (1, 8))),
        "w_in": normal_values(key_of[8], (2, D, FF), D ** -0.5, 0.1875, ((1, 8), (2, 4))),
        "w_down": normal_values(key_of[9], (FF, D), (FF // 4) ** -0.5, 0.25, ((0, 4), (1, 8))),
    }


theta_base = 160000.0
norm_eps = 1e-05
clip_limit = 5.0
score_scale = 0.125

@jax.custom_vjp
def low(v):
    return lax.optimization_barrier(v.astype(jnp.bfloat16)).astype(jnp.float32)

@jax.custom_vjp
def low_back(v):
    return v

def low_keep(v):
    return (low(v), None)

def low_pass(kept, grad):
    return (grad,)

def back_keep(v):
    return (v, None)

def back_low(kept, grad):
    return (low(grad),)
low.defvjp(low_keep, low_pass)
low_back.defvjp(back_keep, back_low)

def highest(pattern, left_side, right_side):
    return jnp.einsum(pattern, left_side, right_side, precision=lax.Precision.HIGHEST)

def normalize(values):
    row_mean = lax.optimization_barrier(jnp.mean(values, axis=-1, keepdims=True))
    centered = values - row_mean
    variance = lax.optimization_barrier(jnp.mean(centered * centered, axis=-1, keepdims=True))
    return centered * lax.rsqrt(variance + norm_eps)

def rope_tables(positions, head_width):
    steps = jnp.arange(head_width // 2, dtype=jnp.float32)
    freqs = jnp.exp(steps * (-2.0 * math.log(theta_base) / head_width))
    angles = positions[:, None] * freqs[None, :]
    cosine_table = jnp.cos(angles)
    sine_table = jnp.sin(angles)
    return (jnp.concatenate([cosine_table, cosine_table], -1), jnp.concatenate([sine_table, sine_table], -1))

def rotate(values, cosine_table, sine_table):
    half_width = values.shape[-1] // 2
    turned = jnp.concatenate([-values[..., half_width:], values[..., :half_width]], axis=-1)
    return values * cosine_table[:, None, :] + turned * sine_table[:, None, :]

def attend(queries, key_rows, values, segment):
    token_count = queries.shape[0]
    block_rows = min(512, token_count)
    block_count = token_count // block_rows
    q_blocks = queries.reshape(block_count, block_rows, queries.shape[1], queries.shape[2])
    s_blocks = segment.reshape(block_count, block_rows)

    def one_block(pieces):
        query_block, seg_block = pieces
        scores = low_back(highest('bhd,thd->hbt', query_block, key_rows) * score_scale)
        same_seq = (seg_block[:, None] == segment[None, :])[None]
        masked = jnp.where(same_seq, scores, -1e+30)
        weights_low = low(jax.nn.softmax(masked, axis=-1))
        attended = highest('hbt,thd->bhd', weights_low, values)
        return (attended, lax.optimization_barrier(jnp.max(masked, axis=(1, 2))))
    attended, peak_rows = lax.map(jax.checkpoint(one_block), (q_blocks, s_blocks))
    return (attended.reshape(queries.shape), lax.optimization_barrier(jnp.max(peak_rows, axis=0)))

def block_layer(tokens, first_len, params):
    attn_gain, mlp_gain, w_qkv, w_out, w_in, w_down = params
    token_count, model_width = tokens.shape
    places = jnp.arange(token_count, dtype=jnp.int32)
    second_seq = places >= first_len
    segment = second_seq.astype(jnp.int32)
    cosine_table, sine_table = rope_tables(jnp.where(second_seq, places - first_len, places).astype(jnp.float32), HEAD_DIM)
    normed_one = low_back(low(normalize(tokens) * attn_gain))
    projected = highest('td,kdc->ktc', normed_one, w_qkv)
    split_shape = (token_count, HEADS, HEAD_DIM)
    queries = low(rotate(low_back(projected[0]).reshape(split_shape), cosine_table, sine_table))
    key_rows = low(rotate(low_back(projected[1]).reshape(split_shape), cosine_table, sine_table))
    values = low_back(low(projected[2])).reshape(split_shape)
    attended, peaks = attend(queries, key_rows, values, segment)
    attended = low_back(low(attended.reshape(token_count, model_width)))
    branch = low_back(low(highest('tc,ce->te', attended, w_out)))
    after_attn = tokens + branch
    normed_two = low(normalize(after_attn) * mlp_gain)
    gate_up = low_back(highest('td,kdf->ktf', normed_two, w_in))
    activated = low(jax.nn.gelu(gate_up[0], approximate=False) * gate_up[1])
    return (after_attn + highest('tf,fe->te', activated, w_down), peaks)

def reference(hidden_in, out_grad, seq_lengths, dealing, attn_gain, mlp_gain, w_qkv, w_out, w_in, w_down):
    model_width = hidden_in.shape[1]
    tokens = jnp.take(hidden_in.astype(jnp.float32), dealing, axis=0).reshape(N_DP, TOK_DEV, model_width)
    grads_in = jnp.take(out_grad.astype(jnp.float32), dealing, axis=0).reshape(N_DP, TOK_DEV, model_width)
    first_lens = seq_lengths.reshape(N_DP, 2)[:, 0]
    params = (attn_gain.astype(jnp.float32), mlp_gain.astype(jnp.float32), w_qkv.astype(jnp.float32), w_out.astype(jnp.float32), w_in.astype(jnp.float32), w_down.astype(jnp.float32))

    def per_owner(running, pieces):
        weight_sums, logit_top = running
        owner_tokens, owner_grad, first_len = pieces

        def forward(token_rows, param_set):
            return block_layer(token_rows, first_len, param_set)
        result, pullback, peaks = jax.vjp(forward, owner_tokens, params, has_aux=True)
        gradients = pullback(owner_grad)
        weight_sums = tuple((running_sum + update for running_sum, update in zip(weight_sums, gradients[1])))
        return ((weight_sums, jnp.maximum(logit_top, peaks)), (result, gradients[0]))
    zero_grads = tuple((jnp.zeros_like(param_value) for param_value in params))
    start_top = jnp.full((HEADS,), -1e+30, jnp.float32)
    (weight_sums, logit_top), (results, input_grads) = lax.scan(per_owner, (zero_grads, start_top), (tokens, grads_in, first_lens))
    flat_out = results.reshape(-1, model_width)
    output = jnp.zeros_like(flat_out).at[dealing].set(flat_out).astype(jnp.bfloat16)
    flat_grad = input_grads.reshape(-1, model_width)
    input_grad = jnp.zeros_like(flat_grad).at[dealing].set(flat_grad).astype(jnp.bfloat16)
    factor = jnp.sqrt(clip_limit / jnp.maximum(logit_top, clip_limit))
    column_factor = jnp.repeat(factor, HEAD_DIM)
    scaling = jnp.stack([column_factor, column_factor, jnp.ones_like(column_factor)])[:, None, :]
    clipped = (w_qkv.astype(jnp.float32) * scaling).astype(jnp.bfloat16)
    return (output, input_grad, weight_sums[0], weight_sums[1], weight_sums[2], weight_sums[3], weight_sums[4], weight_sums[5], clipped)
```

```python
import functools
import math

import jax
import jax.numpy as jnp
from jax import lax
from jax.experimental import pallas as pl
from jax.experimental.pallas import tpu as pltpu
from jax.sharding import PartitionSpec as P

HEAD_DIM = 64
LANES = 128
theta_base = 160000.0
norm_eps = 1e-05
clip_limit = 5.0
score_scale = 0.125
exp_scale = score_scale * math.log2(math.e)
far_away = -1e30
lowest = -3e38

BF16 = jnp.bfloat16
F32 = jnp.float32


def dot(left, right, left_dim, right_dim):
    return lax.dot_general(
        left, right, (((left_dim,), (right_dim,)), ((), ())), preferred_element_type=F32
    )


def split_three(values):
    high = values.astype(BF16).astype(F32)
    rest = values - high
    middle = rest.astype(BF16).astype(F32)
    return high, middle, rest - middle


def row_stats(values):
    mean = jnp.mean(values, axis=-1, keepdims=True)
    centered = values - mean
    variance = jnp.mean(centered * centered, axis=-1, keepdims=True)
    scale = lax.rsqrt(variance + norm_eps)
    return centered * scale, scale


def turn(values, lane):
    return jnp.where(
        lane % HEAD_DIM < HEAD_DIM // 2,
        pltpu.roll(values, LANES - HEAD_DIM // 2, 1),
        pltpu.roll(values, HEAD_DIM // 2, 1),
    )


def swap_bit(values, axis_name, bit):
    count = lax.axis_size(axis_name)
    return lax.ppermute(values, axis_name, [(i, i ^ bit) for i in range(count)])


def lane_iota(rows):
    return lax.broadcasted_iota(jnp.int32, (rows, LANES), 1)


def vmem(mib):
    return pltpu.CompilerParams(vmem_limit_bytes=mib << 20)


def resident(shape):
    zeros = (0,) * len(shape)
    return pl.BlockSpec(shape, lambda *_: zeros, pipeline_mode=pl.Buffered(1))


def qkv_kernel(step, s_ref, x_ref, gain_ref, w_ref, cos_ref, sin_ref, q_ref, k_ref, v_ref, n_ref):
    first_len = s_ref[1]
    normed, _ = row_stats(x_ref[...].astype(F32))
    n1 = (normed * gain_ref[...]).astype(BF16)
    n_ref[...] = n1
    lane = lane_iota(step)
    row = pl.program_id(0) * step + lax.broadcasted_iota(jnp.int32, (step, LANES), 0)
    second = row >= first_len
    one, zero = jnp.float32(1), jnp.float32(0)
    q_tail = jnp.where(lane == 64 + second.astype(jnp.int32), one, zero)
    k_tail = jnp.where(
        lane == 65 - second.astype(jnp.int32),
        jnp.float32(far_away),
        jnp.where((lane >= 66) & (lane < 69), one, zero),
    )
    cos, sin = cos_ref[...], sin_ref[...]
    for which, (out, tail) in enumerate(((q_ref, q_tail), (k_ref, k_tail), (v_ref, one))):
        projected = dot(n1, w_ref[which], 1, 0)
        for pair in range(projected.shape[1] // LANES):
            part = projected[:, pair * LANES : (pair + 1) * LANES]
            if which < 2:
                part = part * cos + turn(part, lane) * sin
            out[2 * pair] = jnp.where(lane < HEAD_DIM, part, tail).astype(BF16)
            out[2 * pair + 1] = jnp.where(
                lane < HEAD_DIM, pltpu.roll(part, HEAD_DIM, 1), tail
            ).astype(BF16)


def qkv_call(scalars, x_rel, gain, w_qkv, cos, sin, step=256):
    lanes, rows, width = x_rel.shape
    tokens = lanes * rows
    heads = w_qkv.shape[2] // HEAD_DIM
    per = rows // step
    ext = jax.ShapeDtypeStruct((heads, tokens, LANES), BF16)
    row_spec = lambda i, s: (i, 0)
    head_spec = pl.BlockSpec((heads, step, LANES), lambda i, s: (0, i, 0))
    return pl.pallas_call(
        functools.partial(qkv_kernel, step),
        out_shape=(ext, ext, ext, jax.ShapeDtypeStruct((tokens, width), BF16)),
        grid_spec=pltpu.PrefetchScalarGridSpec(
            num_scalar_prefetch=1,
            grid=(tokens // step,),
            in_specs=[
                pl.BlockSpec((None, step, width), lambda i, s: ((i // per) ^ s[0], i % per, 0)),
                resident(gain.shape),
                resident(w_qkv.shape),
                pl.BlockSpec((step, LANES), row_spec),
                pl.BlockSpec((step, LANES), row_spec),
            ],
            out_specs=[head_spec, head_spec, head_spec, pl.BlockSpec((step, width), row_spec)],
        ),
        compiler_params=vmem(40),
        cost_estimate=pl.CostEstimate(
            flops=2 * tokens * width * w_qkv.shape[2] * 3,
            bytes_accessed=20 << 20,
            transcendentals=tokens,
        ),
        name="qkv",
    )(scalars, x_rel, gain, w_qkv, cos, sin)


def key_range(first_len, row, q_rows, k_rows, tokens):
    low = jnp.where(row >= first_len, first_len // k_rows, 0)
    high = jnp.where(row + q_rows <= first_len, (first_len + k_rows - 1) // k_rows, tokens // k_rows)
    return low, high


def fwd_kernel(
    base, q_rows, k_rows, s_ref, q_ref, k_ref, v_ref, o_ref, q2_ref, top_ref, score, peak, acc
):
    heads, tokens, _ = k_ref.shape
    low, high = key_range(
        s_ref[1], base + pl.program_id(0) * q_rows, q_rows, k_rows, tokens
    )
    lane = lane_iota(q_rows)
    peak[...] = jnp.full(peak.shape, lowest, F32)
    acc[...] = jnp.zeros(acc.shape, F32)

    def first_pass(block, carry):
        keys = pl.ds(pl.multiple_of(block * k_rows, k_rows), k_rows)
        for h in range(heads):
            s = dot(q_ref[h], k_ref[h, keys, :], 1, 1)
            score[h, :, keys] = s
            most = peak[h]
            for t in range(k_rows // LANES):
                most = jnp.maximum(most, s[:, t * LANES : (t + 1) * LANES])
            peak[h] = most
        return carry

    lax.fori_loop(low, high, first_pass, 0)
    for h in range(heads):
        peak[h] = jnp.broadcast_to(jnp.max(peak[h], axis=1, keepdims=True), (q_rows, LANES))

    def second_pass(block, carry):
        keys = pl.ds(pl.multiple_of(block * k_rows, k_rows), k_rows)
        for h in range(heads):
            s, most = score[h, :, keys], peak[h]
            p = jnp.concatenate(
                [
                    jnp.exp2((s[:, t * LANES : (t + 1) * LANES] - most) * exp_scale).astype(BF16)
                    for t in range(k_rows // LANES)
                ],
                axis=1,
            )
            acc[h] += dot(p, v_ref[h, keys, :], 1, 0)
        return carry

    lax.fori_loop(low, high, second_pass, 0)
    held = None
    for h in range(heads):
        sums = acc[h]
        total = jnp.where(lane < HEAD_DIM, pltpu.roll(sums, HEAD_DIM, 1), sums)
        out = sums / total
        log_total = peak[h] + jnp.log2(total) * (1.0 / exp_scale)
        a, b, c = split_three(-log_total)
        q2 = q_ref[h].astype(F32)
        q2 = jnp.where(lane == 66, a, jnp.where(lane == 67, b, jnp.where(lane == 68, c, q2)))
        q2_ref[h] = q2.astype(BF16)
        top_ref[h] = jnp.broadcast_to(jnp.max(peak[h], axis=0, keepdims=True), (8, LANES))
        if h % 2 == 0:
            held = out
        else:
            both = jnp.where(lane < HEAD_DIM, held, pltpu.roll(out, HEAD_DIM, 1))
            o_ref[:, (h // 2) * LANES : (h // 2 + 1) * LANES] = both.astype(BF16)


def attend_forward(scalars, q, k, v, chunk, rows, q_rows=256, k_rows=512):
    heads, tokens, _ = k.shape
    count = rows // q_rows
    k_rows = min(k_rows, tokens)
    return pl.pallas_call(
        functools.partial(fwd_kernel, chunk * rows, q_rows, k_rows),
        out_shape=(
            jax.ShapeDtypeStruct((rows, heads * HEAD_DIM), BF16),
            jax.ShapeDtypeStruct((heads, rows, LANES), BF16),
            jax.ShapeDtypeStruct((count, heads, 8, LANES), F32),
        ),
        grid_spec=pltpu.PrefetchScalarGridSpec(
            num_scalar_prefetch=1,
            grid=(count,),
            in_specs=[
                pl.BlockSpec((heads, q_rows, LANES), lambda i, s: (0, chunk * count + i, 0)),
                resident(k.shape),
                resident(v.shape),
            ],
            out_specs=[
                pl.BlockSpec((q_rows, heads * HEAD_DIM), lambda i, s: (i, 0)),
                pl.BlockSpec((heads, q_rows, LANES), lambda i, s: (0, i, 0)),
                pl.BlockSpec((None, heads, 8, LANES), lambda i, s: (i, 0, 0, 0)),
            ],
            scratch_shapes=[
                pltpu.VMEM((heads, q_rows, tokens), F32),
                pltpu.VMEM((heads, q_rows, LANES), F32),
                pltpu.VMEM((heads, q_rows, LANES), F32),
            ],
        ),
        compiler_params=vmem(40),
        cost_estimate=pl.CostEstimate(
            flops=8 * rows * tokens * heads * LANES,
            bytes_accessed=6 << 20,
            transcendentals=rows * tokens * heads,
        ),
        name="attend_forward",
    )(scalars, q, k, v)


def bwd_kernel(
    q_rows, k_rows, s_ref, q2_ref, k_ref, v_ref, do_ref, cos_ref, sin_ref, out_ref, dk_ref, dv_ref
):
    heads, tokens, _ = k_ref.shape
    step = pl.program_id(0)
    low, high = key_range(s_ref[1], step * q_rows, q_rows, k_rows, tokens)

    @pl.when(step == 0)
    def _():
        dk_ref[...] = jnp.zeros_like(dk_ref)
        dv_ref[...] = jnp.zeros_like(dv_ref)

    def body(block, sums):
        keys = pl.ds(pl.multiple_of(block * k_rows, k_rows), k_rows)
        new = []
        for h in range(heads):
            key, q2, do = k_ref[h, keys, :], q2_ref[h], do_ref[h]
            p = jnp.exp2(dot(key, q2, 1, 1) * exp_scale)
            ds = (p * dot(v_ref[h, keys, :], do, 1, 1)).astype(BF16)
            dv_ref[h, keys, :] += dot(p.astype(BF16), do, 1, 0)
            dk_ref[h, keys, :] += dot(ds, q2, 1, 0)
            new.append(sums[h] + dot(key, ds, 0, 0))
        return tuple(new)

    sums = lax.fori_loop(
        low, high, body, tuple(jnp.zeros((LANES, q_rows), F32) for _ in range(heads))
    )
    lane = lane_iota(q_rows)

    def unrotate(first, second, rows):
        both = jnp.where(lane < HEAD_DIM, first, pltpu.roll(second, HEAD_DIM, 1)) * score_scale
        return both * cos_ref[rows, :] - turn(both, lane) * sin_ref[rows, :]

    here = pl.ds(pl.multiple_of(step * q_rows, q_rows), q_rows)
    for pair in range(heads // 2):
        cols = slice(pair * LANES, (pair + 1) * LANES)
        out_ref[0, here, cols] = unrotate(sums[2 * pair].T, sums[2 * pair + 1].T, here).astype(BF16)

    @pl.when(step == pl.num_programs(0) - 1)
    def _():
        def finish(block, carry):
            rows = pl.ds(pl.multiple_of(block * q_rows, q_rows), q_rows)
            for pair in range(heads // 2):
                cols = slice(pair * LANES, (pair + 1) * LANES)
                one, two = 2 * pair, 2 * pair + 1
                out_ref[1, rows, cols] = unrotate(
                    dk_ref[one, rows, :], dk_ref[two, rows, :], rows
                ).astype(BF16)
                out_ref[2, rows, cols] = jnp.where(
                    lane < HEAD_DIM,
                    dv_ref[one, rows, :],
                    pltpu.roll(dv_ref[two, rows, :], HEAD_DIM, 1),
                ).astype(BF16)
            return carry

        lax.fori_loop(0, tokens // q_rows, finish, 0)


def attend_backward(scalars, q2, k, v, do, cos, sin, q_rows=256, k_rows=256):
    heads, tokens, _ = k.shape
    block = lambda: pl.BlockSpec((heads, q_rows, LANES), lambda i, s: (0, i, 0))
    out = (3, tokens, heads * HEAD_DIM)
    return pl.pallas_call(
        functools.partial(bwd_kernel, q_rows, k_rows),
        out_shape=jax.ShapeDtypeStruct(out, BF16),
        grid_spec=pltpu.PrefetchScalarGridSpec(
            num_scalar_prefetch=1,
            grid=(tokens // q_rows,),
            in_specs=[
                block(),
                resident(k.shape),
                resident(v.shape),
                block(),
                resident(cos.shape),
                resident(sin.shape),
            ],
            out_specs=resident(out),
            scratch_shapes=[
                pltpu.VMEM((heads, tokens, LANES), F32),
                pltpu.VMEM((heads, tokens, LANES), F32),
            ],
        ),
        compiler_params=vmem(48),
        cost_estimate=pl.CostEstimate(
            flops=20 * tokens * tokens * heads * LANES,
            bytes_accessed=14 << 20,
            transcendentals=tokens * tokens * heads,
        ),
        name="attend_backward",
    )(scalars, q2, k, v, do, cos, sin)


def mlp_kernel(
    s_ref, x_ref, g_ref, o0, o1, o2, o3, w0, w1, w2, w3, gain_ref, win_ref, wdown_ref, *rest
):
    a_ref, n_ref, act_ref, dgate_ref, dup_ref, keep_ref, send_ref = rest[-7:]
    branch = dot(o0[...], w0[...], 1, 0) + dot(o1[...], w1[...], 1, 0)
    branch = branch + dot(o2[...], w2[...], 1, 0) + dot(o3[...], w3[...], 1, 0)
    branch = branch.astype(BF16)
    a_ref[...] = branch
    normed, _ = row_stats(x_ref[...].astype(F32) + branch.astype(F32))
    n2 = (normed * gain_ref[...]).astype(BF16)
    n_ref[...] = n2
    gate = dot(n2, win_ref[0], 1, 0)
    up = dot(n2, win_ref[1], 1, 0)
    dact = dot(g_ref[...], wdown_ref[...], 1, 1)
    phi = 0.5 + 0.5 * lax.erf(gate * math.sqrt(0.5))
    gelu = gate * phi
    act_ref[...] = (gelu * up).astype(BF16)
    density = jnp.exp(-0.5 * gate * gate) * (1.0 / math.sqrt(2.0 * math.pi))
    dgate = (dact * up * (phi + gate * density)).astype(BF16)
    dup = (dact * gelu).astype(BF16)
    dgate_ref[...] = dgate
    dup_ref[...] = dup
    partial = dot(dgate, win_ref[0], 1, 1) + dot(dup, win_ref[1], 1, 1)
    mine = pl.program_id(0) == s_ref[2]

    @pl.when(mine)
    def _():
        keep_ref[...] = partial

    @pl.when(jnp.logical_not(mine))
    def _():
        send_ref[...] = partial.astype(BF16)


def mlp_call(scalars, x_rel, g_rel, heads_rel, w_out_rel, gain, w_in, w_down, chunk, held):
    lanes, rows, width = x_rel.shape
    units = w_down.shape[0]
    step = rows // 2
    rel = lambda i, s: (s[0] ^ chunk, i, 0)
    wide = pl.BlockSpec((None, step, width), rel)
    narrow = pl.BlockSpec((None, step, units), rel)
    wide_out = jax.ShapeDtypeStruct(x_rel.shape, BF16)
    narrow_out = jax.ShapeDtypeStruct((lanes, rows, units), BF16)
    half = pl.BlockSpec((step, width), lambda i, s: (0, 0))
    head_spec = pl.BlockSpec((step, heads_rel[0].shape[1]), lambda i, s: (i, 0))
    held = list(held)
    first = 1 + 2 + len(heads_rel) + len(w_out_rel) + 3
    return pl.pallas_call(
        mlp_kernel,
        out_shape=(
            wide_out,
            wide_out,
            narrow_out,
            narrow_out,
            narrow_out,
            jax.ShapeDtypeStruct((step, width), F32),
            jax.ShapeDtypeStruct((step, width), BF16),
        ),
        grid_spec=pltpu.PrefetchScalarGridSpec(
            num_scalar_prefetch=1,
            grid=(2,),
            in_specs=[wide, wide]
            + [head_spec] * len(heads_rel)
            + [resident(w.shape) for w in w_out_rel]
            + [resident(gain.shape), resident(w_in.shape), resident(w_down.shape)]
            + [pl.BlockSpec(memory_space=pl.ANY)] * len(held),
            out_specs=[wide, wide, narrow, narrow, narrow, half, half],
        ),
        input_output_aliases={first + i: i for i in range(len(held))},
        compiler_params=vmem(48),
        cost_estimate=pl.CostEstimate(
            flops=2 * rows * width * (width + 5 * units),
            bytes_accessed=16 << 20,
            transcendentals=2 * rows * units,
        ),
        name="mlp",
    )(scalars, x_rel, g_rel, *heads_rel, *w_out_rel, gain, w_in, w_down, *held)


def pull_norm(normed, scale, cotangent):
    mean = jnp.mean(cotangent, axis=-1, keepdims=True)
    along = jnp.mean(cotangent * normed, axis=-1, keepdims=True)
    return (cotangent - mean - normed * along) * scale


def fold_rows(values):
    rows, width = values.shape
    return jnp.sum(values.reshape(rows // 8, 8, width), axis=0)


def resid_kernel(s_ref, mine_ref, other_ref, x_ref, a_ref, g_ref, gain_ref, da_ref, gain_out):
    dn = mine_ref[...].astype(F32) + other_ref[...].astype(F32)
    normed, scale = row_stats(x_ref[...].astype(F32) + a_ref[...].astype(F32))
    gain_out[...] = fold_rows(dn * normed)
    dx = g_ref[...].astype(F32) + pull_norm(normed, scale, dn * gain_ref[...])
    da_ref[...] = dx.astype(BF16)


def resid_call(scalars, mine, other, x_rel, a_rel, g_rel, gain, chunk):
    rows, width = mine.shape
    flat = pl.BlockSpec((rows, width), lambda i, s: (0, 0))
    rel = pl.BlockSpec((None, rows, width), lambda i, s: (s[0] ^ chunk, s[2], 0))
    return pl.pallas_call(
        resid_kernel,
        out_shape=(
            jax.ShapeDtypeStruct((rows, width), BF16),
            jax.ShapeDtypeStruct((8, width), F32),
        ),
        grid_spec=pltpu.PrefetchScalarGridSpec(
            num_scalar_prefetch=1,
            grid=(1,),
            in_specs=[flat, flat, rel, rel, rel, resident(gain.shape)],
            out_specs=[flat, pl.BlockSpec((8, width), lambda i, s: (0, 0))],
        ),
        compiler_params=vmem(32),
        cost_estimate=pl.CostEstimate(
            flops=20 * rows * width, bytes_accessed=12 * rows * width, transcendentals=rows
        ),
        name="resid",
    )(scalars, mine, other, x_rel, a_rel, g_rel, gain)


def head_grad_kernel(s_ref, own_ref, other_ref, w_ref, o_ref, *rest):
    do_ref, da_ref = rest[-2:]
    own = pl.program_id(0) == s_ref[2]
    da = jnp.where(own, own_ref[...], other_ref[...])
    da_ref[...] = da
    do = dot(da, w_ref[...], 1, 1).astype(BF16).astype(F32)
    rows = do.shape[0]
    lane = lane_iota(rows)
    product = do * o_ref[...].astype(F32)
    for pair in range(do.shape[1] // LANES):
        cols = slice(pair * LANES, (pair + 1) * LANES)
        part = do[:, cols]
        for odd in range(2):
            inside = (lane >= HEAD_DIM) if odd else (lane < HEAD_DIM)
            delta = jnp.sum(jnp.where(inside, product[:, cols], 0.0), axis=1, keepdims=True)
            a, b, c = split_three(jnp.broadcast_to(-delta, (rows, LANES)))
            head = pltpu.roll(part, HEAD_DIM, 1) if odd else part
            tail = jnp.where(
                lane == 64, a, jnp.where(lane == 65, b, jnp.where(lane == 66, c, 0.0))
            )
            do_ref[2 * pair + odd] = jnp.where(lane < HEAD_DIM, head, tail).astype(BF16)


def head_grad_call(scalars, own, other, w_out, o_chunk, chunk, tokens, held):
    rows, width = own.shape
    heads = o_chunk.shape[1] // HEAD_DIM
    flat = pl.BlockSpec((rows, width), lambda i, s: (0, 0))
    held = list(held)
    return pl.pallas_call(
        head_grad_kernel,
        out_shape=(
            jax.ShapeDtypeStruct((heads, tokens, LANES), BF16),
            jax.ShapeDtypeStruct((tokens, width), BF16),
        ),
        grid_spec=pltpu.PrefetchScalarGridSpec(
            num_scalar_prefetch=1,
            grid=(2,),
            in_specs=[
                flat,
                flat,
                resident(w_out.shape),
                pl.BlockSpec((rows, o_chunk.shape[1]), lambda i, s: (i, 0)),
            ]
            + [pl.BlockSpec(memory_space=pl.ANY)] * len(held),
            out_specs=[
                pl.BlockSpec((heads, rows, LANES), lambda i, s: (0, 2 * chunk + i, 0)),
                pl.BlockSpec((rows, width), lambda i, s: (2 * chunk + i, 0)),
            ],
        ),
        input_output_aliases={5 + i: i for i in range(len(held))},
        compiler_params=vmem(32),
        cost_estimate=pl.CostEstimate(
            flops=4 * rows * width * heads * HEAD_DIM,
            bytes_accessed=5 << 20,
            transcendentals=0,
        ),
        name="head_grad",
    )(scalars, own, other, w_out, o_chunk, *held)


def dn_kernel(p_ref, w_ref, out_ref):
    total = dot(p_ref[0], w_ref[0], 1, 1) + dot(p_ref[1], w_ref[1], 1, 1)
    out_ref[...] = (total + dot(p_ref[2], w_ref[2], 1, 1)).astype(BF16)


def dn_call(scalars, dproj, w_qkv, parity, rows, step=256):
    kinds, tokens, cols = dproj.shape
    width = w_qkv.shape[1]
    per = rows // step
    return pl.pallas_call(
        lambda s_ref, p_ref, w_ref, out_ref: dn_kernel(p_ref, w_ref, out_ref),
        out_shape=jax.ShapeDtypeStruct((2 * rows, width), BF16),
        grid_spec=pltpu.PrefetchScalarGridSpec(
            num_scalar_prefetch=1,
            grid=(2 * per,),
            in_specs=[
                pl.BlockSpec(
                    (kinds, step, cols),
                    lambda i, s: (0, ((2 * (i // per) + parity) ^ s[0]) * per + i % per, 0),
                ),
                resident(w_qkv.shape),
            ],
            out_specs=pl.BlockSpec((step, width), lambda i, s: (i, 0)),
        ),
        compiler_params=vmem(32),
        cost_estimate=pl.CostEstimate(
            flops=4 * rows * width * cols * kinds, bytes_accessed=8 << 20, transcendentals=0
        ),
        name="dn",
    )(scalars, dproj, w_qkv)


def last_kernel(mine_ref, other_ref, x_ref, da_ref, gain_ref, out_ref, gain_out):
    dn = (mine_ref[...] + other_ref[...].astype(F32)).astype(BF16).astype(F32)
    normed, scale = row_stats(x_ref[...].astype(F32))
    gain_out[...] = fold_rows(dn * normed)
    dx = da_ref[...].astype(F32) + pull_norm(normed, scale, dn * gain_ref[...])
    out_ref[...] = dx.astype(BF16)


def last_call(scalars, mine, other, x_rel, da, gain, step=256):
    rows, width = mine.shape
    per = rows // step
    flat = pl.BlockSpec((step, width), lambda i, s: (i, 0))
    return pl.pallas_call(
        lambda s_ref, *refs: last_kernel(*refs),
        out_shape=(
            jax.ShapeDtypeStruct((rows, width), BF16),
            jax.ShapeDtypeStruct((per, 8, width), F32),
        ),
        grid_spec=pltpu.PrefetchScalarGridSpec(
            num_scalar_prefetch=1,
            grid=(per,),
            in_specs=[
                flat,
                flat,
                pl.BlockSpec((None, step, width), lambda i, s: (0, i, 0)),
                pl.BlockSpec((step, width), lambda i, s: (s[0] * per + i, 0)),
                resident(gain.shape),
            ],
            out_specs=[flat, pl.BlockSpec((None, 8, width), lambda i, s: (i, 0, 0))],
        ),
        compiler_params=vmem(32),
        cost_estimate=pl.CostEstimate(
            flops=20 * rows * width, bytes_accessed=12 * rows * width, transcendentals=rows
        ),
        name="last",
    )(scalars, mine, other, x_rel, da, gain)


def bits_of(count):
    return [1 << i for i in range(count.bit_length() - 1)]


def pick(values, axis, index):
    return lax.dynamic_index_in_dim(values, index, axis, keepdims=False)


def halve(values, axis, axis_name):
    me = lax.axis_index(axis_name)
    carried = values
    for bit in bits_of(lax.axis_size(axis_name)):
        shape = carried.shape
        view = carried.reshape(shape[:axis] + (shape[axis] // 2, 2) + shape[axis + 1 :])
        mine = (me // bit) % 2
        arrived = swap_bit(pick(view, axis + 1, 1 - mine).astype(BF16), axis_name, bit)
        carried = pick(view, axis + 1, mine).astype(F32) + arrived.astype(F32)
    return lax.squeeze(carried, (axis,))


def spread(values, axes):
    for axis_name in reversed(axes):
        me = lax.axis_index(axis_name)
        for bit in bits_of(lax.axis_size(axis_name)):
            other = swap_bit(values, axis_name, bit)
            high = (me // bit) % 2 == 1
            values = jnp.concatenate(
                [jnp.where(high, other, values), jnp.where(high, values, other)], axis=-1
            )
    return values


def gather_sum(values, axes):
    for axis_name in axes:
        me = lax.axis_index(axis_name)
        for bit in reversed(bits_of(lax.axis_size(axis_name))):
            half = values.shape[-1] // 2
            low, top = values[..., :half], values[..., half:]
            high = (me // bit) % 2 == 1
            other = swap_bit(jnp.where(high, low, top), axis_name, bit)
            values = jnp.where(high, top, low) + other
    return values


def local(
    hidden_in, out_grad, seq_lengths, dealing, attn_gain, mlp_gain, w_qkv, w_out, w_in, w_down
):
    dp_count = lax.axis_size("dp")
    mp_count = lax.axis_size("mp")
    owner = lax.axis_index("dp")
    lane = lax.axis_index("mp")
    rows, width = hidden_in.shape
    tokens = rows * mp_count
    slots = rows // dp_count
    first_len = pick(seq_lengths, 0, 2 * owner)
    scalars = jnp.stack([lane, first_len, lane % 2]).astype(jnp.int32)

    lane_rows = pick(dealing.reshape(dp_count, mp_count, rows), 1, lane)
    local_row = lane_rows - (owner * mp_count + lane) * rows
    inside = (local_row >= 0) & (local_row < rows)
    order = jnp.arange(rows, dtype=jnp.int32)
    upto = (order[:, None] <= order[None, :]).astype(BF16)
    rank = dot(inside.astype(BF16), upto, 1, 0).astype(jnp.int32) - 1
    slot_hit = inside[:, None, :] & (rank[:, None, :] == jnp.arange(slots)[None, :, None])
    send_row = jnp.sum(jnp.where(slot_hit, local_row[:, None, :], 0), axis=2).reshape(rows)
    to_slot = (send_row[:, None] == order[None, :]).astype(BF16)
    source = pick(lane_rows, 0, owner) // (rows * mp_count)
    from_src = source[None, :] == jnp.arange(dp_count, dtype=jnp.int32)[:, None]
    src_rank = dot(from_src.astype(BF16), upto, 1, 0).astype(jnp.int32) - 1
    slot_of = source * slots + jnp.sum(jnp.where(from_src, src_rank, 0), axis=0)
    to_dealt = (slot_of[:, None] == order[None, :]).astype(BF16)

    def exchange(values):
        packed = values.reshape(dp_count, slots, width)
        arrived = lax.all_to_all(packed, "dp", split_axis=0, concat_axis=0, tiled=True)
        return arrived.reshape(rows, width)

    def to_owners(values):
        return dot(to_dealt, exchange(dot(to_slot, values, 1, 0).astype(BF16)), 1, 0).astype(BF16)

    def from_owners(values):
        return dot(to_slot, exchange(dot(to_dealt, values, 0, 0).astype(BF16)), 0, 0).astype(BF16)

    def group(values):
        across = swap_bit(values, "mp", 2)
        return [values, swap_bit(values, "mp", 1), across, swap_bit(across, "mp", 1)]

    x_rel = jnp.stack(group(to_owners(hidden_in)))
    gains = spread(jnp.stack([attn_gain, mlp_gain]), ("dp", "mp"))
    gain_one, gain_two = gains[0:1], gains[1:2]
    qkv_full = lax.all_gather(w_qkv, "dp", axis=1, tiled=True)
    outer_own = lax.all_gather(w_out, "dp", axis=1, tiled=True)
    inner_full = lax.all_gather(w_in, "dp", axis=1, tiled=True)
    down_full = lax.all_gather(w_down, "dp", axis=1, tiled=True)
    outer_rel = group(outer_own)
    g_rel = jnp.stack(group(to_owners(out_grad)))

    place = jnp.arange(tokens, dtype=jnp.int32)
    place = jnp.where(place >= first_len, place - first_len, place).astype(F32)
    freq_index = jnp.arange(LANES, dtype=jnp.int32) % (HEAD_DIM // 2)
    freqs = jnp.exp(freq_index.astype(F32) * (-2.0 * math.log(theta_base) / HEAD_DIM))
    angles = place[:, None] * freqs[None, :]
    first_half = jnp.arange(LANES) % HEAD_DIM < HEAD_DIM // 2
    cos = jnp.cos(angles)
    sin = jnp.sin(angles) * jnp.where(first_half, -1.0, 1.0)[None, :]

    q, k, v, n1 = qkv_call(scalars, x_rel, gain_one, qkv_full, cos, sin)
    o_chunks, q2_chunks, peaks, sums = [], [], [], []
    held = ()
    for chunk in range(mp_count):
        o, q2, top = attend_forward(scalars, q, k, v, chunk, rows)
        o_chunks.append(o)
        q2_chunks.append(q2)
        peaks.append(top)
        *held, keep, send = mlp_call(
            scalars, x_rel, g_rel, group(o), outer_rel, gain_two, inner_full, down_full, chunk, held
        )
        sums.append((keep, send))
    a_rel, n2, act, dgate, dup = held
    flat = lambda values: values.reshape(tokens, values.shape[2])

    held = ()
    gain_parts = []
    for chunk in range(mp_count):
        keep, send = sums[chunk]
        mine = (keep + swap_bit(send, "mp", 1).astype(F32)).astype(BF16)
        own, gain_part = resid_call(
            scalars, mine, swap_bit(mine, "mp", 2), x_rel, a_rel, g_rel, gain_two, chunk
        )
        gain_parts.append(gain_part)
        held = head_grad_call(
            scalars, own, swap_bit(own, "mp", 1), outer_own, o_chunks[chunk], chunk, tokens, held
        )
    do, da = held
    mlp_gain_part = 0.5 * jnp.sum(jnp.stack(gain_parts), axis=(0, 1))

    g_flat, n2_flat, act_flat = flat(g_rel), flat(n2), flat(act)
    units = act_flat.shape[1]
    shards = width // dp_count
    down_grad = halve(dot(act_flat, g_flat, 0, 0).reshape(units, dp_count, shards), 1, "dp")
    inner_grad = jnp.stack([dot(n2_flat, flat(dgate), 0, 0), dot(n2_flat, flat(dup), 0, 0)])
    inner_grad = halve(inner_grad.reshape(2, dp_count, shards, units), 1, "dp")
    o_all = jnp.concatenate(o_chunks, axis=0)
    outer_grad = dot(o_all, da, 0, 0).reshape(o_all.shape[1], dp_count, shards)
    outer_grad = halve(outer_grad, 1, "dp")

    def sum_lanes(keep, send):
        both = keep.astype(F32) + swap_bit(send, "mp", 1).astype(F32)
        return both[:rows], swap_bit(both[rows:].astype(BF16), "mp", 2)

    def down_part(one, two):
        pair = jnp.concatenate([act[one], act[two]], axis=0)
        return dot(pair, down_full, 1, 0).astype(BF16)

    mlp_own, mlp_other = sum_lanes(down_part(0, 2), down_part(1, 3))
    after = x_rel[0].astype(F32) + a_rel[0].astype(F32)
    output = from_owners((after + (mlp_own + mlp_other.astype(F32))).astype(BF16))

    head_peaks = jnp.max(jnp.stack(peaks), axis=(0, 1, 3, 4)) * score_scale
    for bit in bits_of(dp_count):
        head_peaks = jnp.maximum(head_peaks, swap_bit(head_peaks, "dp", bit))
    factor = jnp.sqrt(clip_limit / jnp.maximum(head_peaks, clip_limit))
    column_factor = jnp.repeat(factor, HEAD_DIM)
    scaling = jnp.stack([column_factor, column_factor, jnp.ones_like(column_factor)])[:, None, :]
    clipped = (w_qkv.astype(F32) * scaling).astype(BF16)

    dproj = attend_backward(scalars, jnp.concatenate(q2_chunks, axis=1), k, v, do, cos, sin)
    send = dn_call(scalars, dproj, qkv_full, 1, rows)
    keep = dn_call(scalars, dproj, qkv_full, 0, rows)
    proj_grad = jnp.einsum("td,ktc->kdc", n1, dproj, preferred_element_type=F32)
    proj_grad = halve(proj_grad.reshape(3, dp_count, shards, dproj.shape[2]), 1, "dp")
    dn_own, dn_other = sum_lanes(keep, send)
    dx, attn_gain_part = last_call(scalars, dn_own, dn_other, x_rel, da, gain_one)
    input_grad = from_owners(dx)
    gain_grads = jnp.stack([jnp.sum(attn_gain_part, axis=(0, 1)), mlp_gain_part])
    gain_grads = gather_sum(gain_grads, ("dp", "mp"))
    return (
        output,
        input_grad,
        gain_grads[0],
        gain_grads[1],
        proj_grad,
        outer_grad,
        inner_grad,
        down_grad,
        clipped,
    )


def solution(mesh):
    in_specs = (
        P(("dp", "mp"), None),
        P(("dp", "mp"), None),
        P(),
        P(),
        P(("dp", "mp")),
        P(("dp", "mp")),
        P(None, "dp", "mp"),
        P("mp", "dp"),
        P(None, "dp", "mp"),
        P("mp", "dp"),
    )
    out_specs = (
        P(("dp", "mp"), None),
        P(("dp", "mp"), None),
        P(("dp", "mp")),
        P(("dp", "mp")),
        P(None, "dp", "mp"),
        P("mp", "dp"),
        P(None, "dp", "mp"),
        P("mp", "dp"),
        P(None, "dp", "mp"),
    )
    return jax.shard_map(local, mesh=mesh, in_specs=in_specs, out_specs=out_specs, check_vma=False)
```

```python
import functools
import math

import jax
import jax.numpy as jnp
from jax import lax
from jax.experimental import pallas as pl
from jax.experimental.pallas import tpu as pltpu
from jax.sharding import PartitionSpec as P

HEAD_DIM = 64
LANES = 128
theta_base = 160000.0
norm_eps = 1e-05
clip_limit = 5.0
score_scale = 0.125
exp_scale = score_scale * math.log2(math.e)
far_away = -1e30
lowest = -3e38

BF16 = jnp.bfloat16
F32 = jnp.float32


def dot(left, right, left_dim, right_dim):
    return lax.dot_general(
        left, right, (((left_dim,), (right_dim,)), ((), ())), preferred_element_type=F32
    )


def split_three(values):
    high = values.astype(BF16).astype(F32)
    rest = values - high
    middle = rest.astype(BF16).astype(F32)
    return high, middle, rest - middle


def row_stats(values):
    mean = jnp.mean(values, axis=-1, keepdims=True)
    centered = values - mean
    variance = jnp.mean(centered * centered, axis=-1, keepdims=True)
    scale = lax.rsqrt(variance + norm_eps)
    return centered * scale, scale


def turn(values, lane):
    return jnp.where(
        lane % HEAD_DIM < HEAD_DIM // 2,
        pltpu.roll(values, LANES - HEAD_DIM // 2, 1),
        pltpu.roll(values, HEAD_DIM // 2, 1),
    )


def swap_bit(values, axis_name, bit):
    count = lax.axis_size(axis_name)
    return lax.ppermute(values, axis_name, [(i, i ^ bit) for i in range(count)])


def lane_iota(rows):
    return lax.broadcasted_iota(jnp.int32, (rows, LANES), 1)


def vmem(mib):
    return pltpu.CompilerParams(vmem_limit_bytes=mib << 20)


def takes(micros):
    return pl.CostEstimate(flops=micros * 1_100_000_000, bytes_accessed=1 << 20, transcendentals=0)


def resident(shape):
    zeros = (0,) * len(shape)
    return pl.BlockSpec(shape, lambda *_: zeros, pipeline_mode=pl.Buffered(1))


def qkv_kernel(step, per, first, s_ref, xa_ref, xb_ref, gain_ref, w_ref, cos_ref, sin_ref, *rest):
    q_ref, k_ref, v_ref, n_ref = rest[-4:]
    first_len = s_ref[1]
    at = pl.program_id(0)
    x = jnp.where(at < per, xa_ref[...], xb_ref[...])
    normed, _ = row_stats(x.astype(F32))
    n1 = (normed * gain_ref[...]).astype(BF16)
    n_ref[...] = n1
    lane = lane_iota(step)
    start = (((first + at // per) ^ s_ref[0]) * per + at % per) * step
    row = start + lax.broadcasted_iota(jnp.int32, (step, LANES), 0)
    second = row >= first_len
    one, zero = jnp.float32(1), jnp.float32(0)
    q_tail = jnp.where(lane == 64 + second.astype(jnp.int32), one, zero)
    k_tail = jnp.where(
        lane == 65 - second.astype(jnp.int32),
        jnp.float32(far_away),
        jnp.where((lane >= 66) & (lane < 69), one, zero),
    )
    cos, sin = cos_ref[...], sin_ref[...]
    for which, (out, tail) in enumerate(((q_ref, q_tail), (k_ref, k_tail), (v_ref, one))):
        projected = dot(n1, w_ref[which], 1, 0)
        for pair in range(projected.shape[1] // LANES):
            part = projected[:, pair * LANES : (pair + 1) * LANES]
            if which < 2:
                part = part * cos + turn(part, lane) * sin
            out[2 * pair] = jnp.where(lane < HEAD_DIM, part, tail).astype(BF16)
            out[2 * pair + 1] = jnp.where(
                lane < HEAD_DIM, pltpu.roll(part, HEAD_DIM, 1), tail
            ).astype(BF16)


def qkv_call(scalars, xa, xb, gain, w_qkv, cos, sin, first, held, step=512):
    rows, width = xa.shape
    tokens = cos.shape[0]
    cols = w_qkv.shape[2]
    heads = cols // HEAD_DIM
    per = rows // step
    ext = jax.ShapeDtypeStruct((heads, tokens, LANES), BF16)
    place = lambda i, s: (((first + i // per) ^ s[0]) * per + i % per, 0)
    head_spec = pl.BlockSpec((heads, step, LANES), lambda i, s: (0, *place(i, s)))
    held = list(held)
    return pl.pallas_call(
        functools.partial(qkv_kernel, step, per, first),
        out_shape=(ext, ext, ext, jax.ShapeDtypeStruct((tokens, width), BF16)),
        grid_spec=pltpu.PrefetchScalarGridSpec(
            num_scalar_prefetch=1,
            grid=(2 * per,),
            in_specs=[
                pl.BlockSpec((step, width), lambda i, s: (jnp.minimum(i, per - 1), 0)),
                pl.BlockSpec((step, width), lambda i, s: (jnp.maximum(i - per, 0), 0)),
                resident(gain.shape),
                resident((3, width, cols)),
                pl.BlockSpec((step, LANES), place),
                pl.BlockSpec((step, LANES), place),
            ]
            + [pl.BlockSpec(memory_space=pl.ANY)] * len(held),
            out_specs=[head_spec] * 3 + [pl.BlockSpec((step, width), place)],
        ),
        input_output_aliases={7 + i: i for i in range(len(held))},
        compiler_params=vmem(60),
        cost_estimate=takes(9),
        name="qkv",
    )(scalars, xa, xb, gain, w_qkv, cos, sin, *held)


def key_range(first_len, row, q_rows, k_rows, tokens):
    low = jnp.where(row >= first_len, first_len // k_rows, 0)
    high = jnp.where(row + q_rows <= first_len, (first_len + k_rows - 1) // k_rows, tokens // k_rows)
    return low, high


def fwd_kernel(
    far, q_rows, k_rows, s_ref, q_ref, k_ref, v_ref, *rest
):
    o_ref, q2_ref, top_ref, score, peak, acc = rest[-6:]
    heads, tokens, _ = k_ref.shape
    low, high = key_range(
        s_ref[1],
        ((s_ref[3] ^ far) * pl.num_programs(0) + pl.program_id(0)) * q_rows,
        q_rows,
        k_rows,
        tokens,
    )
    lane = lane_iota(q_rows)
    peak[...] = jnp.full(peak.shape, lowest, F32)
    acc[...] = jnp.zeros(acc.shape, F32)

    def first_pass(block, carry):
        keys = pl.ds(pl.multiple_of(block * k_rows, k_rows), k_rows)
        for h in range(heads):
            s = dot(q_ref[h], k_ref[h, keys, :], 1, 1)
            score[h, :, keys] = s
            most = peak[h]
            for t in range(k_rows // LANES):
                most = jnp.maximum(most, s[:, t * LANES : (t + 1) * LANES])
            peak[h] = most
        return carry

    lax.fori_loop(low, high, first_pass, 0)
    for h in range(heads):
        peak[h] = jnp.broadcast_to(jnp.max(peak[h], axis=1, keepdims=True), (q_rows, LANES))

    def second_pass(block, carry):
        keys = pl.ds(pl.multiple_of(block * k_rows, k_rows), k_rows)
        for h in range(heads):
            s, most = score[h, :, keys], peak[h]
            p = jnp.concatenate(
                [
                    jnp.exp2((s[:, t * LANES : (t + 1) * LANES] - most) * exp_scale).astype(BF16)
                    for t in range(k_rows // LANES)
                ],
                axis=1,
            )
            acc[h] += dot(p, v_ref[h, keys, :], 1, 0)
        return carry

    lax.fori_loop(low, high, second_pass, 0)
    held = None
    for h in range(heads):
        sums = acc[h]
        total = jnp.where(lane < HEAD_DIM, pltpu.roll(sums, HEAD_DIM, 1), sums)
        out = sums / total
        log_total = peak[h] + jnp.log2(total) * (1.0 / exp_scale)
        a, b, c = split_three(-log_total)
        q2 = q_ref[h].astype(F32)
        q2 = jnp.where(lane == 66, a, jnp.where(lane == 67, b, jnp.where(lane == 68, c, q2)))
        q2_ref[h] = q2.astype(BF16)
        top_ref[h] = jnp.broadcast_to(jnp.max(peak[h], axis=0, keepdims=True), (8, LANES))
        if h % 2 == 0:
            held = out
        else:
            both = jnp.where(lane < HEAD_DIM, held, pltpu.roll(out, HEAD_DIM, 1))
            o_ref[:, (h // 2) * LANES : (h // 2 + 1) * LANES] = both.astype(BF16)


def attend_forward(scalars, q, k, v, far, rows, held, q_rows=256, k_rows=512):
    heads, tokens, _ = k.shape
    count = rows // q_rows
    k_rows = min(k_rows, tokens)
    return pl.pallas_call(
        functools.partial(fwd_kernel, far, q_rows, k_rows),
        out_shape=(
            jax.ShapeDtypeStruct((rows, heads * HEAD_DIM), BF16),
            jax.ShapeDtypeStruct(q.shape, BF16),
            jax.ShapeDtypeStruct((count, heads, 8, LANES), F32),
        ),
        grid_spec=pltpu.PrefetchScalarGridSpec(
            num_scalar_prefetch=1,
            grid=(count,),
            in_specs=[
                pl.BlockSpec((heads, q_rows, LANES), lambda i, s: (0, (s[3] ^ far) * count + i, 0)),
                resident(k.shape),
                resident(v.shape),
            ]
            + [pl.BlockSpec(memory_space=pl.ANY)] * len(held),
            out_specs=[
                pl.BlockSpec((q_rows, heads * HEAD_DIM), lambda i, s: (i, 0)),
                pl.BlockSpec((heads, q_rows, LANES), lambda i, s: (0, (s[3] ^ far) * count + i, 0)),
                pl.BlockSpec((None, heads, 8, LANES), lambda i, s: (i, 0, 0, 0)),
            ],
            scratch_shapes=[
                pltpu.VMEM((heads, q_rows, tokens), F32),
                pltpu.VMEM((heads, q_rows, LANES), F32),
                pltpu.VMEM((heads, q_rows, LANES), F32),
            ],
        ),
        compiler_params=vmem(60),
        cost_estimate=takes(20),
        input_output_aliases={4 + i: 1 + i for i in range(len(held))},
        name="attend_forward",
    )(scalars, q, k, v, *held)


def bwd_kernel(
    q_rows, k_rows, s_ref, q2_ref, k_ref, v_ref, do_ref, cos_ref, sin_ref, out_ref, dk_ref, dv_ref
):
    heads, tokens, _ = k_ref.shape
    step = pl.program_id(0)
    low, high = key_range(s_ref[1], step * q_rows, q_rows, k_rows, tokens)

    @pl.when(step == 0)
    def _():
        dk_ref[...] = jnp.zeros_like(dk_ref)
        dv_ref[...] = jnp.zeros_like(dv_ref)

    def body(block, sums):
        keys = pl.ds(pl.multiple_of(block * k_rows, k_rows), k_rows)
        new = []
        for h in range(heads):
            key, q2, do = k_ref[h, keys, :], q2_ref[h], do_ref[h]
            p = jnp.exp2(dot(key, q2, 1, 1) * exp_scale)
            ds = (p * dot(v_ref[h, keys, :], do, 1, 1)).astype(BF16)
            dv_ref[h, keys, :] += dot(p.astype(BF16), do, 1, 0)
            dk_ref[h, keys, :] += dot(ds, q2, 1, 0)
            new.append(sums[h] + dot(key, ds, 0, 0))
        return tuple(new)

    sums = lax.fori_loop(
        low, high, body, tuple(jnp.zeros((LANES, q_rows), F32) for _ in range(heads))
    )
    lane = lane_iota(q_rows)

    def unrotate(first, second, rows):
        both = jnp.where(lane < HEAD_DIM, first, pltpu.roll(second, HEAD_DIM, 1)) * score_scale
        return both * cos_ref[rows, :] - turn(both, lane) * sin_ref[rows, :]

    here = pl.ds(pl.multiple_of(step * q_rows, q_rows), q_rows)
    for pair in range(heads // 2):
        cols = slice(pair * LANES, (pair + 1) * LANES)
        out_ref[0, here, cols] = unrotate(sums[2 * pair].T, sums[2 * pair + 1].T, here).astype(BF16)

    @pl.when(step == pl.num_programs(0) - 1)
    def _():
        def finish(block, carry):
            rows = pl.ds(pl.multiple_of(block * q_rows, q_rows), q_rows)
            for pair in range(heads // 2):
                cols = slice(pair * LANES, (pair + 1) * LANES)
                one, two = 2 * pair, 2 * pair + 1
                out_ref[1, rows, cols] = unrotate(
                    dk_ref[one, rows, :], dk_ref[two, rows, :], rows
                ).astype(BF16)
                out_ref[2, rows, cols] = jnp.where(
                    lane < HEAD_DIM,
                    dv_ref[one, rows, :],
                    pltpu.roll(dv_ref[two, rows, :], HEAD_DIM, 1),
                ).astype(BF16)
            return carry

        lax.fori_loop(0, tokens // q_rows, finish, 0)


def attend_backward(scalars, q2, k, v, do, cos, sin, q_rows=256, k_rows=512):
    heads, tokens, _ = k.shape
    block = lambda: pl.BlockSpec((heads, q_rows, LANES), lambda i, s: (0, i, 0))
    out = (3, tokens, heads * HEAD_DIM)
    return pl.pallas_call(
        functools.partial(bwd_kernel, q_rows, k_rows),
        out_shape=jax.ShapeDtypeStruct(out, BF16),
        grid_spec=pltpu.PrefetchScalarGridSpec(
            num_scalar_prefetch=1,
            grid=(tokens // q_rows,),
            in_specs=[
                block(),
                resident(k.shape),
                resident(v.shape),
                block(),
                resident(cos.shape),
                resident(sin.shape),
            ],
            out_specs=resident(out),
            scratch_shapes=[
                pltpu.VMEM((heads, tokens, LANES), F32),
                pltpu.VMEM((heads, tokens, LANES), F32),
            ],
        ),
        compiler_params=vmem(60),
        cost_estimate=takes(57),
        name="attend_backward",
    )(scalars, q2, k, v, do, cos, sin)


def mlp_kernel(
    s_ref, xs_ref, xk_ref, gs_ref, gk_ref, o0, o1, o2, o3, w0, w1, w2, w3, gain_ref, w_ref, *rest
):
    a_ref, n_ref, act_ref, dgate_ref, dup_ref, keep_ref, send_ref, keep_out, send_out = rest[-9:]
    units = w_ref.shape[2]
    sending = pl.program_id(0) < pl.num_programs(0) // 2
    x = jnp.where(sending, xs_ref[...], xk_ref[...])
    g = jnp.where(sending, gs_ref[...], gk_ref[...])
    branch = dot(o0[...], w0[...], 1, 1) + dot(o1[...], w1[...], 1, 1)
    branch = branch + dot(o2[...], w2[...], 1, 1) + dot(o3[...], w3[...], 1, 1)
    branch = branch.astype(BF16)
    a_ref[...] = branch
    normed, _ = row_stats(x.astype(F32) + branch.astype(F32))
    n2 = (normed * gain_ref[...]).astype(BF16)
    n_ref[...] = n2
    partial = out_partial = 0.0
    for low in range(0, units, 256):
        cols = slice(low, min(low + 256, units))
        gate = dot(n2, w_ref[0, :, cols], 1, 0)
        up = dot(n2, w_ref[1, :, cols], 1, 0)
        dact = dot(g, w_ref[2, :, cols], 1, 0)
        phi = 0.5 + 0.5 * lax.erf(gate * math.sqrt(0.5))
        gelu = gate * phi
        act = (gelu * up).astype(BF16)
        act_ref[:, cols] = act
        density = jnp.exp(-0.5 * gate * gate) * (1.0 / math.sqrt(2.0 * math.pi))
        dgate = (dact * up * (phi + gate * density)).astype(BF16)
        dup = (dact * gelu).astype(BF16)
        dgate_ref[:, cols] = dgate
        dup_ref[:, cols] = dup
        partial = partial + dot(dgate, w_ref[0, :, cols], 1, 1) + dot(dup, w_ref[1, :, cols], 1, 1)
        out_partial = out_partial + dot(act, w_ref[2, :, cols], 1, 1)

    @pl.when(sending)
    def _():
        send_ref[...] = partial.astype(BF16)
        send_out[...] = out_partial.astype(BF16)

    @pl.when(jnp.logical_not(sending))
    def _():
        keep_ref[...] = partial
        keep_out[...] = out_partial.astype(BF16)


def mlp_call(scalars, x_pair, g_pair, heads_rel, w_out_rel, gain, w_mlp, first, held, step=256):
    rows, width = x_pair[0].shape
    units = w_mlp.shape[2]
    per = rows // step
    rel = lambda i, s: (first + 1 - i // per, i % per, 0)
    wide = pl.BlockSpec((None, step, width), rel)
    narrow = pl.BlockSpec((None, step, units), rel)
    wide_out = jax.ShapeDtypeStruct((4, rows, width), BF16)
    narrow_out = jax.ShapeDtypeStruct((4, rows, units), BF16)
    send = pl.BlockSpec((step, width), lambda i, s: (jnp.minimum(i, per - 1), 0))
    keep = pl.BlockSpec((step, width), lambda i, s: (jnp.maximum(i - per, 0), 0))
    head_spec = pl.BlockSpec(
        (step, heads_rel[0].shape[1]), lambda i, s: (((i // per) ^ 1 ^ s[2]) * per + i % per, 0)
    )
    held = list(held)
    half = lambda kind: jax.ShapeDtypeStruct((rows, width), kind)
    return pl.pallas_call(
        mlp_kernel,
        out_shape=(
            wide_out,
            wide_out,
            narrow_out,
            narrow_out,
            narrow_out,
            half(F32),
            half(BF16),
            half(BF16),
            half(BF16),
        ),
        grid_spec=pltpu.PrefetchScalarGridSpec(
            num_scalar_prefetch=1,
            grid=(2 * per,),
            in_specs=[send, keep, send, keep]
            + [head_spec] * len(heads_rel)
            + [resident(w.shape) for w in w_out_rel]
            + [resident(gain.shape), resident(w_mlp.shape)]
            + [pl.BlockSpec(memory_space=pl.ANY)] * len(held),
            out_specs=[wide, wide, narrow, narrow, narrow, keep, send, keep, send],
        ),
        input_output_aliases={15 + i: i for i in range(len(held))},
        compiler_params=vmem(60),
        cost_estimate=takes(24),
        name="mlp",
    )(scalars, *x_pair, *g_pair, *heads_rel, *w_out_rel, gain, w_mlp, *held)


def pull_norm(normed, scale, cotangent):
    mean = jnp.mean(cotangent, axis=-1, keepdims=True)
    along = jnp.mean(cotangent * normed, axis=-1, keepdims=True)
    return (cotangent - mean - normed * along) * scale


def resid_kernel(mine_ref, arrived_ref, x_ref, a_ref, g_ref, gain_ref, dx_ref, da_ref):
    dn = mine_ref[...] + arrived_ref[...].astype(F32)
    normed, scale = row_stats(x_ref[...].astype(F32) + a_ref[...].astype(F32))
    dx = g_ref[...].astype(F32) + pull_norm(normed, scale, dn * gain_ref[...])
    dx_ref[...] = dx
    da_ref[...] = dx.astype(BF16)


def resid_call(mine, arrived, x, a_rel, g, gain, step=256):
    rows, width = mine.shape
    per = rows // step
    flat = pl.BlockSpec((step, width), lambda i: (i, 0))
    return pl.pallas_call(
        resid_kernel,
        out_shape=(
            jax.ShapeDtypeStruct((rows, width), F32),
            jax.ShapeDtypeStruct((rows, width), BF16),
        ),
        grid=(per,),
        in_specs=[
            flat,
            flat,
            flat,
            pl.BlockSpec((None, step, width), lambda i: (0, i, 0)),
            flat,
            resident(gain.shape),
        ],
        out_specs=[flat, flat],
        compiler_params=vmem(60),
        cost_estimate=takes(5),
        name="resid",
    )(mine, arrived, x, a_rel, g, gain)


def head_grad_kernel(s_ref, even_ref, odd_ref, w_ref, o_ref, *rest):
    do_ref, da_ref = rest[-2:]
    own = pl.program_id(0) == s_ref[2]
    da = jnp.where(own, even_ref[...], odd_ref[...])
    da_ref[...] = da
    do = dot(da, w_ref[...], 1, 0).astype(BF16).astype(F32)
    rows = do.shape[0]
    lane = lane_iota(rows)
    product = do * o_ref[...].astype(F32)
    for pair in range(do.shape[1] // LANES):
        cols = slice(pair * LANES, (pair + 1) * LANES)
        part = do[:, cols]
        for odd in range(2):
            inside = (lane >= HEAD_DIM) if odd else (lane < HEAD_DIM)
            delta = jnp.sum(jnp.where(inside, product[:, cols], 0.0), axis=1, keepdims=True)
            a, b, c = split_three(jnp.broadcast_to(-delta, (rows, LANES)))
            head = pltpu.roll(part, HEAD_DIM, 1) if odd else part
            tail = jnp.where(
                lane == 64, a, jnp.where(lane == 65, b, jnp.where(lane == 66, c, 0.0))
            )
            do_ref[2 * pair + odd] = jnp.where(lane < HEAD_DIM, head, tail).astype(BF16)


def head_grad_call(scalars, even, odd, w_out, o_chunk, far, tokens, held):
    rows, width = even.shape
    heads = o_chunk.shape[1] // HEAD_DIM
    held = list(held)
    return pl.pallas_call(
        head_grad_kernel,
        out_shape=(
            jax.ShapeDtypeStruct((heads, tokens, LANES), BF16),
            jax.ShapeDtypeStruct((2 * rows, width), BF16),
        ),
        grid_spec=pltpu.PrefetchScalarGridSpec(
            num_scalar_prefetch=1,
            grid=(2,),
            in_specs=[
                resident(even.shape),
                resident(odd.shape),
                resident(w_out.shape),
                pl.BlockSpec((rows, o_chunk.shape[1]), lambda i, s: (i, 0)),
            ]
            + [pl.BlockSpec(memory_space=pl.ANY)] * len(held),
            out_specs=[
                pl.BlockSpec((heads, rows, LANES), lambda i, s: (0, 2 * (s[3] ^ far) + i, 0)),
                pl.BlockSpec((rows, width), lambda i, s: (i, 0)),
            ],
        ),
        input_output_aliases={5 + i: i for i in range(len(held))},
        compiler_params=vmem(60),
        cost_estimate=takes(6),
        name="head_grad",
    )(scalars, even, odd, w_out, o_chunk, *held)


def inner_kernel(n_ref, g0, g1, g2, g3, dgate_ref, dup_ref, act_ref, out_ref):
    n2 = n_ref[...]
    out_ref[0] = dot(n2, dgate_ref[...], 0, 0).astype(BF16)
    out_ref[1] = dot(n2, dup_ref[...], 0, 0).astype(BF16)
    rows = g0.shape[0]
    g = jnp.concatenate([g0[...], g1[...], g2[...], g3[...]], axis=0)
    out_ref[2] = dot(g, act_ref[...], 0, 0).astype(BF16)


def inner_call(n2, g_rel, dgate, dup, act):
    tokens, width = n2.shape
    units = act.shape[1]
    rows = g_rel[0].shape[0]
    count = width // LANES
    return pl.pallas_call(
        inner_kernel,
        out_shape=jax.ShapeDtypeStruct((count, 3, LANES, units), BF16),
        grid=(count,),
        in_specs=[pl.BlockSpec((tokens, LANES), lambda i: (0, i))]
        + [pl.BlockSpec((rows, LANES), lambda i: (0, i))] * 4
        + [resident(act.shape)] * 3,
        out_specs=pl.BlockSpec((None, 3, LANES, units), lambda i: (i, 0, 0, 0)),
        compiler_params=vmem(60),
        cost_estimate=takes(17),
        name="inner_grads",
    )(n2, *g_rel, dgate, dup, act)


def store_slices(out_ref, at, sums):
    for i in range(out_ref.shape[0]):
        out_ref[i, at] = sums[:, i * LANES : (i + 1) * LANES].astype(BF16)


def outer_kernel(o0, o1, da0, da1, out_ref):
    store_slices(out_ref, 0, dot(o0[...], da0[...], 0, 0) + dot(o1[...], da1[...], 0, 0))


def outer_call(o_chunks, da_chunks):
    rows, width = da_chunks[0].shape
    cols = o_chunks[0].shape[1]
    out = (width // LANES, 1, cols, LANES)
    return pl.pallas_call(
        outer_kernel,
        out_shape=jax.ShapeDtypeStruct(out, BF16),
        compiler_params=vmem(60),
        cost_estimate=takes(5),
        name="outer_grad",
    )(*o_chunks, *da_chunks)


def proj_kernel(n_ref, d_ref, out_ref, acc):
    step = pl.program_id(0)
    for at in range(d_ref.shape[0]):
        sums = dot(d_ref[at], n_ref[...], 0, 0)

        @pl.when(step == 0)
        def _(sums=sums, at=at):
            acc[at] = sums

        @pl.when(step > 0)
        def _(sums=sums, at=at):
            store_slices(out_ref, at, acc[at] + sums)


def proj_call(n1, dproj):
    tokens, width = n1.shape
    kinds, _, cols = dproj.shape
    step = tokens // 2
    out = (width // LANES, kinds, cols, LANES)
    return pl.pallas_call(
        proj_kernel,
        out_shape=jax.ShapeDtypeStruct(out, BF16),
        grid=(2,),
        in_specs=[
            pl.BlockSpec((step, width), lambda i: (i, 0)),
            pl.BlockSpec((kinds, step, cols), lambda i: (0, i, 0)),
        ],
        out_specs=resident(out),
        scratch_shapes=[pltpu.VMEM((kinds, cols, width), F32)],
        compiler_params=vmem(60),
        cost_estimate=takes(8),
        name="proj_grads",
    )(n1, dproj)


def dn_kernel(p_ref, w_ref, out_ref):
    total = dot(p_ref[0], w_ref[0], 1, 1) + dot(p_ref[1], w_ref[1], 1, 1)
    out_ref[...] = (total + dot(p_ref[2], w_ref[2], 1, 1)).astype(BF16)


def dn_call(scalars, dproj, w_qkv, parity, rows, step=256):
    kinds, tokens, cols = dproj.shape
    width = w_qkv.shape[1]
    per = rows // step
    return pl.pallas_call(
        lambda s_ref, p_ref, w_ref, out_ref: dn_kernel(p_ref, w_ref, out_ref),
        out_shape=jax.ShapeDtypeStruct((2 * rows, width), BF16),
        grid_spec=pltpu.PrefetchScalarGridSpec(
            num_scalar_prefetch=1,
            grid=(2 * per,),
            in_specs=[
                pl.BlockSpec(
                    (kinds, step, cols),
                    lambda i, s: (0, ((2 * (i // per) + parity) ^ s[0]) * per + i % per, 0),
                ),
                resident((kinds, width, cols)),
            ],
            out_specs=pl.BlockSpec((step, width), lambda i, s: (i, 0)),
        ),
        compiler_params=vmem(60),
        cost_estimate=takes(6),
        name="dn",
    )(scalars, dproj, w_qkv)


def last_kernel(mine_ref, arrived_ref, x_ref, dx_ref, gain_ref, out_ref):
    dn = (mine_ref[...] + arrived_ref[...].astype(F32)).astype(BF16).astype(F32)
    normed, scale = row_stats(x_ref[...].astype(F32))
    out_ref[...] = (dx_ref[...] + pull_norm(normed, scale, dn * gain_ref[...])).astype(BF16)


def last_call(mine, arrived, x, dx, gain, step=256):
    rows, width = x.shape
    per = rows // step
    flat = pl.BlockSpec((step, width), lambda i: (i, 0))
    return pl.pallas_call(
        last_kernel,
        out_shape=jax.ShapeDtypeStruct((rows, width), BF16),
        grid=(per,),
        in_specs=[flat, flat, flat, flat, resident(gain.shape)],
        out_specs=flat,
        compiler_params=vmem(60),
        cost_estimate=takes(5),
        name="last",
    )(mine, arrived, x, dx, gain)


def bits_of(count):
    return [1 << i for i in range(count.bit_length() - 1)]


def pick(values, axis, index):
    return lax.dynamic_index_in_dim(values, index, axis, keepdims=False)


def by_device(values, count):
    blocks = values.shape[0]
    if blocks == count:
        return values
    axis = values.shape.index(LANES, 2)
    shape = values.shape[:axis] + (count // blocks, LANES * blocks // count) + values.shape[axis + 1 :]
    values = jnp.moveaxis(values.reshape(shape), axis, 1)
    return values.reshape((count,) + values.shape[2:])


def halve(values, axis_name, point):
    me = lax.axis_index(axis_name)
    carried = values
    for bit in bits_of(lax.axis_size(axis_name)):
        view = carried.reshape((carried.shape[0] // 2, 2) + carried.shape[1:])
        mine = (me // bit) % 2
        arrived = swap_bit(pick(view, 1, 1 - mine).astype(BF16), axis_name, bit)
        (arrived,) = after(point, arrived)
        carried = pick(view, 1, mine).astype(F32) + arrived.astype(F32)
    return carried[0]


def after(point, *values):
    return lax.optimization_barrier((point, *values))[1:]


def gather_bits(values, axis_name):
    me = lax.axis_index(axis_name)
    count = lax.axis_size(axis_name)
    shape = values.shape
    for bit in reversed(bits_of(count)):
        other = swap_bit(values, axis_name, bit)
        high = (me // bit) % 2 == 1
        values = jnp.stack([jnp.where(high, other, values), jnp.where(high, values, other)])
    lead = values.ndim - len(shape)
    order = tuple(reversed(range(lead))) + tuple(range(lead, values.ndim))
    return values.transpose(order).reshape((count,) + shape)


def scatter_lanes(values):
    me = lax.axis_index("mp")
    for bit in reversed(bits_of(lax.axis_size("mp"))):
        half = values.shape[-1] // 2
        low, top = values[..., :half], values[..., half:]
        high = (me // bit) % 2 == 1
        other = swap_bit(jnp.where(high, low, top), "mp", bit)
        values = jnp.where(high, top, low) + other
    return values


def local(
    hidden_in, out_grad, seq_lengths, dealing, attn_gain, mlp_gain, w_qkv, w_out, w_in, w_down
):
    dp_count = lax.axis_size("dp")
    mp_count = lax.axis_size("mp")
    owner = lax.axis_index("dp")
    lane = lax.axis_index("mp")
    rows, width = hidden_in.shape
    tokens = rows * mp_count
    shards = width // dp_count
    slots = rows // dp_count
    first_len = pick(seq_lengths, 0, 2 * owner)
    scalars = jnp.stack([lane, first_len, lane % 2, lane // 2]).astype(jnp.int32)

    lane_rows = pick(dealing.reshape(dp_count, mp_count, rows), 1, lane)
    local_row = lane_rows - (owner * mp_count + lane) * rows
    inside = (local_row >= 0) & (local_row < rows)
    order = jnp.arange(rows, dtype=jnp.int32)
    upto = (order[:, None] <= order[None, :]).astype(BF16)
    rank = dot(inside.astype(BF16), upto, 1, 0).astype(jnp.int32) - 1
    slot_hit = inside[:, None, :] & (rank[:, None, :] == jnp.arange(slots)[None, :, None])
    send_row = jnp.sum(jnp.where(slot_hit, local_row[:, None, :], 0), axis=2).reshape(rows)
    to_slot = (send_row[:, None] == order[None, :]).astype(BF16)
    source = pick(lane_rows, 0, owner) // (rows * mp_count)
    from_src = source[None, :] == jnp.arange(dp_count, dtype=jnp.int32)[:, None]
    src_rank = dot(from_src.astype(BF16), upto, 1, 0).astype(jnp.int32) - 1
    slot_of = source * slots + jnp.sum(jnp.where(from_src, src_rank, 0), axis=0)
    to_dealt = (slot_of[:, None] == order[None, :]).astype(BF16)

    def exchange(values):
        packed = values.reshape(dp_count, slots, width)
        arrived = lax.all_to_all(packed, "dp", split_axis=0, concat_axis=0, tiled=True)
        return arrived.reshape(rows, width)

    def pack(values):
        return dot(to_slot, values, 1, 0).astype(BF16)

    def unpack(values):
        return dot(to_dealt, values, 1, 0).astype(BF16)

    def pack_back(values):
        return dot(to_dealt, values, 0, 0).astype(BF16)

    def unpack_back(values):
        return dot(to_slot, values, 0, 0).astype(BF16)

    def group(values):
        across = swap_bit(values, "mp", 2)
        return [values, swap_bit(values, "mp", 1), across, swap_bit(across, "mp", 1)]

    gains = gather_bits(gather_bits(jnp.stack([attn_gain, mlp_gain]), "dp"), "mp")
    gains = gains.transpose(2, 1, 0, 3).reshape(2, width)
    w_mlp = jnp.concatenate([w_in, w_down.T[None]], axis=0)
    x_arrived = exchange(pack(hidden_in))
    x_arrived, g_packed, gains, w_mlp = lax.optimization_barrier(
        (x_arrived, pack(out_grad), gains, w_mlp)
    )
    w_mlp = lax.all_gather(w_mlp, "dp", axis=1, tiled=True)
    gain_one, gain_two = gains[0:1], gains[1:2]
    x_mine = unpack(x_arrived)
    x_rel = group(x_mine)
    attn_weights = jnp.concatenate([w_qkv, w_out.T[None]], axis=0)
    attn_weights = jnp.moveaxis(gather_bits(attn_weights, "dp"), 0, 1).reshape(4, width, -1)
    w_out_rel = group(attn_weights[3])
    g_arrived = exchange(g_packed)

    place = jnp.arange(tokens, dtype=jnp.int32)
    place = jnp.where(place >= first_len, place - first_len, place).astype(F32)
    freq_index = jnp.arange(LANES, dtype=jnp.int32) % (HEAD_DIM // 2)
    freqs = jnp.exp(freq_index.astype(F32) * (-2.0 * math.log(theta_base) / HEAD_DIM))
    angles = place[:, None] * freqs[None, :]
    first_half = jnp.arange(LANES) % HEAD_DIM < HEAD_DIM // 2
    cos = jnp.cos(angles)
    sin = jnp.sin(angles) * jnp.where(first_half, -1.0, 1.0)[None, :]

    held = qkv_call(scalars, x_rel[0], x_rel[1], gain_one, attn_weights, cos, sin, 0, ())
    q, k, v, n1 = qkv_call(scalars, x_rel[2], x_rel[3], gain_one, attn_weights, cos, sin, 2, held)
    (g_arrived,) = after(q, g_arrived)
    g_rel = group(unpack(g_arrived))
    near, q2, near_top = attend_forward(scalars, q, k, v, 0, 2 * rows, ())
    near_across = swap_bit(near, "mp", 2)
    distant, q2, far_top = attend_forward(scalars, q, k, v, 1, 2 * rows, (q2,))
    (distant,) = after(near_across, distant)
    far_across = swap_bit(distant, "mp", 2)
    core = lambda values: swap_bit(values, "mp", 1)
    far_heads = [distant, core(distant), near_across, core(near_across)]
    peaks = [near_top, far_top]
    head_peaks = jnp.max(jnp.stack(peaks), axis=(0, 1, 3, 4)) * score_scale
    peak_bits = bits_of(dp_count)
    peak_swap = swap_bit(head_peaks, "dp", peak_bits[0])

    *held, keep, send, keep_out, send_out = mlp_call(
        scalars,
        (x_rel[3], x_rel[2]),
        (g_rel[3], g_rel[2]),
        far_heads,
        w_out_rel,
        gain_two,
        w_mlp,
        2,
        (),
    )
    far_across, peak_swap, send, near = lax.optimization_barrier(
        (far_across, peak_swap, send, near)
    )
    head_peaks = jnp.maximum(head_peaks, peak_swap)
    peak_swap = swap_bit(head_peaks, "dp", peak_bits[1])
    dn_far = (keep + core(send).astype(F32)).astype(BF16)
    dn_arrived = swap_bit(dn_far, "mp", 2)
    near_heads = [near, core(near), far_across, core(far_across)]
    (near_heads[0],) = after(dn_far, near)
    far_out = (keep_out, send_out)
    a_rel, n2, act, dgate, dup, keep, send, keep_out, send_out = mlp_call(
        scalars,
        (x_rel[1], x_rel[0]),
        (g_rel[1], g_rel[0]),
        near_heads,
        w_out_rel,
        gain_two,
        w_mlp,
        0,
        held,
    )
    dn_arrived, peak_swap, send = lax.optimization_barrier((dn_arrived, peak_swap, send))
    head_peaks = jnp.maximum(head_peaks, peak_swap)
    peak_swap = swap_bit(head_peaks, "dp", peak_bits[2])
    dx, da = resid_call(
        keep + core(send).astype(F32), dn_arrived, x_rel[0], a_rel, g_rel[0], gain_two
    )
    da_core, da_across = core(da), swap_bit(da, "mp", 2)

    flat = lambda values: values.reshape(tokens, values.shape[2])
    (act,) = after(da, act)
    inner_grads = inner_call(flat(n2), g_rel, flat(dgate), flat(dup), flat(act))
    inner_grads, da_across, peak_swap = lax.optimization_barrier((inner_grads, da_across, peak_swap))
    head_peaks = jnp.maximum(head_peaks, peak_swap)
    for bit in peak_bits[3:]:
        head_peaks = jnp.maximum(head_peaks, swap_bit(head_peaks, "dp", bit))
    da_rel = [da, da_core, da_across, core(da_across)]
    inner_grads = lax.psum_scatter(by_device(inner_grads, dp_count), "dp").astype(F32)
    inner_grad, down_grad = inner_grads[:2], inner_grads[2].T

    do, da_near = head_grad_call(
        scalars, da_rel[0], da_rel[1], attn_weights[3], near, 0, tokens, ()
    )
    do, da_far = head_grad_call(
        scalars, da_rel[2], da_rel[3], attn_weights[3], distant, 1, tokens, (do,)
    )
    outer_grad = outer_call((near, distant), (da_near, da_far))
    outer_grad = by_device(outer_grad, dp_count)
    outer_grad = lax.all_to_all(outer_grad, "dp", split_axis=0, concat_axis=0, tiled=True)

    far_out = after(da_across, *far_out)
    add_core = lambda keep, send: keep.astype(F32) + core(send).astype(F32)

    factor = jnp.sqrt(clip_limit / jnp.maximum(head_peaks, clip_limit))
    column_factor = jnp.repeat(factor, HEAD_DIM)
    scaling = jnp.stack([column_factor, column_factor, jnp.ones_like(column_factor)])[:, None, :]
    clipped = (w_qkv.astype(F32) * scaling).astype(BF16)

    out_far = add_core(*far_out).astype(BF16)
    out_arrived = swap_bit(out_far, "mp", 2)
    do, out_sum = after(out_far, do, add_core(keep_out, send_out))
    dproj = attend_backward(scalars, q2, k, v, do, cos, sin)
    send = dn_call(scalars, dproj, attn_weights, 1, rows)
    out_arrived, outer_grad, send = lax.optimization_barrier((out_arrived, outer_grad, send))
    outer_grad = jnp.sum(outer_grad.astype(F32), axis=0)[0]
    keep = dn_call(scalars, dproj, attn_weights, 0, rows)
    both = keep.astype(F32) + core(send).astype(F32)
    dn_own, dn_far = both[:rows], both[rows:].astype(BF16)
    dn_arrived = swap_bit(dn_far, "mp", 2)
    (out_arrived,) = after(dn_far, out_arrived)
    x1 = x_rel[0].astype(F32) + a_rel[0].astype(F32)
    out_packed = pack_back((x1 + (out_sum + out_arrived.astype(F32))).astype(BF16))
    (n1,) = after(out_packed, n1)
    proj_grad = proj_call(n1, dproj)
    (dn_arrived,) = after(proj_grad, dn_arrived)
    grad_packed = pack_back(last_call(dn_own, dn_arrived, x_rel[0], dx, gain_one))
    input_grad = unpack_back(exchange(grad_packed))
    (out_arrived,) = after(grad_packed, exchange(out_packed))
    output = unpack_back(out_arrived)
    proj_grad = halve(by_device(proj_grad, dp_count), "dp", grad_packed)
    proj_grad = jnp.swapaxes(proj_grad, 1, 2)

    by_gain = jnp.stack(
        [
            jnp.sum(proj_grad * w_qkv.astype(F32), axis=(0, 2)),
            jnp.sum(inner_grad * w_in.astype(F32), axis=(0, 2)),
        ]
    )
    gain_part = lax.dynamic_slice_in_dim(gains, owner * shards, shards, 1)
    gain_grads = scatter_lanes(by_gain / gain_part)
    return (
        output,
        input_grad,
        gain_grads[0],
        gain_grads[1],
        proj_grad,
        outer_grad,
        inner_grad,
        down_grad,
        clipped,
    )


def solution(mesh):
    in_specs = (
        P(("dp", "mp"), None),
        P(("dp", "mp"), None),
        P(),
        P(),
        P(("dp", "mp")),
        P(("dp", "mp")),
        P(None, "dp", "mp"),
        P("mp", "dp"),
        P(None, "dp", "mp"),
        P("mp", "dp"),
    )
    out_specs = (
        P(("dp", "mp"), None),
        P(("dp", "mp"), None),
        P(("dp", "mp")),
        P(("dp", "mp")),
        P(None, "dp", "mp"),
        P("mp", "dp"),
        P(None, "dp", "mp"),
        P("mp", "dp"),
        P(None, "dp", "mp"),
    )
    return jax.shard_map(local, mesh=mesh, in_specs=in_specs, out_specs=out_specs, check_vma=False)
```

```python
import functools
import math

import jax
import jax.numpy as jnp
from jax import lax
from jax.experimental import pallas as pl
from jax.experimental.pallas import tpu as pltpu
from jax.sharding import PartitionSpec as P

HEAD_DIM = 64
LANES = 128
theta_base = 160000.0
norm_eps = 1e-05
clip_limit = 5.0
score_scale = 0.125
exp_scale = score_scale * math.log2(math.e)
far_away = -1e30
lowest = -3e38

BF16 = jnp.bfloat16
F32 = jnp.float32


def dot(left, right, left_dim, right_dim):
    return lax.dot_general(
        left, right, (((left_dim,), (right_dim,)), ((), ())), preferred_element_type=F32
    )


def split_three(values):
    high = values.astype(BF16).astype(F32)
    rest = values - high
    middle = rest.astype(BF16).astype(F32)
    return high, middle, rest - middle


def row_stats(values):
    mean = jnp.mean(values, axis=-1, keepdims=True)
    centered = values - mean
    variance = jnp.mean(centered * centered, axis=-1, keepdims=True)
    scale = lax.rsqrt(variance + norm_eps)
    return centered * scale, scale


def turn(values, lane):
    return jnp.where(
        lane % HEAD_DIM < HEAD_DIM // 2,
        pltpu.roll(values, LANES - HEAD_DIM // 2, 1),
        pltpu.roll(values, HEAD_DIM // 2, 1),
    )


def swap_bit(values, axis_name, bit):
    count = lax.axis_size(axis_name)
    return lax.ppermute(values, axis_name, [(i, i ^ bit) for i in range(count)])


def lane_iota(rows):
    return lax.broadcasted_iota(jnp.int32, (rows, LANES), 1)


def vmem(mib):
    return pltpu.CompilerParams(vmem_limit_bytes=mib << 20)


def takes(micros):
    flops = max(micros * 1_100_000_000, 1024)
    return pl.CostEstimate(flops=flops, bytes_accessed=flops // 1024, transcendentals=0)


def resident(shape):
    zeros = (0,) * len(shape)
    return pl.BlockSpec(shape, lambda *_: zeros, pipeline_mode=pl.Buffered(1))


def qkv_kernel(step, per, first, s_ref, xa_ref, xb_ref, gain_ref, w_ref, cos_ref, sin_ref, *rest):
    q_ref, k_ref, v_ref, n_ref = rest[-4:]
    first_len = s_ref[1]
    at = pl.program_id(0)
    x = jnp.where(at < per, xa_ref[...], xb_ref[...])
    normed, _ = row_stats(x.astype(F32))
    n1 = (normed * gain_ref[...]).astype(BF16)
    n_ref[...] = n1
    lane = lane_iota(step)
    start = (((first + at // per) ^ s_ref[0]) * per + at % per) * step
    row = start + lax.broadcasted_iota(jnp.int32, (step, LANES), 0)
    second = row >= first_len
    one, zero = jnp.float32(1), jnp.float32(0)
    q_tail = jnp.where(lane == 64 + second.astype(jnp.int32), one, zero)
    k_tail = jnp.where(
        lane == 65 - second.astype(jnp.int32),
        jnp.float32(far_away),
        jnp.where((lane >= 66) & (lane < 69), one, zero),
    )
    cos, sin = cos_ref[...], sin_ref[...]
    for which, (out, tail) in enumerate(((q_ref, q_tail), (k_ref, k_tail), (v_ref, one))):
        projected = dot(n1, w_ref[which], 1, 0)
        for pair in range(projected.shape[1] // LANES):
            part = projected[:, pair * LANES : (pair + 1) * LANES]
            if which < 2:
                part = part * cos + turn(part, lane) * sin
            out[2 * pair] = jnp.where(lane < HEAD_DIM, part, tail).astype(BF16)
            out[2 * pair + 1] = jnp.where(
                lane < HEAD_DIM, pltpu.roll(part, HEAD_DIM, 1), tail
            ).astype(BF16)


def qkv_call(scalars, xa, xb, gain, w_qkv, cos, sin, first, held, step=512):
    rows, width = xa.shape
    tokens = cos.shape[0]
    cols = w_qkv.shape[2]
    heads = cols // HEAD_DIM
    per = rows // step
    ext = jax.ShapeDtypeStruct((heads, tokens, LANES), BF16)
    place = lambda i, s: (((first + i // per) ^ s[0]) * per + i % per, 0)
    head_spec = pl.BlockSpec((heads, step, LANES), lambda i, s: (0, *place(i, s)))
    held = list(held)
    return pl.pallas_call(
        functools.partial(qkv_kernel, step, per, first),
        out_shape=(ext, ext, ext, jax.ShapeDtypeStruct((tokens, width), BF16)),
        grid_spec=pltpu.PrefetchScalarGridSpec(
            num_scalar_prefetch=1,
            grid=(2 * per,),
            in_specs=[
                pl.BlockSpec((step, width), lambda i, s: (jnp.minimum(i, per - 1), 0)),
                pl.BlockSpec((step, width), lambda i, s: (jnp.maximum(i - per, 0), 0)),
                resident(gain.shape),
                resident((3, width, cols)),
                pl.BlockSpec((step, LANES), place),
                pl.BlockSpec((step, LANES), place),
            ]
            + [pl.BlockSpec(memory_space=pl.ANY)] * len(held),
            out_specs=[head_spec] * 3 + [pl.BlockSpec((step, width), place)],
        ),
        input_output_aliases={7 + i: i for i in range(len(held))},
        compiler_params=vmem(48),
        cost_estimate=takes(3),
        name="qkv",
    )(scalars, xa, xb, gain, w_qkv, cos, sin, *held)


def key_range(first_len, row, q_rows, k_rows, tokens):
    low = jnp.where(row >= first_len, first_len // k_rows, 0)
    high = jnp.where(row + q_rows <= first_len, (first_len + k_rows - 1) // k_rows, tokens // k_rows)
    return low, high


def fwd_kernel(
    far, q_rows, k_rows, s_ref, q_ref, k_ref, v_ref, *rest
):
    o_ref, q2_ref, top_ref, score, peak, acc = rest[-6:]
    heads, tokens, _ = k_ref.shape
    low, high = key_range(
        s_ref[1],
        ((s_ref[3] ^ far) * pl.num_programs(0) + pl.program_id(0)) * q_rows,
        q_rows,
        k_rows,
        tokens,
    )
    lane = lane_iota(q_rows)
    peak[...] = jnp.full(peak.shape, lowest, F32)
    acc[...] = jnp.zeros(acc.shape, F32)

    def first_pass(block, carry):
        keys = pl.ds(pl.multiple_of(block * k_rows, k_rows), k_rows)
        for h in range(heads):
            s = dot(q_ref[h], k_ref[h, keys, :], 1, 1)
            score[h, :, keys] = s
            most = peak[h]
            for t in range(k_rows // LANES):
                most = jnp.maximum(most, s[:, t * LANES : (t + 1) * LANES])
            peak[h] = most
        return carry

    lax.fori_loop(low, high, first_pass, 0)
    for h in range(heads):
        peak[h] = jnp.broadcast_to(jnp.max(peak[h], axis=1, keepdims=True), (q_rows, LANES))

    def second_pass(block, carry):
        keys = pl.ds(pl.multiple_of(block * k_rows, k_rows), k_rows)
        for h in range(heads):
            s, most = score[h, :, keys], peak[h]
            p = jnp.concatenate(
                [
                    jnp.exp2((s[:, t * LANES : (t + 1) * LANES] - most) * exp_scale).astype(BF16)
                    for t in range(k_rows // LANES)
                ],
                axis=1,
            )
            acc[h] += dot(p, v_ref[h, keys, :], 1, 0)
        return carry

    lax.fori_loop(low, high, second_pass, 0)
    held = None
    for h in range(heads):
        sums = acc[h]
        total = jnp.where(lane < HEAD_DIM, pltpu.roll(sums, HEAD_DIM, 1), sums)
        out = sums / total
        log_total = peak[h] + jnp.log2(total) * (1.0 / exp_scale)
        a, b, c = split_three(-log_total)
        q2 = q_ref[h].astype(F32)
        q2 = jnp.where(lane == 66, a, jnp.where(lane == 67, b, jnp.where(lane == 68, c, q2)))
        q2_ref[h] = q2.astype(BF16)
        top_ref[h] = jnp.broadcast_to(jnp.max(peak[h], axis=0, keepdims=True), (8, LANES))
        if h % 2 == 0:
            held = out
        else:
            both = jnp.where(lane < HEAD_DIM, held, pltpu.roll(out, HEAD_DIM, 1))
            o_ref[:, (h // 2) * LANES : (h // 2 + 1) * LANES] = both.astype(BF16)


def attend_forward(scalars, q, k, v, far, rows, held, q_rows=256, k_rows=512):
    heads, tokens, _ = k.shape
    count = rows // q_rows
    k_rows = min(k_rows, tokens)
    return pl.pallas_call(
        functools.partial(fwd_kernel, far, q_rows, k_rows),
        out_shape=(
            jax.ShapeDtypeStruct((rows, heads * HEAD_DIM), BF16),
            jax.ShapeDtypeStruct(q.shape, BF16),
            jax.ShapeDtypeStruct((count, heads, 8, LANES), F32),
        ),
        grid_spec=pltpu.PrefetchScalarGridSpec(
            num_scalar_prefetch=1,
            grid=(count,),
            in_specs=[
                pl.BlockSpec((heads, q_rows, LANES), lambda i, s: (0, (s[3] ^ far) * count + i, 0)),
                resident(k.shape),
                resident(v.shape),
            ]
            + [pl.BlockSpec(memory_space=pl.ANY)] * len(held),
            out_specs=[
                pl.BlockSpec((q_rows, heads * HEAD_DIM), lambda i, s: (i, 0)),
                pl.BlockSpec((heads, q_rows, LANES), lambda i, s: (0, (s[3] ^ far) * count + i, 0)),
                pl.BlockSpec((None, heads, 8, LANES), lambda i, s: (i, 0, 0, 0)),
            ],
            scratch_shapes=[
                pltpu.VMEM((heads, q_rows, tokens), F32),
                pltpu.VMEM((heads, q_rows, LANES), F32),
                pltpu.VMEM((heads, q_rows, LANES), F32),
            ],
        ),
        compiler_params=vmem(48),
        cost_estimate=takes(20),
        input_output_aliases={4 + i: 1 + i for i in range(len(held))},
        name="attend_forward",
    )(scalars, q, k, v, *held)


def bwd_kernel(
    q_rows, k_rows, s_ref, q2_ref, k_ref, v_ref, do_ref, cos_ref, sin_ref, out_ref, dk_ref, dv_ref
):
    heads, tokens, _ = k_ref.shape
    step = pl.program_id(0)
    low, high = key_range(s_ref[1], step * q_rows, q_rows, k_rows, tokens)

    @pl.when(step == 0)
    def _():
        dk_ref[...] = jnp.zeros_like(dk_ref)
        dv_ref[...] = jnp.zeros_like(dv_ref)

    def body(block, sums):
        keys = pl.ds(pl.multiple_of(block * k_rows, k_rows), k_rows)
        new = []
        for h in range(heads):
            key, q2, do = k_ref[h, keys, :], q2_ref[h], do_ref[h]
            p = jnp.exp2(dot(key, q2, 1, 1) * exp_scale)
            ds = (p * dot(v_ref[h, keys, :], do, 1, 1)).astype(BF16)
            dv_ref[h, keys, :] += dot(p.astype(BF16), do, 1, 0)
            dk_ref[h, keys, :] += dot(ds, q2, 1, 0)
            new.append(sums[h] + dot(key, ds, 0, 0))
        return tuple(new)

    sums = lax.fori_loop(
        low, high, body, tuple(jnp.zeros((LANES, q_rows), F32) for _ in range(heads))
    )
    lane = lane_iota(q_rows)

    def unrotate(first, second, rows):
        both = jnp.where(lane < HEAD_DIM, first, pltpu.roll(second, HEAD_DIM, 1)) * score_scale
        return both * cos_ref[rows, :] - turn(both, lane) * sin_ref[rows, :]

    here = pl.ds(pl.multiple_of(step * q_rows, q_rows), q_rows)
    for pair in range(heads // 2):
        cols = slice(pair * LANES, (pair + 1) * LANES)
        out_ref[0, here, cols] = unrotate(sums[2 * pair].T, sums[2 * pair + 1].T, here).astype(BF16)

    @pl.when(step == pl.num_programs(0) - 1)
    def _():
        def finish(block, carry):
            rows = pl.ds(pl.multiple_of(block * q_rows, q_rows), q_rows)
            for pair in range(heads // 2):
                cols = slice(pair * LANES, (pair + 1) * LANES)
                one, two = 2 * pair, 2 * pair + 1
                out_ref[1, rows, cols] = unrotate(
                    dk_ref[one, rows, :], dk_ref[two, rows, :], rows
                ).astype(BF16)
                out_ref[2, rows, cols] = jnp.where(
                    lane < HEAD_DIM,
                    dv_ref[one, rows, :],
                    pltpu.roll(dv_ref[two, rows, :], HEAD_DIM, 1),
                ).astype(BF16)
            return carry

        lax.fori_loop(0, tokens // q_rows, finish, 0)


def attend_backward(scalars, q2, k, v, do, cos, sin, q_rows=256, k_rows=512):
    heads, tokens, _ = k.shape
    block = lambda: pl.BlockSpec((heads, q_rows, LANES), lambda i, s: (0, i, 0))
    out = (3, tokens, heads * HEAD_DIM)
    return pl.pallas_call(
        functools.partial(bwd_kernel, q_rows, k_rows),
        out_shape=jax.ShapeDtypeStruct(out, BF16),
        grid_spec=pltpu.PrefetchScalarGridSpec(
            num_scalar_prefetch=1,
            grid=(tokens // q_rows,),
            in_specs=[
                block(),
                resident(k.shape),
                resident(v.shape),
                block(),
                resident(cos.shape),
                resident(sin.shape),
            ],
            out_specs=resident(out),
            scratch_shapes=[
                pltpu.VMEM((heads, tokens, LANES), F32),
                pltpu.VMEM((heads, tokens, LANES), F32),
            ],
        ),
        compiler_params=vmem(48),
        cost_estimate=takes(57),
        name="attend_backward",
    )(scalars, q2, k, v, do, cos, sin)


def mlp_kernel(
    s_ref, xs_ref, xk_ref, gs_ref, gk_ref, o0, o1, o2, o3, w0, w1, w2, w3, gain_ref, w_ref, *rest
):
    a_ref, n_ref, g_out, act_ref, dgate_ref, dup_ref = rest[-10:-4]
    keep_ref, send_ref, keep_out, send_out = rest[-4:]
    units = w_ref.shape[2]
    sending = pl.program_id(0) < pl.num_programs(0) // 2
    x = jnp.where(sending, xs_ref[...], xk_ref[...])
    g = jnp.where(sending, gs_ref[...], gk_ref[...])
    branch = dot(o0[...], w0[...], 1, 1) + dot(o1[...], w1[...], 1, 1)
    branch = branch + dot(o2[...], w2[...], 1, 1) + dot(o3[...], w3[...], 1, 1)
    branch = branch.astype(BF16)
    a_ref[...] = branch
    normed, _ = row_stats(x.astype(F32) + branch.astype(F32))
    n2 = (normed * gain_ref[...]).astype(BF16)
    n_ref[...] = n2
    g_out[...] = g
    partial = out_partial = 0.0
    for low in range(0, units, 256):
        cols = slice(low, min(low + 256, units))
        gate = dot(n2, w_ref[0, :, cols], 1, 0)
        up = dot(n2, w_ref[1, :, cols], 1, 0)
        dact = dot(g, w_ref[2, :, cols], 1, 0)
        phi = 0.5 + 0.5 * lax.erf(gate * math.sqrt(0.5))
        gelu = gate * phi
        act = (gelu * up).astype(BF16)
        act_ref[:, cols] = act
        density = jnp.exp(-0.5 * gate * gate) * (1.0 / math.sqrt(2.0 * math.pi))
        dgate = (dact * up * (phi + gate * density)).astype(BF16)
        dup = (dact * gelu).astype(BF16)
        dgate_ref[:, cols] = dgate
        dup_ref[:, cols] = dup
        partial = partial + dot(dgate, w_ref[0, :, cols], 1, 1) + dot(dup, w_ref[1, :, cols], 1, 1)
        out_partial = out_partial + dot(act, w_ref[2, :, cols], 1, 1)

    @pl.when(sending)
    def _():
        send_ref[...] = partial.astype(BF16)
        send_out[...] = out_partial.astype(BF16)

    @pl.when(jnp.logical_not(sending))
    def _():
        keep_ref[...] = partial
        keep_out[...] = out_partial.astype(BF16)


def mlp_call(scalars, x_pair, g_pair, heads_rel, w_out_rel, gain, w_mlp, first, held, step=256):
    rows, width = x_pair[0].shape
    units = w_mlp.shape[2]
    per = rows // step
    rel = lambda i, s: (first + 1 - i // per, i % per, 0)
    wide = pl.BlockSpec((None, step, width), rel)
    narrow = pl.BlockSpec((None, step, units), rel)
    wide_out = jax.ShapeDtypeStruct((4, rows, width), BF16)
    narrow_out = jax.ShapeDtypeStruct((4, rows, units), BF16)
    send = pl.BlockSpec((step, width), lambda i, s: (jnp.minimum(i, per - 1), 0))
    keep = pl.BlockSpec((step, width), lambda i, s: (jnp.maximum(i - per, 0), 0))
    head_spec = pl.BlockSpec(
        (step, heads_rel[0].shape[1]), lambda i, s: (((i // per) ^ 1 ^ s[2]) * per + i % per, 0)
    )
    held = list(held)
    half = lambda kind: jax.ShapeDtypeStruct((rows, width), kind)
    return pl.pallas_call(
        mlp_kernel,
        out_shape=(
            wide_out,
            wide_out,
            wide_out,
            narrow_out,
            narrow_out,
            narrow_out,
            half(F32),
            half(BF16),
            half(BF16),
            half(BF16),
        ),
        grid_spec=pltpu.PrefetchScalarGridSpec(
            num_scalar_prefetch=1,
            grid=(2 * per,),
            in_specs=[send, keep, send, keep]
            + [head_spec] * len(heads_rel)
            + [resident(w.shape) for w in w_out_rel]
            + [resident(gain.shape), resident(w_mlp.shape)]
            + [pl.BlockSpec(memory_space=pl.ANY)] * len(held),
            out_specs=[wide, wide, wide, narrow, narrow, narrow, keep, send, keep, send],
        ),
        input_output_aliases={15 + i: i for i in range(len(held))},
        compiler_params=vmem(48),
        cost_estimate=takes(24),
        name="mlp",
    )(scalars, *x_pair, *g_pair, *heads_rel, *w_out_rel, gain, w_mlp, *held)


def pull_norm(normed, scale, cotangent):
    mean = jnp.mean(cotangent, axis=-1, keepdims=True)
    along = jnp.mean(cotangent * normed, axis=-1, keepdims=True)
    return (cotangent - mean - normed * along) * scale


def resid_kernel(keep_ref, core_ref, chip_ref, x_ref, a_ref, g_ref, gain_ref, dx_ref, da_ref):
    dn = keep_ref[...] + core_ref[...].astype(F32) + chip_ref[...].astype(F32)
    normed, scale = row_stats(x_ref[...].astype(F32) + a_ref[...].astype(F32))
    dx = g_ref[...].astype(F32) + pull_norm(normed, scale, dn * gain_ref[...])
    dx_ref[...] = dx
    da_ref[...] = dx.astype(BF16)


def resid_call(keep, core, chip, x, a_rel, g, gain, step=256):
    rows, width = keep.shape
    per = rows // step
    flat = pl.BlockSpec((step, width), lambda i: (i, 0))
    return pl.pallas_call(
        resid_kernel,
        out_shape=(
            jax.ShapeDtypeStruct((rows, width), F32),
            jax.ShapeDtypeStruct((rows, width), BF16),
        ),
        grid=(per,),
        in_specs=[
            flat,
            flat,
            flat,
            flat,
            pl.BlockSpec((None, step, width), lambda i: (0, i, 0)),
            flat,
            resident(gain.shape),
        ],
        out_specs=[flat, flat],
        compiler_params=vmem(48),
        cost_estimate=takes(5),
        name="resid",
    )(keep, core, chip, x, a_rel, g, gain)


def head_grad_kernel(s_ref, even_ref, odd_ref, w_ref, o_ref, *rest):
    do_ref, da_ref = rest[-2:]
    own = pl.program_id(0) == s_ref[2]
    da = jnp.where(own, even_ref[...], odd_ref[...])
    da_ref[...] = da
    do = dot(da, w_ref[...], 1, 0).astype(BF16).astype(F32)
    rows = do.shape[0]
    lane = lane_iota(rows)
    product = do * o_ref[...].astype(F32)
    for pair in range(do.shape[1] // LANES):
        cols = slice(pair * LANES, (pair + 1) * LANES)
        part = do[:, cols]
        for odd in range(2):
            inside = (lane >= HEAD_DIM) if odd else (lane < HEAD_DIM)
            delta = jnp.sum(jnp.where(inside, product[:, cols], 0.0), axis=1, keepdims=True)
            a, b, c = split_three(jnp.broadcast_to(-delta, (rows, LANES)))
            head = pltpu.roll(part, HEAD_DIM, 1) if odd else part
            tail = jnp.where(
                lane == 64, a, jnp.where(lane == 65, b, jnp.where(lane == 66, c, 0.0))
            )
            do_ref[2 * pair + odd] = jnp.where(lane < HEAD_DIM, head, tail).astype(BF16)


def head_grad_call(scalars, even, odd, w_out, o_chunk, far, tokens, held):
    rows, width = even.shape
    heads = o_chunk.shape[1] // HEAD_DIM
    held = list(held)
    return pl.pallas_call(
        head_grad_kernel,
        out_shape=(
            jax.ShapeDtypeStruct((heads, tokens, LANES), BF16),
            jax.ShapeDtypeStruct((tokens, width), BF16),
        ),
        grid_spec=pltpu.PrefetchScalarGridSpec(
            num_scalar_prefetch=1,
            grid=(2,),
            in_specs=[
                resident(even.shape),
                resident(odd.shape),
                resident(w_out.shape),
                pl.BlockSpec((rows, o_chunk.shape[1]), lambda i, s: (i, 0)),
            ]
            + [pl.BlockSpec(memory_space=pl.ANY)] * len(held),
            out_specs=[
                pl.BlockSpec((heads, rows, LANES), lambda i, s: (0, 2 * (s[3] ^ far) + i, 0)),
                pl.BlockSpec((rows, width), lambda i, s: (2 * far + i, 0)),
            ],
        ),
        input_output_aliases={5 + i: i for i in range(len(held))},
        compiler_params=vmem(48),
        cost_estimate=takes(6),
        name="head_grad",
    )(scalars, even, odd, w_out, o_chunk, *held)


def store_slices(out_ref, at, sums):
    for i in range(out_ref.shape[0]):
        out_ref[i, at] = sums[:, i * LANES : (i + 1) * LANES].astype(BF16)


def inner_kernel(n_ref, g_ref, dgate_ref, dup_ref, act_ref, out_ref, acc):
    step, last = pl.program_id(0), pl.num_programs(0) - 1
    for at, (right, left) in enumerate(((dgate_ref, n_ref), (dup_ref, n_ref), (act_ref, g_ref))):
        sums = dot(right[...], left[...], 0, 0)

        @pl.when(step == 0)
        def _(sums=sums, at=at):
            acc[at] = sums

        @pl.when((step > 0) & (step < last))
        def _(sums=sums, at=at):
            acc[at] += sums

        @pl.when(step == last)
        def _(sums=sums, at=at):
            store_slices(out_ref, at, acc[at] + sums)


def inner_call(n2, g_rel, dgate, dup, act, steps=4):
    tokens, width = n2.shape
    units = act.shape[1]
    step = tokens // steps
    out = (width // LANES, 3, units, LANES)
    wide = pl.BlockSpec((step, width), lambda i: (i, 0))
    narrow = pl.BlockSpec((step, units), lambda i: (i, 0))
    return pl.pallas_call(
        inner_kernel,
        out_shape=jax.ShapeDtypeStruct(out, BF16),
        grid=(steps,),
        in_specs=[wide, wide, narrow, narrow, narrow],
        out_specs=resident(out),
        scratch_shapes=[pltpu.VMEM((3, units, width), F32)],
        compiler_params=vmem(48),
        cost_estimate=takes(18),
        name="inner_grads",
    )(n2, g_rel, dgate, dup, act)


def proj_kernel(n_ref, d_ref, o0, o1, da_ref, out_ref, acc):
    step = pl.program_id(0)
    kinds = d_ref.shape[0]

    @pl.when(step == 0)
    def _():
        for at in range(kinds):
            acc[at] = dot(d_ref[at], n_ref[...], 0, 0)
        acc[kinds] = dot(o0[...], da_ref[...], 0, 0)

    @pl.when(step == 1)
    def _():
        for at in range(kinds):
            store_slices(out_ref, at, acc[at] + dot(d_ref[at], n_ref[...], 0, 0))
        store_slices(out_ref, kinds, acc[kinds] + dot(o1[...], da_ref[...], 0, 0))


def proj_call(n1, dproj, o_chunks, da):
    tokens, width = n1.shape
    kinds, _, cols = dproj.shape
    step = tokens // 2
    out = (width // LANES, kinds + 1, cols, LANES)
    wide = pl.BlockSpec((step, width), lambda i: (i, 0))
    return pl.pallas_call(
        proj_kernel,
        out_shape=jax.ShapeDtypeStruct(out, BF16),
        grid=(2,),
        in_specs=[
            wide,
            pl.BlockSpec((kinds, step, cols), lambda i: (0, i, 0)),
            resident(o_chunks[0].shape),
            resident(o_chunks[1].shape),
            wide,
        ],
        out_specs=resident(out),
        scratch_shapes=[pltpu.VMEM((kinds + 1, cols, width), F32)],
        compiler_params=vmem(48),
        cost_estimate=takes(10),
        name="proj_grads",
    )(n1, dproj, *o_chunks, da)


def dn_kernel(s_ref, p_ref, w_ref, out_ref):
    total = dot(p_ref[0], w_ref[0], 1, 1) + dot(p_ref[1], w_ref[1], 1, 1)
    out_ref[...] = (total + dot(p_ref[2], w_ref[2], 1, 1)).astype(BF16)


def dn_call(scalars, dproj, w_qkv, rel, rows):
    kinds, _, cols = dproj.shape
    width = w_qkv.shape[1]
    return pl.pallas_call(
        dn_kernel,
        out_shape=jax.ShapeDtypeStruct((rows, width), BF16),
        grid_spec=pltpu.PrefetchScalarGridSpec(
            num_scalar_prefetch=1,
            grid=(1,),
            in_specs=[
                pl.BlockSpec((kinds, rows, cols), lambda i, s: (0, rel ^ s[0], 0)),
                resident((kinds, width, cols)),
            ],
            out_specs=pl.BlockSpec((rows, width), lambda i, s: (0, 0)),
        ),
        compiler_params=vmem(48),
        cost_estimate=takes(0),
        name="dn",
    )(scalars, dproj, w_qkv)


def last_kernel(keep_ref, core_ref, chip_ref, x_ref, dx_ref, gain_ref, out_ref):
    dn = keep_ref[...].astype(F32) + core_ref[...].astype(F32) + chip_ref[...].astype(F32)
    dn = dn.astype(BF16).astype(F32)
    normed, scale = row_stats(x_ref[...].astype(F32))
    out_ref[...] = (dx_ref[...] + pull_norm(normed, scale, dn * gain_ref[...])).astype(BF16)


def last_call(keep, core, chip, x, dx, gain, step=256):
    rows, width = x.shape
    per = rows // step
    flat = pl.BlockSpec((step, width), lambda i: (i, 0))
    return pl.pallas_call(
        last_kernel,
        out_shape=jax.ShapeDtypeStruct((rows, width), BF16),
        grid=(per,),
        in_specs=[flat] * 5 + [resident(gain.shape)],
        out_specs=flat,
        compiler_params=vmem(48),
        cost_estimate=takes(5),
        name="last",
    )(keep, core, chip, x, dx, gain)


def turn_rows_kernel(hot_ref, rows_ref, out_ref):
    out_ref[...] = dot(hot_ref[...], rows_ref[...], 0, 0).astype(BF16)


def turn_rows(one_hot, values):
    return pl.pallas_call(
        turn_rows_kernel,
        out_shape=jax.ShapeDtypeStruct(values.shape, BF16),
        compiler_params=vmem(48),
        cost_estimate=takes(2),
        name="turn_rows",
    )(one_hot, values)


def bits_of(count):
    return [1 << i for i in range(count.bit_length() - 1)]


def pick(values, axis, index):
    return lax.dynamic_index_in_dim(values, index, axis, keepdims=False)


def by_device(values, count):
    blocks = values.shape[0]
    if blocks == count:
        return values
    axis = values.shape.index(LANES, 2)
    shape = values.shape[:axis] + (count // blocks, LANES * blocks // count) + values.shape[axis + 1 :]
    values = jnp.moveaxis(values.reshape(shape), axis, 1)
    return values.reshape((count,) + values.shape[2:])


def after(point, *values):
    return lax.optimization_barrier((point, *values))[1:]


def gather_bits(values, axis_name):
    me = lax.axis_index(axis_name)
    count = lax.axis_size(axis_name)
    shape = values.shape
    for bit in reversed(bits_of(count)):
        other = swap_bit(values, axis_name, bit)
        high = (me // bit) % 2 == 1
        values = jnp.stack([jnp.where(high, other, values), jnp.where(high, values, other)])
    lead = values.ndim - len(shape)
    order = tuple(reversed(range(lead))) + tuple(range(lead, values.ndim))
    return values.transpose(order).reshape((count,) + shape)


def scatter_lanes(values):
    me = lax.axis_index("mp")
    for bit in reversed(bits_of(lax.axis_size("mp"))):
        half = values.shape[-1] // 2
        low, top = values[..., :half], values[..., half:]
        high = (me // bit) % 2 == 1
        other = swap_bit(jnp.where(high, low, top), "mp", bit)
        values = jnp.where(high, top, low) + other
    return values


def local(
    hidden_in, out_grad, seq_lengths, dealing, attn_gain, mlp_gain, w_qkv, w_out, w_in, w_down
):
    dp_count = lax.axis_size("dp")
    mp_count = lax.axis_size("mp")
    owner = lax.axis_index("dp")
    lane = lax.axis_index("mp")
    rows, width = hidden_in.shape
    tokens = rows * mp_count
    shards = width // dp_count
    slots = rows // dp_count
    first_len = pick(seq_lengths, 0, 2 * owner)
    scalars = jnp.stack([lane, first_len, lane % 2, lane // 2]).astype(jnp.int32)

    lane_rows = pick(dealing.reshape(dp_count, mp_count, rows), 1, lane)
    local_row = lane_rows - (owner * mp_count + lane) * rows
    inside = (local_row >= 0) & (local_row < rows)
    order = jnp.arange(rows, dtype=jnp.int32)
    upto = (order[:, None] <= order[None, :]).astype(BF16)
    rank = dot(inside.astype(BF16), upto, 1, 0).astype(jnp.int32) - 1
    slot_hit = inside[:, None, :] & (rank[:, None, :] == jnp.arange(slots)[None, :, None])
    send_row = jnp.sum(jnp.where(slot_hit, local_row[:, None, :], 0), axis=2).reshape(rows)
    to_slot = (send_row[:, None] == order[None, :]).astype(BF16)
    source = pick(lane_rows, 0, owner) // (rows * mp_count)
    from_src = source[None, :] == jnp.arange(dp_count, dtype=jnp.int32)[:, None]
    src_rank = dot(from_src.astype(BF16), upto, 1, 0).astype(jnp.int32) - 1
    slot_of = source * slots + jnp.sum(jnp.where(from_src, src_rank, 0), axis=0)
    to_dealt = (slot_of[:, None] == order[None, :]).astype(BF16)

    def exchange(values):
        packed = values.reshape(dp_count, slots, width)
        arrived = lax.all_to_all(packed, "dp", split_axis=0, concat_axis=0, tiled=True)
        return arrived.reshape(rows, width)

    def pack(values):
        return dot(to_slot, values, 1, 0).astype(BF16)

    def unpack(values):
        return dot(to_dealt, values, 1, 0).astype(BF16)

    def pack_back(values):
        return dot(to_dealt, values, 0, 0).astype(BF16)

    def unpack_back(values):
        return dot(to_slot, values, 0, 0).astype(BF16)

    def group(values):
        across = swap_bit(values, "mp", 2)
        return [values, swap_bit(values, "mp", 1), across, swap_bit(across, "mp", 1)]

    gains = gather_bits(gather_bits(jnp.stack([attn_gain, mlp_gain]), "dp"), "mp")
    gains = gains.transpose(2, 1, 0, 3).reshape(2, width)
    place = jnp.arange(tokens, dtype=jnp.int32)
    place = jnp.where(place >= first_len, place - first_len, place).astype(F32)
    freq_index = jnp.arange(LANES, dtype=jnp.int32) % (HEAD_DIM // 2)
    freqs = jnp.exp(freq_index.astype(F32) * (-2.0 * math.log(theta_base) / HEAD_DIM))
    angles = place[:, None] * freqs[None, :]
    first_half = jnp.arange(LANES) % HEAD_DIM < HEAD_DIM // 2
    cos = jnp.cos(angles)
    sin = jnp.sin(angles) * jnp.where(first_half, -1.0, 1.0)[None, :]

    w_mlp = jnp.concatenate([w_in, w_down.T[None]], axis=0)
    x_arrived = exchange(pack(hidden_in))
    gains, w_mlp = lax.optimization_barrier((gains, w_mlp))
    x_arrived, gains, cos, sin, scalars, g_packed = lax.optimization_barrier(
        (x_arrived, gains, cos, sin, scalars, pack(out_grad))
    )
    w_mlp = lax.all_gather(w_mlp, "dp", axis=1, tiled=True)
    gain_one, gain_two = gains[0:1], gains[1:2]
    x_mine = unpack(x_arrived)
    x_rel = group(x_mine)
    attn_weights = jnp.concatenate([w_qkv, w_out.T[None]], axis=0)
    attn_weights = jnp.moveaxis(gather_bits(attn_weights, "dp"), 0, 1).reshape(4, width, -1)
    w_out_across = swap_bit(attn_weights[3], "mp", 2)
    g_packed, attn_weights = lax.optimization_barrier((g_packed, attn_weights))
    g_arrived = exchange(g_packed)

    held = qkv_call(scalars, x_rel[0], x_rel[1], gain_one, attn_weights, cos, sin, 0, ())
    q, k, v, n1 = qkv_call(scalars, x_rel[2], x_rel[3], gain_one, attn_weights, cos, sin, 2, held)
    q, w_out_across = lax.optimization_barrier((q, w_out_across))
    w_out_rel = [attn_weights[3], None, w_out_across, None]
    w_out_rel[1], w_out_rel[3] = swap_bit(w_out_rel[0], "mp", 1), swap_bit(w_out_across, "mp", 1)
    near, q2, near_top = attend_forward(scalars, q, k, v, 0, 2 * rows, ())
    (g_arrived,) = after(near, g_arrived)
    g_mine = unpack(g_arrived)
    g_core, g_across = swap_bit(g_mine, "mp", 1), swap_bit(g_mine, "mp", 2)
    near_across = swap_bit(near, "mp", 2)
    distant, q2, far_top = attend_forward(scalars, q, k, v, 1, 2 * rows, (q2,))
    distant, near_across, g_across = lax.optimization_barrier((distant, near_across, g_across))
    g_rel = [g_mine, g_core, g_across, swap_bit(g_across, "mp", 1)]
    far_across = swap_bit(distant, "mp", 2)
    core = lambda values: swap_bit(values, "mp", 1)
    far_heads = [distant, core(distant), near_across, core(near_across)]
    peaks = [near_top, far_top]
    head_peaks = jnp.max(jnp.stack(peaks), axis=(0, 1, 3, 4)) * score_scale
    peak_bits = bits_of(dp_count)
    peak_swap = swap_bit(head_peaks, "dp", peak_bits[0])

    *held, keep, send, keep_out, send_out = mlp_call(
        scalars,
        (x_rel[3], x_rel[2]),
        (g_rel[3], g_rel[2]),
        far_heads,
        w_out_rel,
        gain_two,
        w_mlp,
        2,
        (),
    )
    far_across, peak_swap, send, near = lax.optimization_barrier(
        (far_across, peak_swap, send, near)
    )
    head_peaks = jnp.maximum(head_peaks, peak_swap)
    peak_swap = swap_bit(head_peaks, "dp", peak_bits[1])
    dn_far = (keep + core(send).astype(F32)).astype(BF16)
    dn_arrived = swap_bit(dn_far, "mp", 2)
    near_heads = [near, core(near), far_across, core(far_across)]
    (near_heads[0],) = after(dn_far, near)
    far_out = (keep_out, send_out)
    a_rel, n2, g_all, act, dgate, dup, keep, send, keep_out, send_out = mlp_call(
        scalars,
        (x_rel[1], x_rel[0]),
        (g_rel[1], g_rel[0]),
        near_heads,
        w_out_rel,
        gain_two,
        w_mlp,
        0,
        held,
    )
    dn_arrived, peak_swap, send = lax.optimization_barrier((dn_arrived, peak_swap, send))
    head_peaks = jnp.maximum(head_peaks, peak_swap)
    peak_swap = swap_bit(head_peaks, "dp", peak_bits[2])
    dx, da = resid_call(
        keep, core(send), dn_arrived, x_rel[0], a_rel, g_rel[0], gain_two
    )
    da_core, da_across = core(da), swap_bit(da, "mp", 2)

    flat = lambda values: values.reshape(tokens, values.shape[2])
    (act,) = after(da, act)
    inner_grads = inner_call(flat(n2), flat(g_all), flat(dgate), flat(dup), flat(act))
    held = list(head_grad_call(scalars, da, da_core, attn_weights[3], near, 0, tokens, ()))
    inner_grads, da_across, peak_swap, held[0] = lax.optimization_barrier(
        (inner_grads, da_across, peak_swap, held[0])
    )
    do, da_all = head_grad_call(
        scalars, da_across, core(da_across), attn_weights[3], distant, 1, tokens, held
    )
    head_peaks = jnp.maximum(head_peaks, peak_swap)
    for bit in peak_bits[3:]:
        head_peaks = jnp.maximum(head_peaks, swap_bit(head_peaks, "dp", bit))
    inner_grads = by_device(inner_grads, dp_count)
    inner_grads = lax.all_to_all(inner_grads, "dp", split_axis=0, concat_axis=0, tiled=True)


    far_out = after(da_across, *far_out)
    add_core = lambda keep, send: keep.astype(F32) + core(send).astype(F32)

    factor = jnp.sqrt(clip_limit / jnp.maximum(head_peaks, clip_limit))
    column_factor = jnp.repeat(factor, HEAD_DIM)
    scaling = jnp.stack([column_factor, column_factor, jnp.ones_like(column_factor)])[:, None, :]
    clipped = (w_qkv.astype(F32) * scaling).astype(BF16)

    out_far = add_core(*far_out).astype(BF16)
    out_arrived = swap_bit(out_far, "mp", 2)
    do, out_sum = after(out_far, do, add_core(keep_out, send_out))
    dproj = attend_backward(scalars, q2, k, v, do, cos, sin)
    proj_grad = proj_call(n1, dproj, (near, distant), da_all)
    proj_grad, dproj, out_arrived = lax.optimization_barrier((proj_grad, dproj, out_arrived))
    far_core = core(dn_call(scalars, dproj, attn_weights, 3, rows))
    far_keep = dn_call(scalars, dproj, attn_weights, 2, rows)
    dn_far = (far_keep.astype(F32) + far_core.astype(F32)).astype(BF16)
    dn_arrived = swap_bit(dn_far, "mp", 2)
    inner_grads, dn_far, out_arrived = lax.optimization_barrier((inner_grads, dn_far, out_arrived))
    x1 = x_rel[0].astype(F32) + a_rel[0].astype(F32)
    out_packed = pack_back((x1 + (out_sum + out_arrived.astype(F32))).astype(BF16))
    (dproj,) = after(out_packed, dproj)
    out_sent = exchange(out_packed)
    send = dn_call(scalars, dproj, attn_weights, 1, rows)
    keep = dn_call(scalars, dproj, attn_weights, 0, rows)
    dn_core = core(send)
    out_sent, dn_arrived, dn_core = lax.optimization_barrier((out_sent, dn_arrived, dn_core))
    grad_packed = pack_back(last_call(keep, dn_core, dn_arrived, x_rel[0], dx, gain_one))
    grad_arrived = exchange(grad_packed)
    (out_arrived,) = after(grad_packed, out_sent)
    output = turn_rows(to_slot, out_arrived)
    grads = lax.psum_scatter(by_device(proj_grad, dp_count), "dp")
    inner_grads, grads = after(output, inner_grads, grads)
    inner_grads = jnp.sum(inner_grads.astype(F32), axis=0)
    grad_arrived, inner_grads, grads = lax.optimization_barrier(
        (grad_arrived, inner_grads, grads)
    )
    grads = grads.astype(F32)
    input_grad = unpack_back(grad_arrived)
    inner_grad, down_grad = jnp.swapaxes(inner_grads[:2], 1, 2), inner_grads[2]
    proj_grad, outer_grad = jnp.swapaxes(grads[:3], 1, 2), grads[3]

    by_gain = jnp.stack(
        [
            jnp.sum(proj_grad * w_qkv.astype(F32), axis=(0, 2)),
            jnp.sum(inner_grad * w_in.astype(F32), axis=(0, 2)),
        ]
    )
    gain_part = lax.dynamic_slice_in_dim(gains, owner * shards, shards, 1)
    gain_grads = scatter_lanes(by_gain / gain_part)
    return (
        output,
        input_grad,
        gain_grads[0],
        gain_grads[1],
        proj_grad,
        outer_grad,
        inner_grad,
        down_grad,
        clipped,
    )


def solution(mesh):
    in_specs = (
        P(("dp", "mp"), None),
        P(("dp", "mp"), None),
        P(),
        P(),
        P(("dp", "mp")),
        P(("dp", "mp")),
        P(None, "dp", "mp"),
        P("mp", "dp"),
        P(None, "dp", "mp"),
        P("mp", "dp"),
    )
    out_specs = (
        P(("dp", "mp"), None),
        P(("dp", "mp"), None),
        P(("dp", "mp")),
        P(("dp", "mp")),
        P(None, "dp", "mp"),
        P("mp", "dp"),
        P(None, "dp", "mp"),
        P("mp", "dp"),
        P(None, "dp", "mp"),
    )
    return jax.shard_map(local, mesh=mesh, in_specs=in_specs, out_specs=out_specs, check_vma=False)
```

```python
import functools
import math

import jax
import jax.numpy as jnp
from jax import lax
from jax.experimental import pallas as pl
from jax.experimental.pallas import tpu as pltpu
from jax.sharding import PartitionSpec as P

HEAD_DIM = 64
LANES = 128
theta_base = 160000.0
norm_eps = 1e-05
clip_limit = 5.0
score_scale = 0.125
exp_scale = score_scale * math.log2(math.e)
far_away = -1e30
lowest = -3e38

BF16 = jnp.bfloat16
F32 = jnp.float32


def dot(left, right, left_dim, right_dim):
    return lax.dot_general(
        left, right, (((left_dim,), (right_dim,)), ((), ())), preferred_element_type=F32
    )


def split_three(values):
    high = values.astype(BF16).astype(F32)
    rest = values - high
    middle = rest.astype(BF16).astype(F32)
    return high, middle, rest - middle


def row_stats(values):
    mean = jnp.mean(values, axis=-1, keepdims=True)
    centered = values - mean
    variance = jnp.mean(centered * centered, axis=-1, keepdims=True)
    scale = lax.rsqrt(variance + norm_eps)
    return centered * scale, scale


def turn(values, lane):
    return jnp.where(
        lane % HEAD_DIM < HEAD_DIM // 2,
        pltpu.roll(values, LANES - HEAD_DIM // 2, 1),
        pltpu.roll(values, HEAD_DIM // 2, 1),
    )


def swap_bit(values, axis_name, bit):
    count = lax.axis_size(axis_name)
    return lax.ppermute(values, axis_name, [(i, i ^ bit) for i in range(count)])


def lane_iota(rows):
    return lax.broadcasted_iota(jnp.int32, (rows, LANES), 1)


def vmem(mib):
    return pltpu.CompilerParams(vmem_limit_bytes=mib << 20)


def takes(micros):
    flops = max(micros * 1_100_000_000, 1024)
    return pl.CostEstimate(flops=flops, bytes_accessed=flops // 1024, transcendentals=0)


def resident(shape):
    zeros = (0,) * len(shape)
    return pl.BlockSpec(shape, lambda *_: zeros, pipeline_mode=pl.Buffered(1))


def qkv_kernel(step, per, first, s_ref, xa_ref, xb_ref, gain_ref, w_ref, cos_ref, sin_ref, *rest):
    q_ref, k_ref, v_ref, n_ref = rest[-4:]
    first_len = s_ref[1]
    at = pl.program_id(0)
    x = jnp.where(at < per, xa_ref[...], xb_ref[...])
    normed, _ = row_stats(x.astype(F32))
    n1 = (normed * gain_ref[...]).astype(BF16)
    n_ref[...] = n1
    lane = lane_iota(step)
    start = (((first + at // per) ^ s_ref[0]) * per + at % per) * step
    row = start + lax.broadcasted_iota(jnp.int32, (step, LANES), 0)
    second = row >= first_len
    one, zero = jnp.float32(1), jnp.float32(0)
    q_tail = jnp.where(lane == 64 + second.astype(jnp.int32), one, zero)
    k_tail = jnp.where(
        lane == 65 - second.astype(jnp.int32),
        jnp.float32(far_away),
        jnp.where((lane >= 66) & (lane < 69), one, zero),
    )
    cos, sin = cos_ref[...], sin_ref[...]
    for which, (out, tail) in enumerate(((q_ref, q_tail), (k_ref, k_tail), (v_ref, one))):
        projected = dot(n1, w_ref[which], 1, 0)
        for pair in range(projected.shape[1] // LANES):
            part = projected[:, pair * LANES : (pair + 1) * LANES]
            if which < 2:
                part = part * cos + turn(part, lane) * sin
            out[2 * pair] = jnp.where(lane < HEAD_DIM, part, tail).astype(BF16)
            out[2 * pair + 1] = jnp.where(
                lane < HEAD_DIM, pltpu.roll(part, HEAD_DIM, 1), tail
            ).astype(BF16)


def qkv_call(scalars, xa, xb, gain, w_qkv, cos, sin, first, held, step=512):
    rows, width = xa.shape
    tokens = cos.shape[0]
    cols = w_qkv.shape[2]
    heads = cols // HEAD_DIM
    per = rows // step
    ext = jax.ShapeDtypeStruct((heads, tokens, LANES), BF16)
    place = lambda i, s: (((first + i // per) ^ s[0]) * per + i % per, 0)
    head_spec = pl.BlockSpec((heads, step, LANES), lambda i, s: (0, *place(i, s)))
    held = list(held)
    return pl.pallas_call(
        functools.partial(qkv_kernel, step, per, first),
        out_shape=(ext, ext, ext, jax.ShapeDtypeStruct((tokens, width), BF16)),
        grid_spec=pltpu.PrefetchScalarGridSpec(
            num_scalar_prefetch=1,
            grid=(2 * per,),
            in_specs=[
                pl.BlockSpec((step, width), lambda i, s: (jnp.minimum(i, per - 1), 0)),
                pl.BlockSpec((step, width), lambda i, s: (jnp.maximum(i - per, 0), 0)),
                resident(gain.shape),
                resident((3, width, cols)),
                pl.BlockSpec((step, LANES), place),
                pl.BlockSpec((step, LANES), place),
            ]
            + [pl.BlockSpec(memory_space=pl.ANY)] * len(held),
            out_specs=[head_spec] * 3 + [pl.BlockSpec((step, width), place)],
        ),
        input_output_aliases={7 + i: i for i in range(len(held))},
        compiler_params=vmem(48),
        cost_estimate=takes(3),
        name="qkv",
    )(scalars, xa, xb, gain, w_qkv, cos, sin, *held)


def key_range(first_len, row, q_rows, k_rows, tokens):
    low = jnp.where(row >= first_len, first_len // k_rows, 0)
    high = jnp.where(row + q_rows <= first_len, (first_len + k_rows - 1) // k_rows, tokens // k_rows)
    return low, high


def fwd_kernel(
    far, q_rows, k_rows, s_ref, q_ref, k_ref, v_ref, *rest
):
    o_ref, q2_ref, top_ref, score, peak, acc = rest[-6:]
    heads, tokens, _ = k_ref.shape
    low, high = key_range(
        s_ref[1],
        ((s_ref[3] ^ far) * pl.num_programs(0) + pl.program_id(0)) * q_rows,
        q_rows,
        k_rows,
        tokens,
    )
    lane = lane_iota(q_rows)
    peak[...] = jnp.full(peak.shape, lowest, F32)
    acc[...] = jnp.zeros(acc.shape, F32)

    def first_pass(block, carry):
        keys = pl.ds(pl.multiple_of(block * k_rows, k_rows), k_rows)
        for h in range(heads):
            s = dot(q_ref[h], k_ref[h, keys, :], 1, 1)
            score[h, :, keys] = s
            most = peak[h]
            for t in range(k_rows // LANES):
                most = jnp.maximum(most, s[:, t * LANES : (t + 1) * LANES])
            peak[h] = most
        return carry

    lax.fori_loop(low, high, first_pass, 0)
    for h in range(heads):
        peak[h] = jnp.broadcast_to(jnp.max(peak[h], axis=1, keepdims=True), (q_rows, LANES))

    def second_pass(block, carry):
        keys = pl.ds(pl.multiple_of(block * k_rows, k_rows), k_rows)
        for h in range(heads):
            s, most = score[h, :, keys], peak[h]
            p = jnp.concatenate(
                [
                    jnp.exp2((s[:, t * LANES : (t + 1) * LANES] - most) * exp_scale).astype(BF16)
                    for t in range(k_rows // LANES)
                ],
                axis=1,
            )
            acc[h] += dot(p, v_ref[h, keys, :], 1, 0)
        return carry

    lax.fori_loop(low, high, second_pass, 0)
    held = None
    for h in range(heads):
        sums = acc[h]
        total = jnp.where(lane < HEAD_DIM, pltpu.roll(sums, HEAD_DIM, 1), sums)
        out = sums / total
        log_total = peak[h] + jnp.log2(total) * (1.0 / exp_scale)
        a, b, c = split_three(-log_total)
        q2 = q_ref[h].astype(F32)
        q2 = jnp.where(lane == 66, a, jnp.where(lane == 67, b, jnp.where(lane == 68, c, q2)))
        q2_ref[h] = q2.astype(BF16)
        top_ref[h] = jnp.broadcast_to(jnp.max(peak[h], axis=0, keepdims=True), (8, LANES))
        if h % 2 == 0:
            held = out
        else:
            both = jnp.where(lane < HEAD_DIM, held, pltpu.roll(out, HEAD_DIM, 1))
            o_ref[:, (h // 2) * LANES : (h // 2 + 1) * LANES] = both.astype(BF16)


def attend_forward(scalars, q, k, v, far, rows, held, q_rows=256, k_rows=512):
    heads, tokens, _ = k.shape
    count = rows // q_rows
    k_rows = min(k_rows, tokens)
    return pl.pallas_call(
        functools.partial(fwd_kernel, far, q_rows, k_rows),
        out_shape=(
            jax.ShapeDtypeStruct((rows, heads * HEAD_DIM), BF16),
            jax.ShapeDtypeStruct(q.shape, BF16),
            jax.ShapeDtypeStruct((count, heads, 8, LANES), F32),
        ),
        grid_spec=pltpu.PrefetchScalarGridSpec(
            num_scalar_prefetch=1,
            grid=(count,),
            in_specs=[
                pl.BlockSpec((heads, q_rows, LANES), lambda i, s: (0, (s[3] ^ far) * count + i, 0)),
                resident(k.shape),
                resident(v.shape),
            ]
            + [pl.BlockSpec(memory_space=pl.ANY)] * len(held),
            out_specs=[
                pl.BlockSpec((q_rows, heads * HEAD_DIM), lambda i, s: (i, 0)),
                pl.BlockSpec((heads, q_rows, LANES), lambda i, s: (0, (s[3] ^ far) * count + i, 0)),
                pl.BlockSpec((None, heads, 8, LANES), lambda i, s: (i, 0, 0, 0)),
            ],
            scratch_shapes=[
                pltpu.VMEM((heads, q_rows, tokens), F32),
                pltpu.VMEM((heads, q_rows, LANES), F32),
                pltpu.VMEM((heads, q_rows, LANES), F32),
            ],
        ),
        compiler_params=vmem(48),
        cost_estimate=takes(20),
        input_output_aliases={4 + i: 1 + i for i in range(len(held))},
        name="attend_forward",
    )(scalars, q, k, v, *held)


def bwd_kernel(
    q_rows, k_rows, s_ref, q2_ref, k_ref, v_ref, do_ref, cos_ref, sin_ref, out_ref, dk_ref, dv_ref
):
    heads, tokens, _ = k_ref.shape
    step = pl.program_id(0)
    low, high = key_range(s_ref[1], step * q_rows, q_rows, k_rows, tokens)

    @pl.when(step == 0)
    def _():
        dk_ref[...] = jnp.zeros_like(dk_ref)
        dv_ref[...] = jnp.zeros_like(dv_ref)

    def body(block, sums):
        keys = pl.ds(pl.multiple_of(block * k_rows, k_rows), k_rows)
        new = []
        for h in range(heads):
            key, q2, do = k_ref[h, keys, :], q2_ref[h], do_ref[h]
            p = jnp.exp2(dot(key, q2, 1, 1) * exp_scale)
            ds = (p * dot(v_ref[h, keys, :], do, 1, 1)).astype(BF16)
            dv_ref[h, keys, :] += dot(p.astype(BF16), do, 1, 0)
            dk_ref[h, keys, :] += dot(ds, q2, 1, 0)
            new.append(sums[h] + dot(key, ds, 0, 0))
        return tuple(new)

    sums = lax.fori_loop(
        low, high, body, tuple(jnp.zeros((LANES, q_rows), F32) for _ in range(heads))
    )
    lane = lane_iota(q_rows)

    def unrotate(first, second, rows):
        both = jnp.where(lane < HEAD_DIM, first, pltpu.roll(second, HEAD_DIM, 1)) * score_scale
        return both * cos_ref[rows, :] - turn(both, lane) * sin_ref[rows, :]

    here = pl.ds(pl.multiple_of(step * q_rows, q_rows), q_rows)
    for pair in range(heads // 2):
        cols = slice(pair * LANES, (pair + 1) * LANES)
        out_ref[0, here, cols] = unrotate(sums[2 * pair].T, sums[2 * pair + 1].T, here).astype(BF16)

    @pl.when(step == pl.num_programs(0) - 1)
    def _():
        def finish(block, carry):
            rows = pl.ds(pl.multiple_of(block * q_rows, q_rows), q_rows)
            for pair in range(heads // 2):
                cols = slice(pair * LANES, (pair + 1) * LANES)
                one, two = 2 * pair, 2 * pair + 1
                out_ref[1, rows, cols] = unrotate(
                    dk_ref[one, rows, :], dk_ref[two, rows, :], rows
                ).astype(BF16)
                out_ref[2, rows, cols] = jnp.where(
                    lane < HEAD_DIM,
                    dv_ref[one, rows, :],
                    pltpu.roll(dv_ref[two, rows, :], HEAD_DIM, 1),
                ).astype(BF16)
            return carry

        lax.fori_loop(0, tokens // q_rows, finish, 0)


def attend_backward(scalars, q2, k, v, do, cos, sin, q_rows=256, k_rows=512):
    heads, tokens, _ = k.shape
    block = lambda: pl.BlockSpec((heads, q_rows, LANES), lambda i, s: (0, i, 0))
    out = (3, tokens, heads * HEAD_DIM)
    return pl.pallas_call(
        functools.partial(bwd_kernel, q_rows, k_rows),
        out_shape=jax.ShapeDtypeStruct(out, BF16),
        grid_spec=pltpu.PrefetchScalarGridSpec(
            num_scalar_prefetch=1,
            grid=(tokens // q_rows,),
            in_specs=[
                block(),
                resident(k.shape),
                resident(v.shape),
                block(),
                resident(cos.shape),
                resident(sin.shape),
            ],
            out_specs=resident(out),
            scratch_shapes=[
                pltpu.VMEM((heads, tokens, LANES), F32),
                pltpu.VMEM((heads, tokens, LANES), F32),
            ],
        ),
        compiler_params=vmem(48),
        cost_estimate=takes(20),
        name="attend_backward",
    )(scalars, q2, k, v, do, cos, sin)


def mlp_kernel(
    s_ref, xs_ref, xk_ref, gs_ref, gk_ref, o0, o1, o2, o3, w0, w1, w2, w3, gain_ref, w_ref, *rest
):
    a_ref, n_ref, g_out, act_ref, dgate_ref, dup_ref = rest[-10:-4]
    keep_ref, send_ref, keep_out, send_out = rest[-4:]
    units = w_ref.shape[2]
    sending = pl.program_id(0) < pl.num_programs(0) // 2
    x = jnp.where(sending, xs_ref[...], xk_ref[...])
    g = jnp.where(sending, gs_ref[...], gk_ref[...])
    branch = dot(o0[...], w0[...], 1, 1) + dot(o1[...], w1[...], 1, 1)
    branch = branch + dot(o2[...], w2[...], 1, 1) + dot(o3[...], w3[...], 1, 1)
    branch = branch.astype(BF16)
    a_ref[...] = branch
    normed, _ = row_stats(x.astype(F32) + branch.astype(F32))
    n2 = (normed * gain_ref[...]).astype(BF16)
    n_ref[...] = n2
    g_out[...] = g
    partial = out_partial = 0.0
    for low in range(0, units, 256):
        cols = slice(low, min(low + 256, units))
        gate = dot(n2, w_ref[0, :, cols], 1, 0)
        up = dot(n2, w_ref[1, :, cols], 1, 0)
        dact = dot(g, w_ref[2, :, cols], 1, 0)
        phi = 0.5 + 0.5 * lax.erf(gate * math.sqrt(0.5))
        gelu = gate * phi
        act = (gelu * up).astype(BF16)
        act_ref[:, cols] = act
        density = jnp.exp(-0.5 * gate * gate) * (1.0 / math.sqrt(2.0 * math.pi))
        dgate = (dact * up * (phi + gate * density)).astype(BF16)
        dup = (dact * gelu).astype(BF16)
        dgate_ref[:, cols] = dgate
        dup_ref[:, cols] = dup
        partial = partial + dot(dgate, w_ref[0, :, cols], 1, 1) + dot(dup, w_ref[1, :, cols], 1, 1)
        out_partial = out_partial + dot(act, w_ref[2, :, cols], 1, 1)

    @pl.when(sending)
    def _():
        send_ref[...] = partial.astype(BF16)
        send_out[...] = out_partial.astype(BF16)

    @pl.when(jnp.logical_not(sending))
    def _():
        keep_ref[...] = partial
        keep_out[...] = out_partial.astype(BF16)


def mlp_call(scalars, x_pair, g_pair, heads_rel, w_out_rel, gain, w_mlp, first, held, step=256):
    rows, width = x_pair[0].shape
    units = w_mlp.shape[2]
    per = rows // step
    rel = lambda i, s: (first + 1 - i // per, i % per, 0)
    wide = pl.BlockSpec((None, step, width), rel)
    narrow = pl.BlockSpec((None, step, units), rel)
    wide_out = jax.ShapeDtypeStruct((4, rows, width), BF16)
    narrow_out = jax.ShapeDtypeStruct((4, rows, units), BF16)
    send = pl.BlockSpec((step, width), lambda i, s: (jnp.minimum(i, per - 1), 0))
    keep = pl.BlockSpec((step, width), lambda i, s: (jnp.maximum(i - per, 0), 0))
    head_spec = pl.BlockSpec(
        (step, heads_rel[0].shape[1]), lambda i, s: (((i // per) ^ 1 ^ s[2]) * per + i % per, 0)
    )
    held = list(held)
    half = lambda kind: jax.ShapeDtypeStruct((rows, width), kind)
    return pl.pallas_call(
        mlp_kernel,
        out_shape=(
            wide_out,
            wide_out,
            wide_out,
            narrow_out,
            narrow_out,
            narrow_out,
            half(F32),
            half(BF16),
            half(BF16),
            half(BF16),
        ),
        grid_spec=pltpu.PrefetchScalarGridSpec(
            num_scalar_prefetch=1,
            grid=(2 * per,),
            in_specs=[send, keep, send, keep]
            + [head_spec] * len(heads_rel)
            + [resident(w.shape) for w in w_out_rel]
            + [resident(gain.shape), resident(w_mlp.shape)]
            + [pl.BlockSpec(memory_space=pl.ANY)] * len(held),
            out_specs=[wide, wide, wide, narrow, narrow, narrow, keep, send, keep, send],
        ),
        input_output_aliases={15 + i: i for i in range(len(held))},
        compiler_params=vmem(48),
        cost_estimate=takes(24),
        name="mlp",
    )(scalars, *x_pair, *g_pair, *heads_rel, *w_out_rel, gain, w_mlp, *held)


def pull_norm(normed, scale, cotangent):
    mean = jnp.mean(cotangent, axis=-1, keepdims=True)
    along = jnp.mean(cotangent * normed, axis=-1, keepdims=True)
    return (cotangent - mean - normed * along) * scale


def resid_kernel(keep_ref, core_ref, chip_ref, x_ref, a_ref, g_ref, gain_ref, dx_ref, da_ref):
    dn = keep_ref[...] + core_ref[...].astype(F32) + chip_ref[...].astype(F32)
    normed, scale = row_stats(x_ref[...].astype(F32) + a_ref[...].astype(F32))
    dx = g_ref[...].astype(F32) + pull_norm(normed, scale, dn * gain_ref[...])
    dx_ref[...] = dx
    da_ref[...] = dx.astype(BF16)


def resid_call(keep, core, chip, x, a_rel, g, gain, step=256):
    rows, width = keep.shape
    per = rows // step
    flat = pl.BlockSpec((step, width), lambda i: (i, 0))
    return pl.pallas_call(
        resid_kernel,
        out_shape=(
            jax.ShapeDtypeStruct((rows, width), F32),
            jax.ShapeDtypeStruct((rows, width), BF16),
        ),
        grid=(per,),
        in_specs=[
            flat,
            flat,
            flat,
            flat,
            pl.BlockSpec((None, step, width), lambda i: (0, i, 0)),
            flat,
            resident(gain.shape),
        ],
        out_specs=[flat, flat],
        compiler_params=vmem(48),
        cost_estimate=takes(5),
        name="resid",
    )(keep, core, chip, x, a_rel, g, gain)


def head_grad_kernel(s_ref, even_ref, odd_ref, w_ref, o_ref, *rest):
    do_ref, da_ref = rest[-2:]
    own = pl.program_id(0) == s_ref[2]
    da = jnp.where(own, even_ref[...], odd_ref[...])
    da_ref[...] = da
    do = dot(da, w_ref[...], 1, 0).astype(BF16).astype(F32)
    rows = do.shape[0]
    lane = lane_iota(rows)
    product = do * o_ref[...].astype(F32)
    for pair in range(do.shape[1] // LANES):
        cols = slice(pair * LANES, (pair + 1) * LANES)
        part = do[:, cols]
        for odd in range(2):
            inside = (lane >= HEAD_DIM) if odd else (lane < HEAD_DIM)
            delta = jnp.sum(jnp.where(inside, product[:, cols], 0.0), axis=1, keepdims=True)
            a, b, c = split_three(jnp.broadcast_to(-delta, (rows, LANES)))
            head = pltpu.roll(part, HEAD_DIM, 1) if odd else part
            tail = jnp.where(
                lane == 64, a, jnp.where(lane == 65, b, jnp.where(lane == 66, c, 0.0))
            )
            do_ref[2 * pair + odd] = jnp.where(lane < HEAD_DIM, head, tail).astype(BF16)


def head_grad_call(scalars, even, odd, w_out, o_chunk, far, tokens, held):
    rows, width = even.shape
    heads = o_chunk.shape[1] // HEAD_DIM
    held = list(held)
    return pl.pallas_call(
        head_grad_kernel,
        out_shape=(
            jax.ShapeDtypeStruct((heads, tokens, LANES), BF16),
            jax.ShapeDtypeStruct((tokens, width), BF16),
        ),
        grid_spec=pltpu.PrefetchScalarGridSpec(
            num_scalar_prefetch=1,
            grid=(2,),
            in_specs=[
                resident(even.shape),
                resident(odd.shape),
                resident(w_out.shape),
                pl.BlockSpec((rows, o_chunk.shape[1]), lambda i, s: (i, 0)),
            ]
            + [pl.BlockSpec(memory_space=pl.ANY)] * len(held),
            out_specs=[
                pl.BlockSpec((heads, rows, LANES), lambda i, s: (0, 2 * (s[3] ^ far) + i, 0)),
                pl.BlockSpec((rows, width), lambda i, s: (2 * far + i, 0)),
            ],
        ),
        input_output_aliases={5 + i: i for i in range(len(held))},
        compiler_params=vmem(48),
        cost_estimate=takes(6),
        name="head_grad",
    )(scalars, even, odd, w_out, o_chunk, *held)


def store_slices(out_ref, at, sums):
    for i in range(out_ref.shape[0]):
        out_ref[i, at] = sums[:, i * LANES : (i + 1) * LANES].astype(BF16)


def inner_kernel(n_ref, g_ref, dgate_ref, dup_ref, act_ref, out_ref, acc):
    step, last = pl.program_id(0), pl.num_programs(0) - 1
    for at, (right, left) in enumerate(((dgate_ref, n_ref), (dup_ref, n_ref), (act_ref, g_ref))):
        sums = dot(right[...], left[...], 0, 0)

        @pl.when(step == 0)
        def _(sums=sums, at=at):
            acc[at] = sums

        @pl.when((step > 0) & (step < last))
        def _(sums=sums, at=at):
            acc[at] += sums

        @pl.when(step == last)
        def _(sums=sums, at=at):
            store_slices(out_ref, at, acc[at] + sums)


def inner_call(n2, g_rel, dgate, dup, act, steps=4):
    tokens, width = n2.shape
    units = act.shape[1]
    step = tokens // steps
    out = (width // LANES, 3, units, LANES)
    wide = pl.BlockSpec((step, width), lambda i: (i, 0))
    narrow = pl.BlockSpec((step, units), lambda i: (i, 0))
    return pl.pallas_call(
        inner_kernel,
        out_shape=jax.ShapeDtypeStruct(out, BF16),
        grid=(steps,),
        in_specs=[wide, wide, narrow, narrow, narrow],
        out_specs=resident(out),
        scratch_shapes=[pltpu.VMEM((3, units, width), F32)],
        compiler_params=vmem(48),
        cost_estimate=takes(18),
        name="inner_grads",
    )(n2, g_rel, dgate, dup, act)


def proj_kernel(n_ref, d_ref, o0, o1, da_ref, out_ref, acc):
    step = pl.program_id(0)
    kinds = d_ref.shape[0]

    @pl.when(step == 0)
    def _():
        for at in range(kinds):
            acc[at] = dot(d_ref[at], n_ref[...], 0, 0)
        acc[kinds] = dot(o0[...], da_ref[...], 0, 0)

    @pl.when(step == 1)
    def _():
        for at in range(kinds):
            store_slices(out_ref, at, acc[at] + dot(d_ref[at], n_ref[...], 0, 0))
        store_slices(out_ref, kinds, acc[kinds] + dot(o1[...], da_ref[...], 0, 0))


def proj_call(n1, dproj, o_chunks, da):
    tokens, width = n1.shape
    kinds, _, cols = dproj.shape
    step = tokens // 2
    out = (width // LANES, kinds + 1, cols, LANES)
    wide = pl.BlockSpec((step, width), lambda i: (i, 0))
    return pl.pallas_call(
        proj_kernel,
        out_shape=jax.ShapeDtypeStruct(out, BF16),
        grid=(2,),
        in_specs=[
            wide,
            pl.BlockSpec((kinds, step, cols), lambda i: (0, i, 0)),
            resident(o_chunks[0].shape),
            resident(o_chunks[1].shape),
            wide,
        ],
        out_specs=resident(out),
        scratch_shapes=[pltpu.VMEM((kinds + 1, cols, width), F32)],
        compiler_params=vmem(48),
        cost_estimate=takes(10),
        name="proj_grads",
    )(n1, dproj, *o_chunks, da)


def dn_kernel(s_ref, p_ref, w_ref, out_ref):
    total = dot(p_ref[0], w_ref[0], 1, 1) + dot(p_ref[1], w_ref[1], 1, 1)
    out_ref[...] = (total + dot(p_ref[2], w_ref[2], 1, 1)).astype(BF16)


def dn_call(scalars, dproj, w_qkv, rel, rows):
    kinds, _, cols = dproj.shape
    width = w_qkv.shape[1]
    return pl.pallas_call(
        dn_kernel,
        out_shape=jax.ShapeDtypeStruct((rows, width), BF16),
        grid_spec=pltpu.PrefetchScalarGridSpec(
            num_scalar_prefetch=1,
            grid=(1,),
            in_specs=[
                pl.BlockSpec((kinds, rows, cols), lambda i, s: (0, rel ^ s[0], 0)),
                resident((kinds, width, cols)),
            ],
            out_specs=pl.BlockSpec((rows, width), lambda i, s: (0, 0)),
        ),
        compiler_params=vmem(48),
        cost_estimate=takes(0),
        name="dn",
    )(scalars, dproj, w_qkv)


def last_kernel(keep_ref, core_ref, chip_ref, x_ref, dx_ref, gain_ref, out_ref):
    dn = keep_ref[...].astype(F32) + core_ref[...].astype(F32) + chip_ref[...].astype(F32)
    dn = dn.astype(BF16).astype(F32)
    normed, scale = row_stats(x_ref[...].astype(F32))
    out_ref[...] = (dx_ref[...] + pull_norm(normed, scale, dn * gain_ref[...])).astype(BF16)


def last_call(keep, core, chip, x, dx, gain, step=256):
    rows, width = x.shape
    per = rows // step
    flat = pl.BlockSpec((step, width), lambda i: (i, 0))
    return pl.pallas_call(
        last_kernel,
        out_shape=jax.ShapeDtypeStruct((rows, width), BF16),
        grid=(per,),
        in_specs=[flat] * 5 + [resident(gain.shape)],
        out_specs=flat,
        compiler_params=vmem(48),
        cost_estimate=takes(0),
        name="last",
    )(keep, core, chip, x, dx, gain)


def turn_rows_kernel(hot_ref, rows_ref, out_ref):
    out_ref[...] = dot(hot_ref[...], rows_ref[...], 0, 0).astype(BF16)


def turn_rows(one_hot, values):
    return pl.pallas_call(
        turn_rows_kernel,
        out_shape=jax.ShapeDtypeStruct(values.shape, BF16),
        compiler_params=vmem(48),
        cost_estimate=takes(0),
        name="turn_rows",
    )(one_hot, values)


def bits_of(count):
    return [1 << i for i in range(count.bit_length() - 1)]


def pick(values, axis, index):
    return lax.dynamic_index_in_dim(values, index, axis, keepdims=False)


def by_device(values, count):
    blocks = values.shape[0]
    if blocks == count:
        return values
    axis = values.shape.index(LANES, 2)
    shape = values.shape[:axis] + (count // blocks, LANES * blocks // count) + values.shape[axis + 1 :]
    values = jnp.moveaxis(values.reshape(shape), axis, 1)
    return values.reshape((count,) + values.shape[2:])


def after(point, *values):
    return lax.optimization_barrier((point, *values))[1:]


def gather_bits(values, axis_name):
    me = lax.axis_index(axis_name)
    count = lax.axis_size(axis_name)
    shape = values.shape
    for bit in reversed(bits_of(count)):
        other = swap_bit(values, axis_name, bit)
        high = (me // bit) % 2 == 1
        values = jnp.stack([jnp.where(high, other, values), jnp.where(high, values, other)])
    lead = values.ndim - len(shape)
    order = tuple(reversed(range(lead))) + tuple(range(lead, values.ndim))
    return values.transpose(order).reshape((count,) + shape)


def scatter_lanes(values):
    me = lax.axis_index("mp")
    count = lax.axis_size("mp")
    slices = values.reshape(values.shape[0], count, values.shape[1] // count)
    total = pick(slices, 1, me)
    for bits in range(1, count):
        total = total + swap_bit(pick(slices, 1, me ^ bits), "mp", bits)
    return total


def local(
    hidden_in, out_grad, seq_lengths, dealing, attn_gain, mlp_gain, w_qkv, w_out, w_in, w_down
):
    dp_count = lax.axis_size("dp")
    mp_count = lax.axis_size("mp")
    owner = lax.axis_index("dp")
    lane = lax.axis_index("mp")
    rows, width = hidden_in.shape
    tokens = rows * mp_count
    shards = width // dp_count
    slots = rows // dp_count
    first_len = pick(seq_lengths, 0, 2 * owner)
    scalars = jnp.stack([lane, first_len, lane % 2, lane // 2]).astype(jnp.int32)

    lane_rows = pick(dealing.reshape(dp_count, mp_count, rows), 1, lane)
    local_row = lane_rows - (owner * mp_count + lane) * rows
    inside = (local_row >= 0) & (local_row < rows)
    order = jnp.arange(rows, dtype=jnp.int32)
    upto = (order[:, None] <= order[None, :]).astype(BF16)
    rank = dot(inside.astype(BF16), upto, 1, 0).astype(jnp.int32) - 1
    slot_hit = inside[:, None, :] & (rank[:, None, :] == jnp.arange(slots)[None, :, None])
    send_row = jnp.sum(jnp.where(slot_hit, local_row[:, None, :], 0), axis=2).reshape(rows)
    to_slot = (send_row[:, None] == order[None, :]).astype(BF16)
    source = pick(lane_rows, 0, owner) // (rows * mp_count)
    from_src = source[None, :] == jnp.arange(dp_count, dtype=jnp.int32)[:, None]
    src_rank = dot(from_src.astype(BF16), upto, 1, 0).astype(jnp.int32) - 1
    slot_of = source * slots + jnp.sum(jnp.where(from_src, src_rank, 0), axis=0)
    to_dealt = (slot_of[:, None] == order[None, :]).astype(BF16)

    def exchange(values):
        packed = values.reshape(dp_count, slots, width)
        arrived = lax.all_to_all(packed, "dp", split_axis=0, concat_axis=0, tiled=True)
        return arrived.reshape(rows, width)

    def pack(values):
        return dot(to_slot, values, 1, 0).astype(BF16)

    def unpack(values):
        return dot(to_dealt, values, 1, 0).astype(BF16)

    def pack_back(values):
        return dot(to_dealt, values, 0, 0).astype(BF16)

    def unpack_back(values):
        return dot(to_slot, values, 0, 0).astype(BF16)

    def group(values):
        across = swap_bit(values, "mp", 2)
        return [values, swap_bit(values, "mp", 1), across, swap_bit(across, "mp", 1)]

    gains = gather_bits(gather_bits(jnp.stack([attn_gain, mlp_gain]), "dp"), "mp")
    gains = gains.transpose(2, 1, 0, 3).reshape(2, width)
    place = jnp.arange(tokens, dtype=jnp.int32)
    place = jnp.where(place >= first_len, place - first_len, place).astype(F32)
    freq_index = jnp.arange(LANES, dtype=jnp.int32) % (HEAD_DIM // 2)
    freqs = jnp.exp(freq_index.astype(F32) * (-2.0 * math.log(theta_base) / HEAD_DIM))
    angles = place[:, None] * freqs[None, :]
    first_half = jnp.arange(LANES) % HEAD_DIM < HEAD_DIM // 2
    cos = jnp.cos(angles)
    sin = jnp.sin(angles) * jnp.where(first_half, -1.0, 1.0)[None, :]

    w_mlp = jnp.concatenate([w_in, w_down.T[None]], axis=0)
    x_arrived = exchange(pack(hidden_in))
    x_arrived, gains, cos, sin, scalars, g_packed = lax.optimization_barrier(
        (x_arrived, gains, cos, sin, scalars, pack(out_grad))
    )
    w_mlp = lax.all_gather(w_mlp, "dp", axis=1, tiled=True)
    gain_one, gain_two = gains[0:1], gains[1:2]
    x_mine = unpack(x_arrived)
    x_rel = group(x_mine)
    attn_weights = jnp.concatenate([w_qkv, w_out.T[None]], axis=0)
    attn_weights = jnp.moveaxis(gather_bits(attn_weights, "dp"), 0, 1).reshape(4, width, -1)
    w_out_across = swap_bit(attn_weights[3], "mp", 2)
    g_packed, attn_weights = lax.optimization_barrier((g_packed, attn_weights))
    g_arrived = exchange(g_packed)

    held = qkv_call(scalars, x_rel[0], x_rel[1], gain_one, attn_weights, cos, sin, 0, ())
    q, k, v, n1 = qkv_call(scalars, x_rel[2], x_rel[3], gain_one, attn_weights, cos, sin, 2, held)
    q, w_out_across = lax.optimization_barrier((q, w_out_across))
    w_out_rel = [attn_weights[3], None, w_out_across, None]
    w_out_rel[1], w_out_rel[3] = swap_bit(w_out_rel[0], "mp", 1), swap_bit(w_out_across, "mp", 1)
    near, q2, near_top = attend_forward(scalars, q, k, v, 0, 2 * rows, ())
    (g_arrived,) = after(near, g_arrived)
    g_mine = unpack(g_arrived)
    g_core, g_across = swap_bit(g_mine, "mp", 1), swap_bit(g_mine, "mp", 2)
    near_across = swap_bit(near, "mp", 2)
    distant, q2, far_top = attend_forward(scalars, q, k, v, 1, 2 * rows, (q2,))
    distant, near_across, g_across = lax.optimization_barrier((distant, near_across, g_across))
    g_rel = [g_mine, g_core, g_across, swap_bit(g_across, "mp", 1)]
    far_across = swap_bit(distant, "mp", 2)
    core = lambda values: swap_bit(values, "mp", 1)
    far_heads = [distant, core(distant), near_across, core(near_across)]
    peaks = [near_top, far_top]
    head_peaks = jnp.max(jnp.stack(peaks), axis=(0, 1, 3, 4)) * score_scale
    peak_bits = bits_of(dp_count)
    peak_swap = swap_bit(head_peaks, "dp", peak_bits[0])

    *held, keep, send, keep_out, send_out = mlp_call(
        scalars,
        (x_rel[3], x_rel[2]),
        (g_rel[3], g_rel[2]),
        far_heads,
        w_out_rel,
        gain_two,
        w_mlp,
        2,
        (),
    )
    far_across, peak_swap, send, near = lax.optimization_barrier(
        (far_across, peak_swap, send, near)
    )
    head_peaks = jnp.maximum(head_peaks, peak_swap)
    peak_swap = swap_bit(head_peaks, "dp", peak_bits[1])
    dn_far = (keep + core(send).astype(F32)).astype(BF16)
    dn_arrived = swap_bit(dn_far, "mp", 2)
    near_heads = [near, core(near), far_across, core(far_across)]
    (near_heads[0],) = after(dn_far, near)
    far_out = (keep_out, send_out)
    a_rel, n2, g_all, act, dgate, dup, keep, send, keep_out, send_out = mlp_call(
        scalars,
        (x_rel[1], x_rel[0]),
        (g_rel[1], g_rel[0]),
        near_heads,
        w_out_rel,
        gain_two,
        w_mlp,
        0,
        held,
    )
    dn_arrived, peak_swap, send = lax.optimization_barrier((dn_arrived, peak_swap, send))
    head_peaks = jnp.maximum(head_peaks, peak_swap)
    peak_swap = swap_bit(head_peaks, "dp", peak_bits[2])
    dx, da = resid_call(
        keep, core(send), dn_arrived, x_rel[0], a_rel, g_rel[0], gain_two
    )
    da_core, da_across = core(da), swap_bit(da, "mp", 2)

    flat = lambda values: values.reshape(tokens, values.shape[2])
    (act,) = after(da, act)
    inner_grads = inner_call(flat(n2), flat(g_all), flat(dgate), flat(dup), flat(act))
    held = list(head_grad_call(scalars, da, da_core, attn_weights[3], near, 0, tokens, ()))
    _, da_across, held[0] = lax.optimization_barrier((inner_grads, da_across, held[0]))
    do, da_all = head_grad_call(
        scalars, da_across, core(da_across), attn_weights[3], distant, 1, tokens, held
    )
    head_peaks = jnp.maximum(head_peaks, peak_swap)
    for bit in peak_bits[3:]:
        head_peaks = jnp.maximum(head_peaks, swap_bit(head_peaks, "dp", bit))
    inner_grads, peak_swap = lax.optimization_barrier((inner_grads, peak_swap))
    inner_grads = by_device(inner_grads, dp_count)
    inner_grads = lax.all_to_all(inner_grads, "dp", split_axis=0, concat_axis=0, tiled=True)


    far_out = after(da_across, *far_out)
    add_core = lambda keep, send: keep.astype(F32) + core(send).astype(F32)

    out_far = add_core(*far_out).astype(BF16)
    out_arrived = swap_bit(out_far, "mp", 2)
    do, out_sum = after(out_far, do, add_core(keep_out, send_out))
    dproj = attend_backward(scalars, q2, k, v, do, cos, sin)
    head_peaks = jnp.maximum(head_peaks, peak_swap)
    for bit in peak_bits[3:]:
        head_peaks = jnp.maximum(head_peaks, swap_bit(head_peaks, "dp", bit))
    factor = jnp.sqrt(clip_limit / jnp.maximum(head_peaks, clip_limit))
    column_factor = jnp.repeat(factor, HEAD_DIM)
    scaling = jnp.stack([column_factor, column_factor, jnp.ones_like(column_factor)])[:, None, :]
    clipped = (w_qkv.astype(F32) * scaling).astype(BF16)

    proj_grad = proj_call(n1, dproj, (near, distant), da_all)
    proj_grad, dproj, out_arrived = lax.optimization_barrier((proj_grad, dproj, out_arrived))
    far_core = core(dn_call(scalars, dproj, attn_weights, 3, rows))
    far_keep = dn_call(scalars, dproj, attn_weights, 2, rows)
    dn_far = (far_keep.astype(F32) + far_core.astype(F32)).astype(BF16)
    dn_arrived = swap_bit(dn_far, "mp", 2)
    inner_grads, dn_far, out_arrived = lax.optimization_barrier((inner_grads, dn_far, out_arrived))
    x1 = x_rel[0].astype(F32) + a_rel[0].astype(F32)
    out_packed = pack_back((x1 + (out_sum + out_arrived.astype(F32))).astype(BF16))
    (dproj,) = after(out_packed, dproj)
    out_sent = exchange(out_packed)
    send = dn_call(scalars, dproj, attn_weights, 1, rows)
    keep = dn_call(scalars, dproj, attn_weights, 0, rows)
    dn_core = core(send)
    inner_grads = jnp.sum(inner_grads.astype(F32), axis=0)
    inner_grad, down_grad = jnp.swapaxes(inner_grads[:2], 1, 2), inner_grads[2]
    inner_by_gain = jnp.sum(inner_grad * w_in.astype(F32), axis=(0, 2))
    gain_part = lax.dynamic_slice_in_dim(gains, owner * shards, shards, 1)
    inner_grad, down_grad, inner_by_gain, gain_part, clipped, keep = lax.optimization_barrier(
        (inner_grad, down_grad, inner_by_gain, gain_part, clipped, keep)
    )
    out_sent, dn_arrived, dn_core = lax.optimization_barrier((out_sent, dn_arrived, dn_core))
    grad_packed = pack_back(last_call(keep, dn_core, dn_arrived, x_rel[0], dx, gain_one))
    grad_arrived = exchange(grad_packed)
    (out_arrived,) = after(grad_packed, out_sent)
    output = turn_rows(to_slot, out_arrived)
    grads = lax.psum_scatter(by_device(proj_grad, dp_count), "dp")
    (grads,) = after(output, grads)
    grad_arrived, grads = lax.optimization_barrier((grad_arrived, grads))
    grads = grads.astype(F32)
    input_grad = unpack_back(grad_arrived)
    proj_grad, outer_grad = jnp.swapaxes(grads[:3], 1, 2), grads[3]

    by_gain = jnp.stack([jnp.sum(proj_grad * w_qkv.astype(F32), axis=(0, 2)), inner_by_gain])
    gain_grads = scatter_lanes(by_gain / gain_part)
    return (
        output,
        input_grad,
        gain_grads[0],
        gain_grads[1],
        proj_grad,
        outer_grad,
        inner_grad,
        down_grad,
        clipped,
    )


def solution(mesh):
    in_specs = (
        P(("dp", "mp"), None),
        P(("dp", "mp"), None),
        P(),
        P(),
        P(("dp", "mp")),
        P(("dp", "mp")),
        P(None, "dp", "mp"),
        P("mp", "dp"),
        P(None, "dp", "mp"),
        P("mp", "dp"),
    )
    out_specs = (
        P(("dp", "mp"), None),
        P(("dp", "mp"), None),
        P(("dp", "mp")),
        P(("dp", "mp")),
        P(None, "dp", "mp"),
        P("mp", "dp"),
        P(None, "dp", "mp"),
        P("mp", "dp"),
        P(None, "dp", "mp"),
    )
    return jax.shard_map(local, mesh=mesh, in_specs=in_specs, out_specs=out_specs, check_vma=False)
```

```python
import functools
import math

import jax
import jax.numpy as jnp
from jax import lax
from jax.experimental import pallas as pl
from jax.experimental.pallas import tpu as pltpu
from jax.sharding import PartitionSpec as P

HEAD_DIM = 64
LANES = 128
theta_base = 160000.0
norm_eps = 1e-05
clip_limit = 5.0
score_scale = 0.125
exp_scale = score_scale * math.log2(math.e)
far_away = -1e30
lowest = -3e38

BF16 = jnp.bfloat16
F32 = jnp.float32


def dot(left, right, left_dim, right_dim):
    return lax.dot_general(
        left, right, (((left_dim,), (right_dim,)), ((), ())), preferred_element_type=F32
    )


def split_three(values):
    high = values.astype(BF16).astype(F32)
    rest = values - high
    middle = rest.astype(BF16).astype(F32)
    return high, middle, rest - middle


def row_stats(values):
    mean = jnp.mean(values, axis=-1, keepdims=True)
    centered = values - mean
    variance = jnp.mean(centered * centered, axis=-1, keepdims=True)
    scale = lax.rsqrt(variance + norm_eps)
    return centered * scale, scale


def turn(values, lane):
    return jnp.where(
        lane % HEAD_DIM < HEAD_DIM // 2,
        pltpu.roll(values, LANES - HEAD_DIM // 2, 1),
        pltpu.roll(values, HEAD_DIM // 2, 1),
    )


def swap_bit(values, axis_name, bit):
    count = lax.axis_size(axis_name)
    return lax.ppermute(values, axis_name, [(i, i ^ bit) for i in range(count)])


def lane_iota(rows):
    return lax.broadcasted_iota(jnp.int32, (rows, LANES), 1)


def vmem(mib):
    return pltpu.CompilerParams(vmem_limit_bytes=mib << 20)


def takes(micros):
    flops = max(micros * 1_100_000_000, 1024)
    return pl.CostEstimate(flops=flops, bytes_accessed=flops // 1024, transcendentals=0)


def resident(shape):
    zeros = (0,) * len(shape)
    return pl.BlockSpec(shape, lambda *_: zeros, pipeline_mode=pl.Buffered(1))


def qkv_kernel(step, per, first, s_ref, xa_ref, xb_ref, gain_ref, w_ref, cos_ref, sin_ref, *rest):
    q_ref, k_ref, v_ref, n_ref = rest[-4:]
    first_len = s_ref[1]
    at = pl.program_id(0)
    x = jnp.where(at < per, xa_ref[...], xb_ref[...])
    normed, _ = row_stats(x.astype(F32))
    n1 = (normed * gain_ref[...]).astype(BF16)
    n_ref[...] = n1
    lane = lane_iota(step)
    start = (((first + at // per) ^ s_ref[0]) * per + at % per) * step
    row = start + lax.broadcasted_iota(jnp.int32, (step, LANES), 0)
    second = row >= first_len
    one, zero = jnp.float32(1), jnp.float32(0)
    q_tail = jnp.where(lane == 64 + second.astype(jnp.int32), one, zero)
    k_tail = jnp.where(
        lane == 65 - second.astype(jnp.int32),
        jnp.float32(far_away),
        jnp.where((lane >= 66) & (lane < 69), one, zero),
    )
    cos, sin = cos_ref[...], sin_ref[...]
    for which, (out, tail) in enumerate(((q_ref, q_tail), (k_ref, k_tail), (v_ref, one))):
        projected = dot(n1, w_ref[which], 1, 0)
        for pair in range(projected.shape[1] // LANES):
            part = projected[:, pair * LANES : (pair + 1) * LANES]
            if which < 2:
                part = part * cos + turn(part, lane) * sin
            out[2 * pair] = jnp.where(lane < HEAD_DIM, part, tail).astype(BF16)
            out[2 * pair + 1] = jnp.where(
                lane < HEAD_DIM, pltpu.roll(part, HEAD_DIM, 1), tail
            ).astype(BF16)


def qkv_call(scalars, xa, xb, gain, w_qkv, cos, sin, first, held, step=512):
    rows, width = xa.shape
    tokens = cos.shape[0]
    cols = w_qkv.shape[2]
    heads = cols // HEAD_DIM
    per = rows // step
    ext = jax.ShapeDtypeStruct((heads, tokens, LANES), BF16)
    place = lambda i, s: (((first + i // per) ^ s[0]) * per + i % per, 0)
    head_spec = pl.BlockSpec((heads, step, LANES), lambda i, s: (0, *place(i, s)))
    held = list(held)
    return pl.pallas_call(
        functools.partial(qkv_kernel, step, per, first),
        out_shape=(ext, ext, ext, jax.ShapeDtypeStruct((tokens, width), BF16)),
        grid_spec=pltpu.PrefetchScalarGridSpec(
            num_scalar_prefetch=1,
            grid=(2 * per,),
            in_specs=[
                pl.BlockSpec((step, width), lambda i, s: (jnp.minimum(i, per - 1), 0)),
                pl.BlockSpec((step, width), lambda i, s: (jnp.maximum(i - per, 0), 0)),
                resident(gain.shape),
                resident((3, width, cols)),
                pl.BlockSpec((step, LANES), place),
                pl.BlockSpec((step, LANES), place),
            ]
            + [pl.BlockSpec(memory_space=pl.ANY)] * len(held),
            out_specs=[head_spec] * 3 + [pl.BlockSpec((step, width), place)],
        ),
        input_output_aliases={7 + i: i for i in range(len(held))},
        compiler_params=vmem(52),
        cost_estimate=takes(3),
        name="qkv",
    )(scalars, xa, xb, gain, w_qkv, cos, sin, *held)


def key_range(first_len, row, q_rows, k_rows, tokens):
    low = jnp.where(row >= first_len, first_len // k_rows, 0)
    high = jnp.where(row + q_rows <= first_len, (first_len + k_rows - 1) // k_rows, tokens // k_rows)
    return low, high


def fwd_kernel(
    far, q_rows, k_rows, s_ref, q_ref, k_ref, v_ref, *rest
):
    o_ref, q2_ref, top_ref, score, peak, acc = rest[-6:]
    heads, tokens, _ = k_ref.shape
    low, high = key_range(
        s_ref[1],
        ((s_ref[3] ^ far) * pl.num_programs(0) + pl.program_id(0)) * q_rows,
        q_rows,
        k_rows,
        tokens,
    )
    lane = lane_iota(q_rows)
    peak[...] = jnp.full(peak.shape, lowest, F32)
    acc[...] = jnp.zeros(acc.shape, F32)

    def first_pass(block, carry):
        keys = pl.ds(pl.multiple_of(block * k_rows, k_rows), k_rows)
        for h in range(heads):
            s = dot(q_ref[h], k_ref[h, keys, :], 1, 1)
            score[h, :, keys] = s
            most = peak[h]
            for t in range(k_rows // LANES):
                most = jnp.maximum(most, s[:, t * LANES : (t + 1) * LANES])
            peak[h] = most
        return carry

    lax.fori_loop(low, high, first_pass, 0)
    for h in range(heads):
        peak[h] = jnp.broadcast_to(jnp.max(peak[h], axis=1, keepdims=True), (q_rows, LANES))

    def second_pass(block, carry):
        keys = pl.ds(pl.multiple_of(block * k_rows, k_rows), k_rows)
        for h in range(heads):
            s, most = score[h, :, keys], peak[h]
            p = jnp.concatenate(
                [
                    jnp.exp2((s[:, t * LANES : (t + 1) * LANES] - most) * exp_scale).astype(BF16)
                    for t in range(k_rows // LANES)
                ],
                axis=1,
            )
            acc[h] += dot(p, v_ref[h, keys, :], 1, 0)
        return carry

    lax.fori_loop(low, high, second_pass, 0)
    held = None
    for h in range(heads):
        sums = acc[h]
        total = jnp.where(lane < HEAD_DIM, pltpu.roll(sums, HEAD_DIM, 1), sums)
        out = sums / total
        log_total = peak[h] + jnp.log2(total) * (1.0 / exp_scale)
        a, b, c = split_three(-log_total)
        q2 = q_ref[h].astype(F32)
        q2 = jnp.where(lane == 66, a, jnp.where(lane == 67, b, jnp.where(lane == 68, c, q2)))
        q2_ref[h] = q2.astype(BF16)
        top_ref[h] = jnp.broadcast_to(jnp.max(peak[h], axis=0, keepdims=True), (8, LANES))
        if h % 2 == 0:
            held = out
        else:
            both = jnp.where(lane < HEAD_DIM, held, pltpu.roll(out, HEAD_DIM, 1))
            o_ref[:, (h // 2) * LANES : (h // 2 + 1) * LANES] = both.astype(BF16)


def attend_forward(scalars, q, k, v, far, rows, held, q_rows=256, k_rows=512):
    heads, tokens, _ = k.shape
    count = rows // q_rows
    k_rows = min(k_rows, tokens)
    return pl.pallas_call(
        functools.partial(fwd_kernel, far, q_rows, k_rows),
        out_shape=(
            jax.ShapeDtypeStruct((rows, heads * HEAD_DIM), BF16),
            jax.ShapeDtypeStruct(q.shape, BF16),
            jax.ShapeDtypeStruct((count, heads, 8, LANES), F32),
        ),
        grid_spec=pltpu.PrefetchScalarGridSpec(
            num_scalar_prefetch=1,
            grid=(count,),
            in_specs=[
                pl.BlockSpec((heads, q_rows, LANES), lambda i, s: (0, (s[3] ^ far) * count + i, 0)),
                resident(k.shape),
                resident(v.shape),
            ]
            + [pl.BlockSpec(memory_space=pl.ANY)] * len(held),
            out_specs=[
                pl.BlockSpec((q_rows, heads * HEAD_DIM), lambda i, s: (i, 0)),
                pl.BlockSpec((heads, q_rows, LANES), lambda i, s: (0, (s[3] ^ far) * count + i, 0)),
                pl.BlockSpec((None, heads, 8, LANES), lambda i, s: (i, 0, 0, 0)),
            ],
            scratch_shapes=[
                pltpu.VMEM((heads, q_rows, tokens), F32),
                pltpu.VMEM((heads, q_rows, LANES), F32),
                pltpu.VMEM((heads, q_rows, LANES), F32),
            ],
        ),
        compiler_params=vmem(52),
        cost_estimate=takes(20),
        input_output_aliases={4 + i: 1 + i for i in range(len(held))},
        name="attend_forward",
    )(scalars, q, k, v, *held)


def bwd_kernel(
    q_rows, k_rows, s_ref, q2_ref, k_ref, v_ref, do_ref, cos_ref, sin_ref, out_ref, dk_ref, dv_ref
):
    heads, tokens, _ = k_ref.shape
    step = pl.program_id(0)
    low, high = key_range(s_ref[1], step * q_rows, q_rows, k_rows, tokens)

    @pl.when(step == 0)
    def _():
        dk_ref[...] = jnp.zeros_like(dk_ref)
        dv_ref[...] = jnp.zeros_like(dv_ref)

    def body(block, sums):
        keys = pl.ds(pl.multiple_of(block * k_rows, k_rows), k_rows)
        new = []
        for h in range(heads):
            key, q2, do = k_ref[h, keys, :], q2_ref[h], do_ref[h]
            p = jnp.exp2(dot(key, q2, 1, 1) * exp_scale)
            ds = (p * dot(v_ref[h, keys, :], do, 1, 1)).astype(BF16)
            dv_ref[h, keys, :] += dot(p.astype(BF16), do, 1, 0)
            dk_ref[h, keys, :] += dot(ds, q2, 1, 0)
            new.append(sums[h] + dot(key, ds, 0, 0))
        return tuple(new)

    sums = lax.fori_loop(
        low, high, body, tuple(jnp.zeros((LANES, q_rows), F32) for _ in range(heads))
    )
    lane = lane_iota(q_rows)

    def unrotate(first, second, rows):
        both = jnp.where(lane < HEAD_DIM, first, pltpu.roll(second, HEAD_DIM, 1)) * score_scale
        return both * cos_ref[rows, :] - turn(both, lane) * sin_ref[rows, :]

    here = pl.ds(pl.multiple_of(step * q_rows, q_rows), q_rows)
    for pair in range(heads // 2):
        cols = slice(pair * LANES, (pair + 1) * LANES)
        out_ref[0, here, cols] = unrotate(sums[2 * pair].T, sums[2 * pair + 1].T, here).astype(BF16)

    @pl.when(step == pl.num_programs(0) - 1)
    def _():
        def finish(block, carry):
            rows = pl.ds(pl.multiple_of(block * q_rows, q_rows), q_rows)
            for pair in range(heads // 2):
                cols = slice(pair * LANES, (pair + 1) * LANES)
                one, two = 2 * pair, 2 * pair + 1
                out_ref[1, rows, cols] = unrotate(
                    dk_ref[one, rows, :], dk_ref[two, rows, :], rows
                ).astype(BF16)
                out_ref[2, rows, cols] = jnp.where(
                    lane < HEAD_DIM,
                    dv_ref[one, rows, :],
                    pltpu.roll(dv_ref[two, rows, :], HEAD_DIM, 1),
                ).astype(BF16)
            return carry

        lax.fori_loop(0, tokens // q_rows, finish, 0)


def attend_backward(scalars, q2, k, v, do, cos, sin, q_rows=256, k_rows=512):
    heads, tokens, _ = k.shape
    block = lambda: pl.BlockSpec((heads, q_rows, LANES), lambda i, s: (0, i, 0))
    out = (3, tokens, heads * HEAD_DIM)
    return pl.pallas_call(
        functools.partial(bwd_kernel, q_rows, k_rows),
        out_shape=jax.ShapeDtypeStruct(out, BF16),
        grid_spec=pltpu.PrefetchScalarGridSpec(
            num_scalar_prefetch=1,
            grid=(tokens // q_rows,),
            in_specs=[
                block(),
                resident(k.shape),
                resident(v.shape),
                block(),
                resident(cos.shape),
                resident(sin.shape),
            ],
            out_specs=resident(out),
            scratch_shapes=[
                pltpu.VMEM((heads, tokens, LANES), F32),
                pltpu.VMEM((heads, tokens, LANES), F32),
            ],
        ),
        compiler_params=vmem(52),
        cost_estimate=takes(20),
        name="attend_backward",
    )(scalars, q2, k, v, do, cos, sin)


def mlp_kernel(
    s_ref, xs_ref, xk_ref, gs_ref, gk_ref, o0, o1, o2, o3, w0, w1, w2, w3, gain_ref, w_ref, *rest
):
    a_ref, n_ref, g_out, act_ref, dgate_ref, dup_ref = rest[-10:-4]
    keep_ref, send_ref, keep_out, send_out = rest[-4:]
    units = w_ref.shape[2]
    sending = pl.program_id(0) < pl.num_programs(0) // 2
    x = jnp.where(sending, xs_ref[...], xk_ref[...])
    g = jnp.where(sending, gs_ref[...], gk_ref[...])
    branch = dot(o0[...], w0[...], 1, 1) + dot(o1[...], w1[...], 1, 1)
    branch = branch + dot(o2[...], w2[...], 1, 1) + dot(o3[...], w3[...], 1, 1)
    branch = branch.astype(BF16)
    a_ref[...] = branch
    normed, _ = row_stats(x.astype(F32) + branch.astype(F32))
    n2 = (normed * gain_ref[...]).astype(BF16)
    n_ref[...] = n2
    g_out[...] = g
    partial = out_partial = 0.0
    for low in range(0, units, 256):
        cols = slice(low, min(low + 256, units))
        gate = dot(n2, w_ref[0, :, cols], 1, 0)
        up = dot(n2, w_ref[1, :, cols], 1, 0)
        dact = dot(g, w_ref[2, :, cols], 1, 0)
        phi = 0.5 + 0.5 * lax.erf(gate * math.sqrt(0.5))
        gelu = gate * phi
        act = (gelu * up).astype(BF16)
        act_ref[:, cols] = act
        density = jnp.exp(-0.5 * gate * gate) * (1.0 / math.sqrt(2.0 * math.pi))
        dgate = (dact * up * (phi + gate * density)).astype(BF16)
        dup = (dact * gelu).astype(BF16)
        dgate_ref[:, cols] = dgate
        dup_ref[:, cols] = dup
        partial = partial + dot(dgate, w_ref[0, :, cols], 1, 1) + dot(dup, w_ref[1, :, cols], 1, 1)
        out_partial = out_partial + dot(act, w_ref[2, :, cols], 1, 1)

    @pl.when(sending)
    def _():
        send_ref[...] = partial.astype(BF16)
        send_out[...] = out_partial.astype(BF16)

    @pl.when(jnp.logical_not(sending))
    def _():
        keep_ref[...] = partial
        keep_out[...] = out_partial.astype(BF16)


def mlp_call(scalars, x_pair, g_pair, heads_rel, w_out_rel, gain, w_mlp, first, held, step=256):
    rows, width = x_pair[0].shape
    units = w_mlp.shape[2]
    per = rows // step
    rel = lambda i, s: (first + 1 - i // per, i % per, 0)
    wide = pl.BlockSpec((None, step, width), rel)
    narrow = pl.BlockSpec((None, step, units), rel)
    wide_out = jax.ShapeDtypeStruct((4, rows, width), BF16)
    narrow_out = jax.ShapeDtypeStruct((4, rows, units), BF16)
    send = pl.BlockSpec((step, width), lambda i, s: (jnp.minimum(i, per - 1), 0))
    keep = pl.BlockSpec((step, width), lambda i, s: (jnp.maximum(i - per, 0), 0))
    head_spec = pl.BlockSpec(
        (step, heads_rel[0].shape[1]), lambda i, s: (((i // per) ^ 1 ^ s[2]) * per + i % per, 0)
    )
    held = list(held)
    half = lambda kind: jax.ShapeDtypeStruct((rows, width), kind)
    return pl.pallas_call(
        mlp_kernel,
        out_shape=(
            wide_out,
            wide_out,
            wide_out,
            narrow_out,
            narrow_out,
            narrow_out,
            half(F32),
            half(BF16),
            half(BF16),
            half(BF16),
        ),
        grid_spec=pltpu.PrefetchScalarGridSpec(
            num_scalar_prefetch=1,
            grid=(2 * per,),
            in_specs=[send, keep, send, keep]
            + [head_spec] * len(heads_rel)
            + [resident(w.shape) for w in w_out_rel]
            + [resident(gain.shape), resident(w_mlp.shape)]
            + [pl.BlockSpec(memory_space=pl.ANY)] * len(held),
            out_specs=[wide, wide, wide, narrow, narrow, narrow, keep, send, keep, send],
        ),
        input_output_aliases={15 + i: i for i in range(len(held))},
        compiler_params=vmem(52),
        cost_estimate=takes(24),
        name="mlp",
    )(scalars, *x_pair, *g_pair, *heads_rel, *w_out_rel, gain, w_mlp, *held)


def pull_norm(normed, scale, cotangent):
    mean = jnp.mean(cotangent, axis=-1, keepdims=True)
    along = jnp.mean(cotangent * normed, axis=-1, keepdims=True)
    return (cotangent - mean - normed * along) * scale


def resid_kernel(keep_ref, core_ref, chip_ref, x_ref, a_ref, g_ref, gain_ref, dx_ref, da_ref):
    dn = keep_ref[...] + core_ref[...].astype(F32) + chip_ref[...].astype(F32)
    normed, scale = row_stats(x_ref[...].astype(F32) + a_ref[...].astype(F32))
    dx = g_ref[...].astype(F32) + pull_norm(normed, scale, dn * gain_ref[...])
    dx_ref[...] = dx
    da_ref[...] = dx.astype(BF16)


def resid_call(keep, core, chip, x, a_rel, g, gain, step=256):
    rows, width = keep.shape
    per = rows // step
    flat = pl.BlockSpec((step, width), lambda i: (i, 0))
    return pl.pallas_call(
        resid_kernel,
        out_shape=(
            jax.ShapeDtypeStruct((rows, width), F32),
            jax.ShapeDtypeStruct((rows, width), BF16),
        ),
        grid=(per,),
        in_specs=[
            flat,
            flat,
            flat,
            flat,
            pl.BlockSpec((None, step, width), lambda i: (0, i, 0)),
            flat,
            resident(gain.shape),
        ],
        out_specs=[flat, flat],
        compiler_params=vmem(52),
        cost_estimate=takes(5),
        name="resid",
    )(keep, core, chip, x, a_rel, g, gain)


def head_grad_kernel(s_ref, even_ref, odd_ref, w_ref, o_ref, *rest):
    do_ref, da_ref = rest[-2:]
    own = pl.program_id(0) == s_ref[2]
    da = jnp.where(own, even_ref[...], odd_ref[...])
    da_ref[...] = da
    do = dot(da, w_ref[...], 1, 0).astype(BF16).astype(F32)
    rows = do.shape[0]
    lane = lane_iota(rows)
    product = do * o_ref[...].astype(F32)
    for pair in range(do.shape[1] // LANES):
        cols = slice(pair * LANES, (pair + 1) * LANES)
        part = do[:, cols]
        for odd in range(2):
            inside = (lane >= HEAD_DIM) if odd else (lane < HEAD_DIM)
            delta = jnp.sum(jnp.where(inside, product[:, cols], 0.0), axis=1, keepdims=True)
            a, b, c = split_three(jnp.broadcast_to(-delta, (rows, LANES)))
            head = pltpu.roll(part, HEAD_DIM, 1) if odd else part
            tail = jnp.where(
                lane == 64, a, jnp.where(lane == 65, b, jnp.where(lane == 66, c, 0.0))
            )
            do_ref[2 * pair + odd] = jnp.where(lane < HEAD_DIM, head, tail).astype(BF16)


def head_grad_call(scalars, even, odd, w_out, o_chunk, far, tokens, held):
    rows, width = even.shape
    heads = o_chunk.shape[1] // HEAD_DIM
    held = list(held)
    return pl.pallas_call(
        head_grad_kernel,
        out_shape=(
            jax.ShapeDtypeStruct((heads, tokens, LANES), BF16),
            jax.ShapeDtypeStruct((tokens, width), BF16),
        ),
        grid_spec=pltpu.PrefetchScalarGridSpec(
            num_scalar_prefetch=1,
            grid=(2,),
            in_specs=[
                resident(even.shape),
                resident(odd.shape),
                resident(w_out.shape),
                pl.BlockSpec((rows, o_chunk.shape[1]), lambda i, s: (i, 0)),
            ]
            + [pl.BlockSpec(memory_space=pl.ANY)] * len(held),
            out_specs=[
                pl.BlockSpec((heads, rows, LANES), lambda i, s: (0, 2 * (s[3] ^ far) + i, 0)),
                pl.BlockSpec((rows, width), lambda i, s: (2 * far + i, 0)),
            ],
        ),
        input_output_aliases={5 + i: i for i in range(len(held))},
        compiler_params=vmem(52),
        cost_estimate=takes(6),
        name="head_grad",
    )(scalars, even, odd, w_out, o_chunk, *held)


def store_slices(out_ref, at, sums):
    for i in range(out_ref.shape[0]):
        out_ref[i, at] = sums[:, i * LANES : (i + 1) * LANES].astype(BF16)


def inner_kernel(n_ref, g_ref, dgate_ref, dup_ref, act_ref, out_ref, acc):
    step, last = pl.program_id(0), pl.num_programs(0) - 1
    for at, (right, left) in enumerate(((dgate_ref, n_ref), (dup_ref, n_ref), (act_ref, g_ref))):
        sums = dot(right[...], left[...], 0, 0)

        @pl.when(step == 0)
        def _(sums=sums, at=at):
            acc[at] = sums

        @pl.when((step > 0) & (step < last))
        def _(sums=sums, at=at):
            acc[at] += sums

        @pl.when(step == last)
        def _(sums=sums, at=at):
            store_slices(out_ref, at, acc[at] + sums)


def inner_call(n2, g_rel, dgate, dup, act, steps=4):
    tokens, width = n2.shape
    units = act.shape[1]
    step = tokens // steps
    out = (width // LANES, 3, units, LANES)
    wide = pl.BlockSpec((step, width), lambda i: (i, 0))
    narrow = pl.BlockSpec((step, units), lambda i: (i, 0))
    return pl.pallas_call(
        inner_kernel,
        out_shape=jax.ShapeDtypeStruct(out, BF16),
        grid=(steps,),
        in_specs=[wide, wide, narrow, narrow, narrow],
        out_specs=resident(out),
        scratch_shapes=[pltpu.VMEM((3, units, width), F32)],
        compiler_params=vmem(52),
        cost_estimate=takes(18),
        name="inner_grads",
    )(n2, g_rel, dgate, dup, act)


def proj_kernel(n_ref, d_ref, o0, o1, da_ref, out_ref, acc):
    step = pl.program_id(0)
    kinds = d_ref.shape[0]

    @pl.when(step == 0)
    def _():
        for at in range(kinds):
            acc[at] = dot(d_ref[at], n_ref[...], 0, 0)
        acc[kinds] = dot(o0[...], da_ref[...], 0, 0)

    @pl.when(step == 1)
    def _():
        for at in range(kinds):
            store_slices(out_ref, at, acc[at] + dot(d_ref[at], n_ref[...], 0, 0))
        store_slices(out_ref, kinds, acc[kinds] + dot(o1[...], da_ref[...], 0, 0))


def proj_call(n1, dproj, o_chunks, da):
    tokens, width = n1.shape
    kinds, _, cols = dproj.shape
    step = tokens // 2
    out = (width // LANES, kinds + 1, cols, LANES)
    wide = pl.BlockSpec((step, width), lambda i: (i, 0))
    return pl.pallas_call(
        proj_kernel,
        out_shape=jax.ShapeDtypeStruct(out, BF16),
        grid=(2,),
        in_specs=[
            wide,
            pl.BlockSpec((kinds, step, cols), lambda i: (0, i, 0)),
            resident(o_chunks[0].shape),
            resident(o_chunks[1].shape),
            wide,
        ],
        out_specs=resident(out),
        scratch_shapes=[pltpu.VMEM((kinds + 1, cols, width), F32)],
        compiler_params=vmem(52),
        cost_estimate=takes(10),
        name="proj_grads",
    )(n1, dproj, *o_chunks, da)


def dn_kernel(s_ref, p_ref, w_ref, out_ref):
    total = dot(p_ref[0], w_ref[0], 1, 1) + dot(p_ref[1], w_ref[1], 1, 1)
    out_ref[...] = (total + dot(p_ref[2], w_ref[2], 1, 1)).astype(BF16)


def dn_call(scalars, dproj, w_qkv, rel, rows):
    kinds, _, cols = dproj.shape
    width = w_qkv.shape[1]
    return pl.pallas_call(
        dn_kernel,
        out_shape=jax.ShapeDtypeStruct((rows, width), BF16),
        grid_spec=pltpu.PrefetchScalarGridSpec(
            num_scalar_prefetch=1,
            grid=(1,),
            in_specs=[
                pl.BlockSpec((kinds, rows, cols), lambda i, s: (0, rel ^ s[0], 0)),
                resident((kinds, width, cols)),
            ],
            out_specs=pl.BlockSpec((rows, width), lambda i, s: (0, 0)),
        ),
        compiler_params=vmem(52),
        cost_estimate=takes(0),
        name="dn",
    )(scalars, dproj, w_qkv)


def last_kernel(keep_ref, core_ref, chip_ref, x_ref, dx_ref, gain_ref, out_ref):
    dn = keep_ref[...].astype(F32) + core_ref[...].astype(F32) + chip_ref[...].astype(F32)
    dn = dn.astype(BF16).astype(F32)
    normed, scale = row_stats(x_ref[...].astype(F32))
    out_ref[...] = (dx_ref[...] + pull_norm(normed, scale, dn * gain_ref[...])).astype(BF16)


def last_call(keep, core, chip, x, dx, gain, step=256):
    rows, width = x.shape
    per = rows // step
    flat = pl.BlockSpec((step, width), lambda i: (i, 0))
    return pl.pallas_call(
        last_kernel,
        out_shape=jax.ShapeDtypeStruct((rows, width), BF16),
        grid=(per,),
        in_specs=[flat] * 5 + [resident(gain.shape)],
        out_specs=flat,
        compiler_params=vmem(52),
        cost_estimate=takes(0),
        name="last",
    )(keep, core, chip, x, dx, gain)


def turn_rows_kernel(hot_ref, rows_ref, out_ref):
    out_ref[...] = dot(hot_ref[...], rows_ref[...], 0, 0).astype(BF16)


def turn_rows(one_hot, values):
    return pl.pallas_call(
        turn_rows_kernel,
        out_shape=jax.ShapeDtypeStruct(values.shape, BF16),
        compiler_params=vmem(52),
        cost_estimate=takes(0),
        name="turn_rows",
    )(one_hot, values)


def bits_of(count):
    return [1 << i for i in range(count.bit_length() - 1)]


def pick(values, axis, index):
    return lax.dynamic_index_in_dim(values, index, axis, keepdims=False)


def by_device(values, count):
    blocks = values.shape[0]
    if blocks == count:
        return values
    axis = values.shape.index(LANES, 2)
    shape = values.shape[:axis] + (count // blocks, LANES * blocks // count) + values.shape[axis + 1 :]
    values = jnp.moveaxis(values.reshape(shape), axis, 1)
    return values.reshape((count,) + values.shape[2:])


def after(point, *values):
    return lax.optimization_barrier((point, *values))[1:]


def gather_bits(values, axis_name):
    me = lax.axis_index(axis_name)
    count = lax.axis_size(axis_name)
    shape = values.shape
    for bit in reversed(bits_of(count)):
        other = swap_bit(values, axis_name, bit)
        high = (me // bit) % 2 == 1
        values = jnp.stack([jnp.where(high, other, values), jnp.where(high, values, other)])
    lead = values.ndim - len(shape)
    order = tuple(reversed(range(lead))) + tuple(range(lead, values.ndim))
    return values.transpose(order).reshape((count,) + shape)


def scatter_lanes(values):
    me = lax.axis_index("mp")
    count = lax.axis_size("mp")
    slices = values.reshape(values.shape[0], count, values.shape[1] // count)
    total = pick(slices, 1, me)
    for bits in range(1, count):
        total = total + swap_bit(pick(slices, 1, me ^ bits), "mp", bits)
    return total


def local(
    hidden_in, out_grad, seq_lengths, dealing, attn_gain, mlp_gain, w_qkv, w_out, w_in, w_down
):
    dp_count = lax.axis_size("dp")
    mp_count = lax.axis_size("mp")
    owner = lax.axis_index("dp")
    lane = lax.axis_index("mp")
    rows, width = hidden_in.shape
    tokens = rows * mp_count
    shards = width // dp_count
    slots = rows // dp_count
    first_len = pick(seq_lengths, 0, 2 * owner)
    scalars = jnp.stack([lane, first_len, lane % 2, lane // 2]).astype(jnp.int32)

    lane_rows = pick(dealing.reshape(dp_count, mp_count, rows), 1, lane)
    local_row = lane_rows - (owner * mp_count + lane) * rows
    inside = (local_row >= 0) & (local_row < rows)
    order = jnp.arange(rows, dtype=jnp.int32)
    upto = (order[:, None] <= order[None, :]).astype(BF16)
    rank = dot(inside.astype(BF16), upto, 1, 0).astype(jnp.int32) - 1
    slot_hit = inside[:, None, :] & (rank[:, None, :] == jnp.arange(slots)[None, :, None])
    send_row = jnp.sum(jnp.where(slot_hit, local_row[:, None, :], 0), axis=2).reshape(rows)
    to_slot = (send_row[:, None] == order[None, :]).astype(BF16)
    source = pick(lane_rows, 0, owner) // (rows * mp_count)
    from_src = source[None, :] == jnp.arange(dp_count, dtype=jnp.int32)[:, None]
    src_rank = dot(from_src.astype(BF16), upto, 1, 0).astype(jnp.int32) - 1
    slot_of = source * slots + jnp.sum(jnp.where(from_src, src_rank, 0), axis=0)
    to_dealt = (slot_of[:, None] == order[None, :]).astype(BF16)

    def exchange(values):
        packed = values.reshape(dp_count, slots, width)
        arrived = lax.all_to_all(packed, "dp", split_axis=0, concat_axis=0, tiled=True)
        return arrived.reshape(rows, width)

    def pack(values):
        return dot(to_slot, values, 1, 0).astype(BF16)

    def unpack(values):
        return dot(to_dealt, values, 1, 0).astype(BF16)

    def pack_back(values):
        return dot(to_dealt, values, 0, 0).astype(BF16)

    def unpack_back(values):
        return dot(to_slot, values, 0, 0).astype(BF16)

    def group(values):
        across = swap_bit(values, "mp", 2)
        return [values, swap_bit(values, "mp", 1), across, swap_bit(across, "mp", 1)]

    gains = gather_bits(gather_bits(jnp.stack([attn_gain, mlp_gain]), "dp"), "mp")
    gains = gains.transpose(2, 1, 0, 3).reshape(2, width)
    place = jnp.arange(tokens, dtype=jnp.int32)
    place = jnp.where(place >= first_len, place - first_len, place).astype(F32)
    freq_index = jnp.arange(LANES, dtype=jnp.int32) % (HEAD_DIM // 2)
    freqs = jnp.exp(freq_index.astype(F32) * (-2.0 * math.log(theta_base) / HEAD_DIM))
    angles = place[:, None] * freqs[None, :]
    first_half = jnp.arange(LANES) % HEAD_DIM < HEAD_DIM // 2
    cos = jnp.cos(angles)
    sin = jnp.sin(angles) * jnp.where(first_half, -1.0, 1.0)[None, :]

    w_mlp = jnp.concatenate([w_in, w_down.T[None]], axis=0)
    x_arrived = exchange(pack(hidden_in))
    x_arrived, gains, cos, sin, scalars, g_packed = lax.optimization_barrier(
        (x_arrived, gains, cos, sin, scalars, pack(out_grad))
    )
    w_mlp = lax.all_gather(w_mlp, "dp", axis=1, tiled=True)
    gain_one, gain_two = gains[0:1], gains[1:2]
    x_mine = unpack(x_arrived)
    x_rel = group(x_mine)
    attn_weights = jnp.concatenate([w_qkv, w_out.T[None]], axis=0)
    attn_weights = jnp.moveaxis(gather_bits(attn_weights, "dp"), 0, 1).reshape(4, width, -1)
    w_out_across = swap_bit(attn_weights[3], "mp", 2)
    g_packed, attn_weights = lax.optimization_barrier((g_packed, attn_weights))
    g_arrived = exchange(g_packed)

    held = qkv_call(scalars, x_rel[0], x_rel[1], gain_one, attn_weights, cos, sin, 0, ())
    q, k, v, n1 = qkv_call(scalars, x_rel[2], x_rel[3], gain_one, attn_weights, cos, sin, 2, held)
    q, w_out_across = lax.optimization_barrier((q, w_out_across))
    w_out_rel = [attn_weights[3], None, w_out_across, None]
    w_out_rel[1], w_out_rel[3] = swap_bit(w_out_rel[0], "mp", 1), swap_bit(w_out_across, "mp", 1)
    near, q2, near_top = attend_forward(scalars, q, k, v, 0, 2 * rows, ())
    (g_arrived,) = after(near, g_arrived)
    g_mine = unpack(g_arrived)
    g_core, g_across = swap_bit(g_mine, "mp", 1), swap_bit(g_mine, "mp", 2)
    near_across = swap_bit(near, "mp", 2)
    distant, q2, far_top = attend_forward(scalars, q, k, v, 1, 2 * rows, (q2,))
    distant, near_across, g_across = lax.optimization_barrier((distant, near_across, g_across))
    g_rel = [g_mine, g_core, g_across, swap_bit(g_across, "mp", 1)]
    far_across = swap_bit(distant, "mp", 2)
    core = lambda values: swap_bit(values, "mp", 1)
    far_heads = [distant, core(distant), near_across, core(near_across)]
    peaks = [near_top, far_top]
    head_peaks = jnp.max(jnp.stack(peaks), axis=(0, 1, 3, 4)) * score_scale
    peak_bits = bits_of(dp_count)
    peak_swap = swap_bit(head_peaks, "dp", peak_bits[0])

    *held, keep, send, keep_out, send_out = mlp_call(
        scalars,
        (x_rel[3], x_rel[2]),
        (g_rel[3], g_rel[2]),
        far_heads,
        w_out_rel,
        gain_two,
        w_mlp,
        2,
        (),
    )
    far_across, peak_swap, send, near = lax.optimization_barrier(
        (far_across, peak_swap, send, near)
    )
    head_peaks = jnp.maximum(head_peaks, peak_swap)
    peak_swap = swap_bit(head_peaks, "dp", peak_bits[1])
    dn_far = (keep + core(send).astype(F32)).astype(BF16)
    dn_arrived = swap_bit(dn_far, "mp", 2)
    near_heads = [near, core(near), far_across, core(far_across)]
    (near_heads[0],) = after(dn_far, near)
    far_out = (keep_out, send_out)
    a_rel, n2, g_all, act, dgate, dup, keep, send, keep_out, send_out = mlp_call(
        scalars,
        (x_rel[1], x_rel[0]),
        (g_rel[1], g_rel[0]),
        near_heads,
        w_out_rel,
        gain_two,
        w_mlp,
        0,
        held,
    )
    dn_arrived, peak_swap, send = lax.optimization_barrier((dn_arrived, peak_swap, send))
    head_peaks = jnp.maximum(head_peaks, peak_swap)
    peak_swap = swap_bit(head_peaks, "dp", peak_bits[2])
    dx, da = resid_call(
        keep, core(send), dn_arrived, x_rel[0], a_rel, g_rel[0], gain_two
    )
    da_core, da_across = core(da), swap_bit(da, "mp", 2)

    flat = lambda values: values.reshape(tokens, values.shape[2])
    (act,) = after(da, act)
    inner_grads = inner_call(flat(n2), flat(g_all), flat(dgate), flat(dup), flat(act))
    held = list(head_grad_call(scalars, da, da_core, attn_weights[3], near, 0, tokens, ()))
    _, da_across, held[0] = lax.optimization_barrier((inner_grads, da_across, held[0]))
    do, da_all = head_grad_call(
        scalars, da_across, core(da_across), attn_weights[3], distant, 1, tokens, held
    )
    head_peaks = jnp.maximum(head_peaks, peak_swap)
    for bit in peak_bits[3:]:
        head_peaks = jnp.maximum(head_peaks, swap_bit(head_peaks, "dp", bit))
    inner_grads, peak_swap = lax.optimization_barrier((inner_grads, peak_swap))
    inner_grads = by_device(inner_grads, dp_count)
    inner_grads = lax.all_to_all(inner_grads, "dp", split_axis=0, concat_axis=0, tiled=True)


    far_out = after(da_across, *far_out)
    add_core = lambda keep, send: keep.astype(F32) + core(send).astype(F32)

    out_far = add_core(*far_out).astype(BF16)
    out_arrived = swap_bit(out_far, "mp", 2)
    do, out_sum = after(out_far, do, add_core(keep_out, send_out))
    dproj = attend_backward(scalars, q2, k, v, do, cos, sin)
    head_peaks = jnp.maximum(head_peaks, peak_swap)
    for bit in peak_bits[3:]:
        head_peaks = jnp.maximum(head_peaks, swap_bit(head_peaks, "dp", bit))
    factor = jnp.sqrt(clip_limit / jnp.maximum(head_peaks, clip_limit))
    column_factor = jnp.repeat(factor, HEAD_DIM)
    scaling = jnp.stack([column_factor, column_factor, jnp.ones_like(column_factor)])[:, None, :]
    clipped = (w_qkv.astype(F32) * scaling).astype(BF16)

    proj_grad = proj_call(n1, dproj, (near, distant), da_all)
    proj_grad, dproj, out_arrived = lax.optimization_barrier((proj_grad, dproj, out_arrived))
    far_core = core(dn_call(scalars, dproj, attn_weights, 3, rows))
    far_keep = dn_call(scalars, dproj, attn_weights, 2, rows)
    dn_far = (far_keep.astype(F32) + far_core.astype(F32)).astype(BF16)
    dn_arrived = swap_bit(dn_far, "mp", 2)
    inner_grads, dn_far, out_arrived = lax.optimization_barrier((inner_grads, dn_far, out_arrived))
    x1 = x_rel[0].astype(F32) + a_rel[0].astype(F32)
    out_packed = pack_back((x1 + (out_sum + out_arrived.astype(F32))).astype(BF16))
    (dproj,) = after(out_packed, dproj)
    out_sent = exchange(out_packed)
    send = dn_call(scalars, dproj, attn_weights, 1, rows)
    keep = dn_call(scalars, dproj, attn_weights, 0, rows)
    dn_core = core(send)
    inner_grads = jnp.sum(inner_grads.astype(F32), axis=0)
    inner_grad, down_grad = jnp.swapaxes(inner_grads[:2], 1, 2), inner_grads[2]
    inner_by_gain = jnp.sum(inner_grad * w_in.astype(F32), axis=(0, 2))
    gain_part = lax.dynamic_slice_in_dim(gains, owner * shards, shards, 1)
    inner_grad, down_grad, inner_by_gain, gain_part, clipped, keep = lax.optimization_barrier(
        (inner_grad, down_grad, inner_by_gain, gain_part, clipped, keep)
    )
    out_sent, dn_arrived, dn_core = lax.optimization_barrier((out_sent, dn_arrived, dn_core))
    grad_packed = pack_back(last_call(keep, dn_core, dn_arrived, x_rel[0], dx, gain_one))
    grad_arrived = exchange(grad_packed)
    (out_arrived,) = after(grad_packed, out_sent)
    output = turn_rows(to_slot, out_arrived)
    grads = lax.psum_scatter(by_device(proj_grad, dp_count), "dp")
    (grads,) = after(output, grads)
    grad_arrived, grads = lax.optimization_barrier((grad_arrived, grads))
    grads = grads.astype(F32)
    input_grad = unpack_back(grad_arrived)
    proj_grad, outer_grad = jnp.swapaxes(grads[:3], 1, 2), grads[3]

    by_gain = jnp.stack([jnp.sum(proj_grad * w_qkv.astype(F32), axis=(0, 2)), inner_by_gain])
    gain_grads = scatter_lanes(by_gain / gain_part)
    return (
        output,
        input_grad,
        gain_grads[0],
        gain_grads[1],
        proj_grad,
        outer_grad,
        inner_grad,
        down_grad,
        clipped,
    )


def solution(mesh):
    in_specs = (
        P(("dp", "mp"), None),
        P(("dp", "mp"), None),
        P(),
        P(),
        P(("dp", "mp")),
        P(("dp", "mp")),
        P(None, "dp", "mp"),
        P("mp", "dp"),
        P(None, "dp", "mp"),
        P("mp", "dp"),
    )
    out_specs = (
        P(("dp", "mp"), None),
        P(("dp", "mp"), None),
        P(("dp", "mp")),
        P(("dp", "mp")),
        P(None, "dp", "mp"),
        P("mp", "dp"),
        P(None, "dp", "mp"),
        P("mp", "dp"),
        P(None, "dp", "mp"),
    )
    return jax.shard_map(local, mesh=mesh, in_specs=in_specs, out_specs=out_specs, check_vma=False)
```

```python
import functools
import math

import jax
import jax.numpy as jnp
from jax import lax
from jax.experimental import pallas as pl
from jax.experimental.pallas import tpu as pltpu
from jax.sharding import PartitionSpec as P

HEAD_DIM = 64
LANES = 128
theta_base = 160000.0
norm_eps = 1e-05
clip_limit = 5.0
score_scale = 0.125
exp_scale = score_scale * math.log2(math.e)
far_away = -1e30
lowest = -3e38

BF16 = jnp.bfloat16
F32 = jnp.float32


def dot(left, right, left_dim, right_dim):
    return lax.dot_general(
        left, right, (((left_dim,), (right_dim,)), ((), ())), preferred_element_type=F32
    )


def split_three(values):
    high = values.astype(BF16).astype(F32)
    rest = values - high
    middle = rest.astype(BF16).astype(F32)
    return high, middle, rest - middle


def row_stats(values):
    mean = jnp.mean(values, axis=-1, keepdims=True)
    centered = values - mean
    variance = jnp.mean(centered * centered, axis=-1, keepdims=True)
    scale = lax.rsqrt(variance + norm_eps)
    return centered * scale, scale


def turn(values, lane):
    return jnp.where(
        lane % HEAD_DIM < HEAD_DIM // 2,
        pltpu.roll(values, LANES - HEAD_DIM // 2, 1),
        pltpu.roll(values, HEAD_DIM // 2, 1),
    )


def swap_bit(values, axis_name, bit):
    count = lax.axis_size(axis_name)
    return lax.ppermute(values, axis_name, [(i, i ^ bit) for i in range(count)])


def lane_iota(rows):
    return lax.broadcasted_iota(jnp.int32, (rows, LANES), 1)


def vmem(mib):
    return pltpu.CompilerParams(vmem_limit_bytes=mib << 20)


def takes(micros):
    flops = max(micros * 1_100_000_000, 1024)
    return pl.CostEstimate(flops=flops, bytes_accessed=flops // 1024, transcendentals=0)


def resident(shape):
    zeros = (0,) * len(shape)
    return pl.BlockSpec(shape, lambda *_: zeros, pipeline_mode=pl.Buffered(1))


def qkv_kernel(step, per, first, s_ref, xa_ref, xb_ref, gain_ref, w_ref, cos_ref, sin_ref, *rest):
    q_ref, k_ref, v_ref, n_ref = rest[-4:]
    first_len = s_ref[1]
    at = pl.program_id(0)
    x = jnp.where(at < per, xa_ref[...], xb_ref[...])
    normed, _ = row_stats(x.astype(F32))
    n1 = (normed * gain_ref[...]).astype(BF16)
    n_ref[...] = n1
    lane = lane_iota(step)
    start = (((first + at // per) ^ s_ref[0]) * per + at % per) * step
    row = start + lax.broadcasted_iota(jnp.int32, (step, LANES), 0)
    second = row >= first_len
    one, zero = jnp.float32(1), jnp.float32(0)
    q_tail = jnp.where(lane == 64 + second.astype(jnp.int32), one, zero)
    k_tail = jnp.where(
        lane == 65 - second.astype(jnp.int32),
        jnp.float32(far_away),
        jnp.where((lane >= 66) & (lane < 69), one, zero),
    )
    cos, sin = cos_ref[...], sin_ref[...]
    for which, (out, tail) in enumerate(((q_ref, q_tail), (k_ref, k_tail), (v_ref, one))):
        projected = dot(n1, w_ref[which], 1, 0)
        for pair in range(projected.shape[1] // LANES):
            part = projected[:, pair * LANES : (pair + 1) * LANES]
            if which < 2:
                part = part * cos + turn(part, lane) * sin
            out[2 * pair] = jnp.where(lane < HEAD_DIM, part, tail).astype(BF16)
            out[2 * pair + 1] = jnp.where(
                lane < HEAD_DIM, pltpu.roll(part, HEAD_DIM, 1), tail
            ).astype(BF16)


def qkv_call(scalars, xa, xb, gain, w_qkv, cos, sin, first, held, step=512):
    rows, width = xa.shape
    tokens = cos.shape[0]
    cols = w_qkv.shape[2]
    heads = cols // HEAD_DIM
    per = rows // step
    ext = jax.ShapeDtypeStruct((heads, tokens, LANES), BF16)
    place = lambda i, s: (((first + i // per) ^ s[0]) * per + i % per, 0)
    head_spec = pl.BlockSpec((heads, step, LANES), lambda i, s: (0, *place(i, s)))
    held = list(held)
    return pl.pallas_call(
        functools.partial(qkv_kernel, step, per, first),
        out_shape=(ext, ext, ext, jax.ShapeDtypeStruct((tokens, width), BF16)),
        grid_spec=pltpu.PrefetchScalarGridSpec(
            num_scalar_prefetch=1,
            grid=(2 * per,),
            in_specs=[
                pl.BlockSpec((step, width), lambda i, s: (jnp.minimum(i, per - 1), 0)),
                pl.BlockSpec((step, width), lambda i, s: (jnp.maximum(i - per, 0), 0)),
                resident(gain.shape),
                resident((3, width, cols)),
                pl.BlockSpec((step, LANES), place),
                pl.BlockSpec((step, LANES), place),
            ]
            + [pl.BlockSpec(memory_space=pl.ANY)] * len(held),
            out_specs=[head_spec] * 3 + [pl.BlockSpec((step, width), place)],
        ),
        input_output_aliases={7 + i: i for i in range(len(held))},
        compiler_params=vmem(52),
        cost_estimate=takes(3),
        name="qkv",
    )(scalars, xa, xb, gain, w_qkv, cos, sin, *held)


def key_range(first_len, row, q_rows, k_rows, tokens):
    low = jnp.where(row >= first_len, first_len // k_rows, 0)
    high = jnp.where(row + q_rows <= first_len, (first_len + k_rows - 1) // k_rows, tokens // k_rows)
    return low, high


def fwd_kernel(
    far, q_rows, k_rows, s_ref, q_ref, k_ref, v_ref, *rest
):
    o_ref, q2_ref, top_ref, score, peak, acc = rest[-6:]
    heads, tokens, _ = k_ref.shape
    low, high = key_range(
        s_ref[1],
        ((s_ref[3] ^ far) * pl.num_programs(0) + pl.program_id(0)) * q_rows,
        q_rows,
        k_rows,
        tokens,
    )
    lane = lane_iota(q_rows)
    peak[...] = jnp.full(peak.shape, lowest, F32)
    acc[...] = jnp.zeros(acc.shape, F32)

    def first_pass(block, carry):
        keys = pl.ds(pl.multiple_of(block * k_rows, k_rows), k_rows)
        for h in range(heads):
            s = dot(q_ref[h], k_ref[h, keys, :], 1, 1)
            score[h, :, keys] = s
            most = peak[h]
            for t in range(k_rows // LANES):
                most = jnp.maximum(most, s[:, t * LANES : (t + 1) * LANES])
            peak[h] = most
        return carry

    lax.fori_loop(low, high, first_pass, 0)
    for h in range(heads):
        peak[h] = jnp.broadcast_to(jnp.max(peak[h], axis=1, keepdims=True), (q_rows, LANES))

    def second_pass(block, carry):
        keys = pl.ds(pl.multiple_of(block * k_rows, k_rows), k_rows)
        for h in range(heads):
            s, most = score[h, :, keys], peak[h]
            p = jnp.concatenate(
                [
                    jnp.exp2((s[:, t * LANES : (t + 1) * LANES] - most) * exp_scale).astype(BF16)
                    for t in range(k_rows // LANES)
                ],
                axis=1,
            )
            acc[h] += dot(p, v_ref[h, keys, :], 1, 0)
        return carry

    lax.fori_loop(low, high, second_pass, 0)
    held = None
    for h in range(heads):
        sums = acc[h]
        total = jnp.where(lane < HEAD_DIM, pltpu.roll(sums, HEAD_DIM, 1), sums)
        out = sums / total
        log_total = peak[h] + jnp.log2(total) * (1.0 / exp_scale)
        a, b, c = split_three(-log_total)
        q2 = q_ref[h].astype(F32)
        q2 = jnp.where(lane == 66, a, jnp.where(lane == 67, b, jnp.where(lane == 68, c, q2)))
        q2_ref[h] = q2.astype(BF16)
        top_ref[h] = jnp.broadcast_to(jnp.max(peak[h], axis=0, keepdims=True), (8, LANES))
        if h % 2 == 0:
            held = out
        else:
            both = jnp.where(lane < HEAD_DIM, held, pltpu.roll(out, HEAD_DIM, 1))
            o_ref[:, (h // 2) * LANES : (h // 2 + 1) * LANES] = both.astype(BF16)


def attend_forward(scalars, q, k, v, far, rows, held, q_rows=256, k_rows=1024):
    heads, tokens, _ = k.shape
    count = rows // q_rows
    k_rows = min(k_rows, tokens)
    return pl.pallas_call(
        functools.partial(fwd_kernel, far, q_rows, k_rows),
        out_shape=(
            jax.ShapeDtypeStruct((rows, heads * HEAD_DIM), BF16),
            jax.ShapeDtypeStruct(q.shape, BF16),
            jax.ShapeDtypeStruct((count, heads, 8, LANES), F32),
        ),
        grid_spec=pltpu.PrefetchScalarGridSpec(
            num_scalar_prefetch=1,
            grid=(count,),
            in_specs=[
                pl.BlockSpec((heads, q_rows, LANES), lambda i, s: (0, (s[3] ^ far) * count + i, 0)),
                resident(k.shape),
                resident(v.shape),
            ]
            + [pl.BlockSpec(memory_space=pl.ANY)] * len(held),
            out_specs=[
                pl.BlockSpec((q_rows, heads * HEAD_DIM), lambda i, s: (i, 0)),
                pl.BlockSpec((heads, q_rows, LANES), lambda i, s: (0, (s[3] ^ far) * count + i, 0)),
                pl.BlockSpec((None, heads, 8, LANES), lambda i, s: (i, 0, 0, 0)),
            ],
            scratch_shapes=[
                pltpu.VMEM((heads, q_rows, tokens), F32),
                pltpu.VMEM((heads, q_rows, LANES), F32),
                pltpu.VMEM((heads, q_rows, LANES), F32),
            ],
        ),
        compiler_params=vmem(52),
        cost_estimate=takes(20),
        input_output_aliases={4 + i: 1 + i for i in range(len(held))},
        name="attend_forward",
    )(scalars, q, k, v, *held)


def bwd_kernel(
    q_rows, k_rows, s_ref, q2_ref, k_ref, v_ref, do_ref, cos_ref, sin_ref, out_ref, dk_ref, dv_ref
):
    heads, tokens, _ = k_ref.shape
    step = pl.program_id(0)
    low, high = key_range(s_ref[1], step * q_rows, q_rows, k_rows, tokens)

    @pl.when(step == 0)
    def _():
        dk_ref[...] = jnp.zeros_like(dk_ref)
        dv_ref[...] = jnp.zeros_like(dv_ref)

    def body(block, sums):
        keys = pl.ds(pl.multiple_of(block * k_rows, k_rows), k_rows)
        new = []
        for h in range(heads):
            key, q2, do = k_ref[h, keys, :], q2_ref[h], do_ref[h]
            p = jnp.exp2(dot(key, q2, 1, 1) * exp_scale)
            ds = (p * dot(v_ref[h, keys, :], do, 1, 1)).astype(BF16)
            dv_ref[h, keys, :] += dot(p.astype(BF16), do, 1, 0)
            dk_ref[h, keys, :] += dot(ds, q2, 1, 0)
            new.append(sums[h] + dot(key, ds, 0, 0))
        return tuple(new)

    sums = lax.fori_loop(
        low, high, body, tuple(jnp.zeros((LANES, q_rows), F32) for _ in range(heads))
    )
    lane = lane_iota(q_rows)

    def unrotate(first, second, rows):
        both = jnp.where(lane < HEAD_DIM, first, pltpu.roll(second, HEAD_DIM, 1)) * score_scale
        return both * cos_ref[rows, :] - turn(both, lane) * sin_ref[rows, :]

    here = pl.ds(pl.multiple_of(step * q_rows, q_rows), q_rows)
    for pair in range(heads // 2):
        cols = slice(pair * LANES, (pair + 1) * LANES)
        out_ref[0, here, cols] = unrotate(sums[2 * pair].T, sums[2 * pair + 1].T, here).astype(BF16)

    @pl.when(step == pl.num_programs(0) - 1)
    def _():
        def finish(block, carry):
            rows = pl.ds(pl.multiple_of(block * q_rows, q_rows), q_rows)
            for pair in range(heads // 2):
                cols = slice(pair * LANES, (pair + 1) * LANES)
                one, two = 2 * pair, 2 * pair + 1
                out_ref[1, rows, cols] = unrotate(
                    dk_ref[one, rows, :], dk_ref[two, rows, :], rows
                ).astype(BF16)
                out_ref[2, rows, cols] = jnp.where(
                    lane < HEAD_DIM,
                    dv_ref[one, rows, :],
                    pltpu.roll(dv_ref[two, rows, :], HEAD_DIM, 1),
                ).astype(BF16)
            return carry

        lax.fori_loop(0, tokens // q_rows, finish, 0)


def attend_backward(scalars, q2, k, v, do, cos, sin, q_rows=256, k_rows=512):
    heads, tokens, _ = k.shape
    block = lambda: pl.BlockSpec((heads, q_rows, LANES), lambda i, s: (0, i, 0))
    out = (3, tokens, heads * HEAD_DIM)
    return pl.pallas_call(
        functools.partial(bwd_kernel, q_rows, k_rows),
        out_shape=jax.ShapeDtypeStruct(out, BF16),
        grid_spec=pltpu.PrefetchScalarGridSpec(
            num_scalar_prefetch=1,
            grid=(tokens // q_rows,),
            in_specs=[
                block(),
                resident(k.shape),
                resident(v.shape),
                block(),
                resident(cos.shape),
                resident(sin.shape),
            ],
            out_specs=resident(out),
            scratch_shapes=[
                pltpu.VMEM((heads, tokens, LANES), F32),
                pltpu.VMEM((heads, tokens, LANES), F32),
            ],
        ),
        compiler_params=vmem(52),
        cost_estimate=takes(20),
        name="attend_backward",
    )(scalars, q2, k, v, do, cos, sin)


def mlp_kernel(
    s_ref, xs_ref, xk_ref, gs_ref, gk_ref, o0, o1, o2, o3, w0, w1, w2, w3, gain_ref, w_ref, *rest
):
    a_ref, n_ref, g_out, act_ref, dgate_ref, dup_ref = rest[-10:-4]
    keep_ref, send_ref, keep_out, send_out = rest[-4:]
    units = w_ref.shape[2]
    sending = pl.program_id(0) < pl.num_programs(0) // 2
    x = jnp.where(sending, xs_ref[...], xk_ref[...])
    g = jnp.where(sending, gs_ref[...], gk_ref[...])
    branch = dot(o0[...], w0[...], 1, 1) + dot(o1[...], w1[...], 1, 1)
    branch = branch + dot(o2[...], w2[...], 1, 1) + dot(o3[...], w3[...], 1, 1)
    branch = branch.astype(BF16)
    a_ref[...] = branch
    normed, _ = row_stats(x.astype(F32) + branch.astype(F32))
    n2 = (normed * gain_ref[...]).astype(BF16)
    n_ref[...] = n2
    g_out[...] = g
    partial = out_partial = 0.0
    for low in range(0, units, 256):
        cols = slice(low, min(low + 256, units))
        gate = dot(n2, w_ref[0, :, cols], 1, 0)
        up = dot(n2, w_ref[1, :, cols], 1, 0)
        dact = dot(g, w_ref[2, :, cols], 1, 0)
        phi = 0.5 + 0.5 * lax.erf(gate * math.sqrt(0.5))
        gelu = gate * phi
        act = (gelu * up).astype(BF16)
        act_ref[:, cols] = act
        density = jnp.exp(-0.5 * gate * gate) * (1.0 / math.sqrt(2.0 * math.pi))
        dgate = (dact * up * (phi + gate * density)).astype(BF16)
        dup = (dact * gelu).astype(BF16)
        dgate_ref[:, cols] = dgate
        dup_ref[:, cols] = dup
        partial = partial + dot(dgate, w_ref[0, :, cols], 1, 1) + dot(dup, w_ref[1, :, cols], 1, 1)
        out_partial = out_partial + dot(act, w_ref[2, :, cols], 1, 1)

    @pl.when(sending)
    def _():
        send_ref[...] = partial.astype(BF16)
        send_out[...] = out_partial.astype(BF16)

    @pl.when(jnp.logical_not(sending))
    def _():
        keep_ref[...] = partial
        keep_out[...] = out_partial.astype(BF16)


def mlp_call(scalars, x_pair, g_pair, heads_rel, w_out_rel, gain, w_mlp, first, held, step=256):
    rows, width = x_pair[0].shape
    units = w_mlp.shape[2]
    per = rows // step
    rel = lambda i, s: (first + 1 - i // per, i % per, 0)
    wide = pl.BlockSpec((None, step, width), rel)
    narrow = pl.BlockSpec((None, step, units), rel)
    wide_out = jax.ShapeDtypeStruct((4, rows, width), BF16)
    narrow_out = jax.ShapeDtypeStruct((4, rows, units), BF16)
    send = pl.BlockSpec((step, width), lambda i, s: (jnp.minimum(i, per - 1), 0))
    keep = pl.BlockSpec((step, width), lambda i, s: (jnp.maximum(i - per, 0), 0))
    head_spec = pl.BlockSpec(
        (step, heads_rel[0].shape[1]), lambda i, s: (((i // per) ^ 1 ^ s[2]) * per + i % per, 0)
    )
    held = list(held)
    half = lambda kind: jax.ShapeDtypeStruct((rows, width), kind)
    return pl.pallas_call(
        mlp_kernel,
        out_shape=(
            wide_out,
            wide_out,
            wide_out,
            narrow_out,
            narrow_out,
            narrow_out,
            half(F32),
            half(BF16),
            half(BF16),
            half(BF16),
        ),
        grid_spec=pltpu.PrefetchScalarGridSpec(
            num_scalar_prefetch=1,
            grid=(2 * per,),
            in_specs=[send, keep, send, keep]
            + [head_spec] * len(heads_rel)
            + [resident(w.shape) for w in w_out_rel]
            + [resident(gain.shape), resident(w_mlp.shape)]
            + [pl.BlockSpec(memory_space=pl.ANY)] * len(held),
            out_specs=[wide, wide, wide, narrow, narrow, narrow, keep, send, keep, send],
        ),
        input_output_aliases={15 + i: i for i in range(len(held))},
        compiler_params=vmem(52),
        cost_estimate=takes(24),
        name="mlp",
    )(scalars, *x_pair, *g_pair, *heads_rel, *w_out_rel, gain, w_mlp, *held)


def pull_norm(normed, scale, cotangent):
    mean = jnp.mean(cotangent, axis=-1, keepdims=True)
    along = jnp.mean(cotangent * normed, axis=-1, keepdims=True)
    return (cotangent - mean - normed * along) * scale


def resid_kernel(keep_ref, core_ref, chip_ref, x_ref, a_ref, g_ref, gain_ref, dx_ref, da_ref):
    dn = keep_ref[...] + core_ref[...].astype(F32) + chip_ref[...].astype(F32)
    normed, scale = row_stats(x_ref[...].astype(F32) + a_ref[...].astype(F32))
    dx = g_ref[...].astype(F32) + pull_norm(normed, scale, dn * gain_ref[...])
    dx_ref[...] = dx
    da_ref[...] = dx.astype(BF16)


def resid_call(keep, core, chip, x, a_rel, g, gain, step=256):
    rows, width = keep.shape
    per = rows // step
    flat = pl.BlockSpec((step, width), lambda i: (i, 0))
    return pl.pallas_call(
        resid_kernel,
        out_shape=(
            jax.ShapeDtypeStruct((rows, width), F32),
            jax.ShapeDtypeStruct((rows, width), BF16),
        ),
        grid=(per,),
        in_specs=[
            flat,
            flat,
            flat,
            flat,
            pl.BlockSpec((None, step, width), lambda i: (0, i, 0)),
            flat,
            resident(gain.shape),
        ],
        out_specs=[flat, flat],
        compiler_params=vmem(52),
        cost_estimate=takes(5),
        name="resid",
    )(keep, core, chip, x, a_rel, g, gain)


def head_grad_kernel(s_ref, even_ref, odd_ref, w_ref, o_ref, *rest):
    do_ref, da_ref = rest[-2:]
    own = pl.program_id(0) == s_ref[2]
    da = jnp.where(own, even_ref[...], odd_ref[...])
    da_ref[...] = da
    do = dot(da, w_ref[...], 1, 0).astype(BF16).astype(F32)
    rows = do.shape[0]
    lane = lane_iota(rows)
    product = do * o_ref[...].astype(F32)
    for pair in range(do.shape[1] // LANES):
        cols = slice(pair * LANES, (pair + 1) * LANES)
        part = do[:, cols]
        for odd in range(2):
            inside = (lane >= HEAD_DIM) if odd else (lane < HEAD_DIM)
            delta = jnp.sum(jnp.where(inside, product[:, cols], 0.0), axis=1, keepdims=True)
            a, b, c = split_three(jnp.broadcast_to(-delta, (rows, LANES)))
            head = pltpu.roll(part, HEAD_DIM, 1) if odd else part
            tail = jnp.where(
                lane == 64, a, jnp.where(lane == 65, b, jnp.where(lane == 66, c, 0.0))
            )
            do_ref[2 * pair + odd] = jnp.where(lane < HEAD_DIM, head, tail).astype(BF16)


def head_grad_call(scalars, even, odd, w_out, o_chunk, far, tokens, held):
    rows, width = even.shape
    heads = o_chunk.shape[1] // HEAD_DIM
    held = list(held)
    return pl.pallas_call(
        head_grad_kernel,
        out_shape=(
            jax.ShapeDtypeStruct((heads, tokens, LANES), BF16),
            jax.ShapeDtypeStruct((tokens, width), BF16),
        ),
        grid_spec=pltpu.PrefetchScalarGridSpec(
            num_scalar_prefetch=1,
            grid=(2,),
            in_specs=[
                resident(even.shape),
                resident(odd.shape),
                resident(w_out.shape),
                pl.BlockSpec((rows, o_chunk.shape[1]), lambda i, s: (i, 0)),
            ]
            + [pl.BlockSpec(memory_space=pl.ANY)] * len(held),
            out_specs=[
                pl.BlockSpec((heads, rows, LANES), lambda i, s: (0, 2 * (s[3] ^ far) + i, 0)),
                pl.BlockSpec((rows, width), lambda i, s: (2 * far + i, 0)),
            ],
        ),
        input_output_aliases={5 + i: i for i in range(len(held))},
        compiler_params=vmem(52),
        cost_estimate=takes(6),
        name="head_grad",
    )(scalars, even, odd, w_out, o_chunk, *held)


def store_slices(out_ref, at, sums):
    for i in range(out_ref.shape[0]):
        out_ref[i, at] = sums[:, i * LANES : (i + 1) * LANES].astype(BF16)


def inner_kernel(n_ref, g_ref, dgate_ref, dup_ref, act_ref, out_ref, acc):
    step, last = pl.program_id(0), pl.num_programs(0) - 1
    for at, (right, left) in enumerate(((dgate_ref, n_ref), (dup_ref, n_ref), (act_ref, g_ref))):
        sums = dot(right[...], left[...], 0, 0)

        @pl.when(step == 0)
        def _(sums=sums, at=at):
            acc[at] = sums

        @pl.when((step > 0) & (step < last))
        def _(sums=sums, at=at):
            acc[at] += sums

        @pl.when(step == last)
        def _(sums=sums, at=at):
            store_slices(out_ref, at, acc[at] + sums)


def inner_call(n2, g_rel, dgate, dup, act, steps=4):
    tokens, width = n2.shape
    units = act.shape[1]
    step = tokens // steps
    out = (width // LANES, 3, units, LANES)
    wide = pl.BlockSpec((step, width), lambda i: (i, 0))
    narrow = pl.BlockSpec((step, units), lambda i: (i, 0))
    return pl.pallas_call(
        inner_kernel,
        out_shape=jax.ShapeDtypeStruct(out, BF16),
        grid=(steps,),
        in_specs=[wide, wide, narrow, narrow, narrow],
        out_specs=resident(out),
        scratch_shapes=[pltpu.VMEM((3, units, width), F32)],
        compiler_params=vmem(52),
        cost_estimate=takes(18),
        name="inner_grads",
    )(n2, g_rel, dgate, dup, act)


def proj_kernel(n_ref, d_ref, o0, o1, da_ref, out_ref, acc):
    step = pl.program_id(0)
    kinds = d_ref.shape[0]

    @pl.when(step == 0)
    def _():
        for at in range(kinds):
            acc[at] = dot(d_ref[at], n_ref[...], 0, 0)
        acc[kinds] = dot(o0[...], da_ref[...], 0, 0)

    @pl.when(step == 1)
    def _():
        for at in range(kinds):
            store_slices(out_ref, at, acc[at] + dot(d_ref[at], n_ref[...], 0, 0))
        store_slices(out_ref, kinds, acc[kinds] + dot(o1[...], da_ref[...], 0, 0))


def proj_call(n1, dproj, o_chunks, da):
    tokens, width = n1.shape
    kinds, _, cols = dproj.shape
    step = tokens // 2
    out = (width // LANES, kinds + 1, cols, LANES)
    wide = pl.BlockSpec((step, width), lambda i: (i, 0))
    return pl.pallas_call(
        proj_kernel,
        out_shape=jax.ShapeDtypeStruct(out, BF16),
        grid=(2,),
        in_specs=[
            wide,
            pl.BlockSpec((kinds, step, cols), lambda i: (0, i, 0)),
            resident(o_chunks[0].shape),
            resident(o_chunks[1].shape),
            wide,
        ],
        out_specs=resident(out),
        scratch_shapes=[pltpu.VMEM((kinds + 1, cols, width), F32)],
        compiler_params=vmem(52),
        cost_estimate=takes(10),
        name="proj_grads",
    )(n1, dproj, *o_chunks, da)


def dn_kernel(s_ref, p_ref, w_ref, out_ref):
    total = dot(p_ref[0], w_ref[0], 1, 1) + dot(p_ref[1], w_ref[1], 1, 1)
    out_ref[...] = (total + dot(p_ref[2], w_ref[2], 1, 1)).astype(BF16)


def dn_call(scalars, dproj, w_qkv, rel, rows):
    kinds, _, cols = dproj.shape
    width = w_qkv.shape[1]
    return pl.pallas_call(
        dn_kernel,
        out_shape=jax.ShapeDtypeStruct((rows, width), BF16),
        grid_spec=pltpu.PrefetchScalarGridSpec(
            num_scalar_prefetch=1,
            grid=(1,),
            in_specs=[
                pl.BlockSpec((kinds, rows, cols), lambda i, s: (0, rel ^ s[0], 0)),
                resident((kinds, width, cols)),
            ],
            out_specs=pl.BlockSpec((rows, width), lambda i, s: (0, 0)),
        ),
        compiler_params=vmem(52),
        cost_estimate=takes(0),
        name="dn",
    )(scalars, dproj, w_qkv)


def last_kernel(keep_ref, core_ref, chip_ref, x_ref, dx_ref, gain_ref, out_ref):
    dn = keep_ref[...].astype(F32) + core_ref[...].astype(F32) + chip_ref[...].astype(F32)
    dn = dn.astype(BF16).astype(F32)
    normed, scale = row_stats(x_ref[...].astype(F32))
    out_ref[...] = (dx_ref[...] + pull_norm(normed, scale, dn * gain_ref[...])).astype(BF16)


def last_call(keep, core, chip, x, dx, gain, step=256):
    rows, width = x.shape
    per = rows // step
    flat = pl.BlockSpec((step, width), lambda i: (i, 0))
    return pl.pallas_call(
        last_kernel,
        out_shape=jax.ShapeDtypeStruct((rows, width), BF16),
        grid=(per,),
        in_specs=[flat] * 5 + [resident(gain.shape)],
        out_specs=flat,
        compiler_params=vmem(52),
        cost_estimate=takes(0),
        name="last",
    )(keep, core, chip, x, dx, gain)


def turn_rows_kernel(hot_ref, rows_ref, out_ref):
    out_ref[...] = dot(hot_ref[...], rows_ref[...], 0, 0).astype(BF16)


def turn_rows(one_hot, values):
    return pl.pallas_call(
        turn_rows_kernel,
        out_shape=jax.ShapeDtypeStruct(values.shape, BF16),
        compiler_params=vmem(52),
        cost_estimate=takes(0),
        name="turn_rows",
    )(one_hot, values)


def bits_of(count):
    return [1 << i for i in range(count.bit_length() - 1)]


def pick(values, axis, index):
    return lax.dynamic_index_in_dim(values, index, axis, keepdims=False)


def by_device(values, count):
    blocks = values.shape[0]
    if blocks == count:
        return values
    axis = values.shape.index(LANES, 2)
    shape = values.shape[:axis] + (count // blocks, LANES * blocks // count) + values.shape[axis + 1 :]
    values = jnp.moveaxis(values.reshape(shape), axis, 1)
    return values.reshape((count,) + values.shape[2:])


def after(point, *values):
    return lax.optimization_barrier((point, *values))[1:]


def gather_bits(values, axis_name):
    me = lax.axis_index(axis_name)
    count = lax.axis_size(axis_name)
    shape = values.shape
    for bit in reversed(bits_of(count)):
        other = swap_bit(values, axis_name, bit)
        high = (me // bit) % 2 == 1
        values = jnp.stack([jnp.where(high, other, values), jnp.where(high, values, other)])
    lead = values.ndim - len(shape)
    order = tuple(reversed(range(lead))) + tuple(range(lead, values.ndim))
    return values.transpose(order).reshape((count,) + shape)


def scatter_lanes(values):
    me = lax.axis_index("mp")
    count = lax.axis_size("mp")
    slices = values.reshape(values.shape[0], count, values.shape[1] // count)
    total = pick(slices, 1, me)
    for bits in range(1, count):
        total = total + swap_bit(pick(slices, 1, me ^ bits), "mp", bits)
    return total


def local(
    hidden_in, out_grad, seq_lengths, dealing, attn_gain, mlp_gain, w_qkv, w_out, w_in, w_down
):
    dp_count = lax.axis_size("dp")
    mp_count = lax.axis_size("mp")
    owner = lax.axis_index("dp")
    lane = lax.axis_index("mp")
    rows, width = hidden_in.shape
    tokens = rows * mp_count
    shards = width // dp_count
    slots = rows // dp_count
    first_len = pick(seq_lengths, 0, 2 * owner)
    scalars = jnp.stack([lane, first_len, lane % 2, lane // 2]).astype(jnp.int32)

    lane_rows = pick(dealing.reshape(dp_count, mp_count, rows), 1, lane)
    local_row = lane_rows - (owner * mp_count + lane) * rows
    inside = (local_row >= 0) & (local_row < rows)
    order = jnp.arange(rows, dtype=jnp.int32)
    upto = (order[:, None] <= order[None, :]).astype(BF16)
    rank = dot(inside.astype(BF16), upto, 1, 0).astype(jnp.int32) - 1
    slot_hit = inside[:, None, :] & (rank[:, None, :] == jnp.arange(slots)[None, :, None])
    send_row = jnp.sum(jnp.where(slot_hit, local_row[:, None, :], 0), axis=2).reshape(rows)
    to_slot = (send_row[:, None] == order[None, :]).astype(BF16)
    source = pick(lane_rows, 0, owner) // (rows * mp_count)
    from_src = source[None, :] == jnp.arange(dp_count, dtype=jnp.int32)[:, None]
    src_rank = dot(from_src.astype(BF16), upto, 1, 0).astype(jnp.int32) - 1
    slot_of = source * slots + jnp.sum(jnp.where(from_src, src_rank, 0), axis=0)
    to_dealt = (slot_of[:, None] == order[None, :]).astype(BF16)

    def exchange(values):
        packed = values.reshape(dp_count, slots, width)
        arrived = lax.all_to_all(packed, "dp", split_axis=0, concat_axis=0, tiled=True)
        return arrived.reshape(rows, width)

    def pack(values):
        return dot(to_slot, values, 1, 0).astype(BF16)

    def unpack(values):
        return dot(to_dealt, values, 1, 0).astype(BF16)

    def pack_back(values):
        return dot(to_dealt, values, 0, 0).astype(BF16)

    def unpack_back(values):
        return dot(to_slot, values, 0, 0).astype(BF16)

    def group(values):
        across = swap_bit(values, "mp", 2)
        return [values, swap_bit(values, "mp", 1), across, swap_bit(across, "mp", 1)]

    gains = gather_bits(gather_bits(jnp.stack([attn_gain, mlp_gain]), "dp"), "mp")
    gains = gains.transpose(2, 1, 0, 3).reshape(2, width)
    place = jnp.arange(tokens, dtype=jnp.int32)
    place = jnp.where(place >= first_len, place - first_len, place).astype(F32)
    freq_index = jnp.arange(LANES, dtype=jnp.int32) % (HEAD_DIM // 2)
    freqs = jnp.exp(freq_index.astype(F32) * (-2.0 * math.log(theta_base) / HEAD_DIM))
    angles = place[:, None] * freqs[None, :]
    first_half = jnp.arange(LANES) % HEAD_DIM < HEAD_DIM // 2
    cos = jnp.cos(angles)
    sin = jnp.sin(angles) * jnp.where(first_half, -1.0, 1.0)[None, :]

    w_mlp = jnp.concatenate([w_in, w_down.T[None]], axis=0)
    x_arrived = exchange(pack(hidden_in))
    x_arrived, gains, cos, sin, scalars, g_packed = lax.optimization_barrier(
        (x_arrived, gains, cos, sin, scalars, pack(out_grad))
    )
    w_mlp = lax.all_gather(w_mlp, "dp", axis=1, tiled=True)
    gain_one, gain_two = gains[0:1], gains[1:2]
    x_mine = unpack(x_arrived)
    x_rel = group(x_mine)
    attn_weights = jnp.concatenate([w_qkv, w_out.T[None]], axis=0)
    attn_weights = jnp.moveaxis(gather_bits(attn_weights, "dp"), 0, 1).reshape(4, width, -1)
    w_out_across = swap_bit(attn_weights[3], "mp", 2)
    g_packed, attn_weights = lax.optimization_barrier((g_packed, attn_weights))
    g_arrived = exchange(g_packed)

    held = qkv_call(scalars, x_rel[0], x_rel[1], gain_one, attn_weights, cos, sin, 0, ())
    q, k, v, n1 = qkv_call(scalars, x_rel[2], x_rel[3], gain_one, attn_weights, cos, sin, 2, held)
    q, w_out_across = lax.optimization_barrier((q, w_out_across))
    w_out_rel = [attn_weights[3], None, w_out_across, None]
    w_out_rel[1], w_out_rel[3] = swap_bit(w_out_rel[0], "mp", 1), swap_bit(w_out_across, "mp", 1)
    near, q2, near_top = attend_forward(scalars, q, k, v, 0, 2 * rows, ())
    (g_arrived,) = after(near, g_arrived)
    g_mine = unpack(g_arrived)
    g_core, g_across = swap_bit(g_mine, "mp", 1), swap_bit(g_mine, "mp", 2)
    near_across = swap_bit(near, "mp", 2)
    distant, q2, far_top = attend_forward(scalars, q, k, v, 1, 2 * rows, (q2,))
    distant, near_across, g_across = lax.optimization_barrier((distant, near_across, g_across))
    g_rel = [g_mine, g_core, g_across, swap_bit(g_across, "mp", 1)]
    far_across = swap_bit(distant, "mp", 2)
    core = lambda values: swap_bit(values, "mp", 1)
    far_heads = [distant, core(distant), near_across, core(near_across)]
    peaks = [near_top, far_top]
    head_peaks = jnp.max(jnp.stack(peaks), axis=(0, 1, 3, 4)) * score_scale
    peak_bits = bits_of(dp_count)
    peak_swap = swap_bit(head_peaks, "dp", peak_bits[0])

    *held, keep, send, keep_out, send_out = mlp_call(
        scalars,
        (x_rel[3], x_rel[2]),
        (g_rel[3], g_rel[2]),
        far_heads,
        w_out_rel,
        gain_two,
        w_mlp,
        2,
        (),
    )
    far_across, peak_swap, send, near = lax.optimization_barrier(
        (far_across, peak_swap, send, near)
    )
    head_peaks = jnp.maximum(head_peaks, peak_swap)
    peak_swap = swap_bit(head_peaks, "dp", peak_bits[1])
    dn_far = (keep + core(send).astype(F32)).astype(BF16)
    dn_arrived = swap_bit(dn_far, "mp", 2)
    near_heads = [near, core(near), far_across, core(far_across)]
    (near_heads[0],) = after(dn_far, near)
    far_out = (keep_out, send_out)
    a_rel, n2, g_all, act, dgate, dup, keep, send, keep_out, send_out = mlp_call(
        scalars,
        (x_rel[1], x_rel[0]),
        (g_rel[1], g_rel[0]),
        near_heads,
        w_out_rel,
        gain_two,
        w_mlp,
        0,
        held,
    )
    dn_arrived, peak_swap, send = lax.optimization_barrier((dn_arrived, peak_swap, send))
    head_peaks = jnp.maximum(head_peaks, peak_swap)
    peak_swap = swap_bit(head_peaks, "dp", peak_bits[2])
    dx, da = resid_call(
        keep, core(send), dn_arrived, x_rel[0], a_rel, g_rel[0], gain_two
    )
    da_core, da_across = core(da), swap_bit(da, "mp", 2)

    flat = lambda values: values.reshape(tokens, values.shape[2])
    (act,) = after(da, act)
    inner_grads = inner_call(flat(n2), flat(g_all), flat(dgate), flat(dup), flat(act))
    held = list(head_grad_call(scalars, da, da_core, attn_weights[3], near, 0, tokens, ()))
    _, da_across, held[0] = lax.optimization_barrier((inner_grads, da_across, held[0]))
    do, da_all = head_grad_call(
        scalars, da_across, core(da_across), attn_weights[3], distant, 1, tokens, held
    )
    head_peaks = jnp.maximum(head_peaks, peak_swap)
    for bit in peak_bits[3:]:
        head_peaks = jnp.maximum(head_peaks, swap_bit(head_peaks, "dp", bit))
    inner_grads, peak_swap = lax.optimization_barrier((inner_grads, peak_swap))
    inner_grads = by_device(inner_grads, dp_count)
    inner_grads = lax.all_to_all(inner_grads, "dp", split_axis=0, concat_axis=0, tiled=True)


    far_out = after(da_across, *far_out)
    add_core = lambda keep, send: keep.astype(F32) + core(send).astype(F32)

    out_far = add_core(*far_out).astype(BF16)
    out_arrived = swap_bit(out_far, "mp", 2)
    do, out_sum = after(out_far, do, add_core(keep_out, send_out))
    dproj = attend_backward(scalars, q2, k, v, do, cos, sin)
    head_peaks = jnp.maximum(head_peaks, peak_swap)
    for bit in peak_bits[3:]:
        head_peaks = jnp.maximum(head_peaks, swap_bit(head_peaks, "dp", bit))
    factor = jnp.sqrt(clip_limit / jnp.maximum(head_peaks, clip_limit))
    column_factor = jnp.repeat(factor, HEAD_DIM)
    scaling = jnp.stack([column_factor, column_factor, jnp.ones_like(column_factor)])[:, None, :]
    clipped = (w_qkv.astype(F32) * scaling).astype(BF16)

    proj_grad = proj_call(n1, dproj, (near, distant), da_all)
    proj_grad, dproj, out_arrived = lax.optimization_barrier((proj_grad, dproj, out_arrived))
    far_core = core(dn_call(scalars, dproj, attn_weights, 3, rows))
    far_keep = dn_call(scalars, dproj, attn_weights, 2, rows)
    dn_far = (far_keep.astype(F32) + far_core.astype(F32)).astype(BF16)
    dn_arrived = swap_bit(dn_far, "mp", 2)
    inner_grads, dn_far, out_arrived = lax.optimization_barrier((inner_grads, dn_far, out_arrived))
    x1 = x_rel[0].astype(F32) + a_rel[0].astype(F32)
    out_packed = pack_back((x1 + (out_sum + out_arrived.astype(F32))).astype(BF16))
    (dproj,) = after(out_packed, dproj)
    out_sent = exchange(out_packed)
    send = dn_call(scalars, dproj, attn_weights, 1, rows)
    keep = dn_call(scalars, dproj, attn_weights, 0, rows)
    dn_core = core(send)
    inner_grads = jnp.sum(inner_grads.astype(F32), axis=0)
    inner_grad, down_grad = jnp.swapaxes(inner_grads[:2], 1, 2), inner_grads[2]
    inner_by_gain = jnp.sum(inner_grad * w_in.astype(F32), axis=(0, 2))
    gain_part = lax.dynamic_slice_in_dim(gains, owner * shards, shards, 1)
    inner_grad, down_grad, inner_by_gain, gain_part, clipped, keep = lax.optimization_barrier(
        (inner_grad, down_grad, inner_by_gain, gain_part, clipped, keep)
    )
    out_sent, dn_arrived, dn_core = lax.optimization_barrier((out_sent, dn_arrived, dn_core))
    grad_packed = pack_back(last_call(keep, dn_core, dn_arrived, x_rel[0], dx, gain_one))
    grad_arrived = exchange(grad_packed)
    (out_arrived,) = after(grad_packed, out_sent)
    output = turn_rows(to_slot, out_arrived)
    grads = lax.psum_scatter(by_device(proj_grad, dp_count), "dp")
    (grads,) = after(output, grads)
    grad_arrived, grads = lax.optimization_barrier((grad_arrived, grads))
    grads = grads.astype(F32)
    input_grad = unpack_back(grad_arrived)
    proj_grad, outer_grad = jnp.swapaxes(grads[:3], 1, 2), grads[3]

    by_gain = jnp.stack([jnp.sum(proj_grad * w_qkv.astype(F32), axis=(0, 2)), inner_by_gain])
    gain_grads = scatter_lanes(by_gain / gain_part)
    return (
        output,
        input_grad,
        gain_grads[0],
        gain_grads[1],
        proj_grad,
        outer_grad,
        inner_grad,
        down_grad,
        clipped,
    )


def solution(mesh):
    in_specs = (
        P(("dp", "mp"), None),
        P(("dp", "mp"), None),
        P(),
        P(),
        P(("dp", "mp")),
        P(("dp", "mp")),
        P(None, "dp", "mp"),
        P("mp", "dp"),
        P(None, "dp", "mp"),
        P("mp", "dp"),
    )
    out_specs = (
        P(("dp", "mp"), None),
        P(("dp", "mp"), None),
        P(("dp", "mp")),
        P(("dp", "mp")),
        P(None, "dp", "mp"),
        P("mp", "dp"),
        P(None, "dp", "mp"),
        P("mp", "dp"),
        P(None, "dp", "mp"),
    )
    return jax.shard_map(local, mesh=mesh, in_specs=in_specs, out_specs=out_specs, check_vma=False)
```
